128 devices in a mesh: row: 32 (over x, z, core), col: 4 (over y).
Axes of the slice: x: 4, y: 4, z: 4, core: 2. Of those that a mesh axis runs over, the one named last changes fastest.
Arguments:
- strips: bfloat16 [160, 32, 4, 64, 512], P('col', 'row'), may hold values from -6 to 6
- pair_counts: int32 [160, 32, 2], P('col', 'row'), may hold values from 0 to 5, as said below
- pair_offsets: int32 [160, 32, 2], P('col', 'row'), may hold values from 0 to 63
- tile_stiffness: float32 [160, 32], P('col', 'row'), may hold values from 0.1 to 1
- anchor: float32 [160, 32, 896], P('col', 'row'), may hold values from 0.02 to 0.2
Outputs:
- match_terms: float32 [160, 32, 2, 3, 8], P('col', 'row')
- positions: float32 [160, 32, 2, 896], P('col', 'row')
- residual: float32 [160, 32, 2, 896], P('col', 'row')
The draws below stay inside these ranges and needn't reach their ends.
Inputs may be any that keep to these rules, and one draw needn't show every extreme that they name: `pair_counts`: entry [r, c, 0] belongs to the pair of tiles (r, c) and (r, c + 1), entry [r, c, 1] to tiles (r, c) and (r + 1, c); it is 0 where the second tile does not exist. The 40 tiles of one device (40 consecutive tile rows of one tile column) hold at most 400 valid blocks in all, and some device holds exactly 400.
All inputs are finite; a program needn't handle non-finite values.
Results may differ from the reference program's by a relative error of at most 0.0082.
Values may be sent and summed in bfloat16 or wider, within the bound.
No kernel may reach another device: no remote copies, remote signals or barrier semaphores. Data moves between devices by JAX's collectives and lax.ppermute only.
A program may use at most 128 MiB of HBM per device.

```python
import math
import jax
import jax.numpy as jnp
from jax import lax

TR_DEV = 40
PATCH = 64
BLOCKS = 8
MESH_Y = 28
MESH_X = 32
MATCH_MOST = 5
ITERS = 3
TILE_ROWS = 160
TILE_COLS = 32
NODES = 896


def draw_pair_counts(key, part):
    level_key, raw_key, row_key, col_key = jax.random.split(jax.random.fold_in(key, 17), 4)
    device_rows = TILE_ROWS // TR_DEV
    levels = jax.random.randint(level_key, (device_rows, TILE_COLS), 1, MATCH_MOST + 1)
    tile_levels = jnp.repeat(levels, TR_DEV, axis=0)
    raw_counts = jax.random.randint(raw_key, (TILE_ROWS, TILE_COLS, 2), 0, MATCH_MOST + 1)
    counts = jnp.minimum(raw_counts, tile_levels[:, :, None])
    busy_row = jax.random.randint(row_key, (), 0, device_rows - 1)
    busy_col = jax.random.randint(col_key, (), 0, TILE_COLS - 1)
    tile_row = jnp.arange(TILE_ROWS, dtype=jnp.int32)[:, None]
    col_index = jnp.arange(TILE_COLS, dtype=jnp.int32)[None, :]
    busy_tiles = (tile_row // TR_DEV == busy_row) & (col_index == busy_col)
    counts = jnp.where(busy_tiles[:, :, None], MATCH_MOST, counts)
    east_counts = jnp.where(col_index == TILE_COLS - 1, 0, counts[:, :, 0])
    south_counts = jnp.where(tile_row == TILE_ROWS - 1, 0, counts[:, :, 1])
    return jnp.stack([east_counts, south_counts], axis=2).astype(jnp.int32)


def touch_ends(array, rng, low, top_value):
    longest = array.shape.index(max(array.shape))
    spots = []
    for shift in (0, 1):
        where = [jax.random.randint(jax.random.fold_in(rng, axis), (), 0, length) for axis, length in enumerate(array.shape)]
        where[longest] = (where[longest] + shift) % array.shape[longest]
        spots.append(tuple(where))
    return array.at[spots[0]].set(low).at[spots[1]].set(top_value)


def block_levels(own_key, extent, pieces, least, high):
    level, own = 1.0, jax.random.fold_in(own_key, 6)
    for axis_at, parts in pieces:
        heights = jnp.exp(jax.random.uniform(jax.random.fold_in(own, axis_at), (parts,), jnp.float32, least / len(pieces), high / len(pieces)))
        level = level * jnp.repeat(heights, extent[axis_at] // parts).reshape([-1 if axis == axis_at else 1 for axis in range(len(extent))])
    return level


def noise(stream_key, dims, scale, most, cuts=(), kind=jnp.bfloat16):
    loudness = block_levels(stream_key, dims, cuts, -0.22, 0.18) if cuts else 1.0
    entries = jax.random.normal(stream_key, dims, jnp.float32) * scale * loudness
    return jnp.minimum(jnp.maximum(entries, -most), most).astype(kind)


def setup_inputs(seed: int = 0) -> dict:
    key_of = jax.random.split(jax.random.key(seed), 6)
    return {
        "strips": noise(key_of[0], (TILE_ROWS, TILE_COLS, 4, PATCH, PATCH * BLOCKS), 1.0, 6.0, ((0, 4), (1, 32))),
        "pair_counts": draw_pair_counts(jax.random.fold_in(key_of[5], 71), 0),
        "pair_offsets": touch_ends(jax.random.randint(key_of[2], (TILE_ROWS, TILE_COLS, 2), 0, 64), jax.random.fold_in(key_of[2], 1), 0, 63).astype(jnp.int32),
        "tile_stiffness": jnp.clip(jnp.exp(math.log(1.0) - 2.3025851 * jax.random.uniform(key_of[3], (TILE_ROWS, TILE_COLS), jnp.float32) ** block_levels(key_of[3], (TILE_ROWS, TILE_COLS), ((0, 4), (1, 32)), -0.2, 0.2)), 0.1, 1.0),
        "anchor": jnp.clip(jnp.exp(math.log(0.2) - 2.3025851 * jax.random.uniform(key_of[4], (TILE_ROWS, TILE_COLS, NODES), jnp.float32) ** block_levels(key_of[4], (TILE_ROWS, TILE_COLS, NODES), ((0, 4), (1, 32)), -0.2, 0.2)), 0.02, 0.2),
    }


SMALL_WEIGHT = 1e-6
NODE_GAP = 16.0
HIGHEST_PREC = lax.Precision.HIGHEST


def dft_tables(patch_len):
    index_line = jnp.arange(patch_len, dtype=jnp.int32)
    product = (index_line[:, None] * index_line[None, :]) % patch_len
    angles = product.astype(jnp.float32) * (2.0 * math.pi / patch_len)
    return jnp.cos(angles).astype(jnp.bfloat16), jnp.sin(angles).astype(jnp.bfloat16)


def spectrum(patches, cosine, sine_table):
    patch_len = cosine.shape[0]
    depth_table = jnp.concatenate([cosine, -sine_table], axis=0).astype(jnp.float32)
    length_table = jnp.concatenate([cosine, sine_table], axis=1).astype(jnp.float32)
    half_spec = jnp.einsum("fd,ndbk->nfbk", depth_table, patches.astype(jnp.float32), precision=HIGHEST_PREC)
    half_spec = half_spec.astype(jnp.bfloat16)
    full_spec = jnp.einsum("nfbk,kg->nfbg", half_spec.astype(jnp.float32), length_table, precision=HIGHEST_PREC)
    real_part = full_spec[:, :patch_len, :, :patch_len] + full_spec[:, patch_len:, :, patch_len:]
    imag_part = full_spec[:, patch_len:, :, :patch_len] - full_spec[:, :patch_len, :, patch_len:]
    return real_part, imag_part


def correlate(first_blocks, second_blocks, cosine, sine_table):
    patch_len = cosine.shape[0]
    first_real, first_imag = spectrum(first_blocks, cosine, sine_table)
    second_real, second_imag = spectrum(second_blocks, cosine, sine_table)
    denominator = 0.5 * (first_real * first_real + first_imag * first_imag
                         + second_real * second_real + second_imag * second_imag) + 1.0
    cross_real = ((first_real * second_real + first_imag * second_imag) / denominator).astype(jnp.bfloat16)
    cross_imag = ((first_imag * second_real - first_real * second_imag) / denominator).astype(jnp.bfloat16)
    cross_stack = jnp.concatenate([cross_real, cross_imag], axis=1).astype(jnp.float32)
    length_table = jnp.concatenate([cosine, sine_table], axis=1).astype(jnp.float32)
    back_spec = jnp.einsum("nubv,vg->nubg", cross_stack, length_table, precision=HIGHEST_PREC)
    inverse_real = back_spec[:, :patch_len, :, :patch_len] - back_spec[:, patch_len:, :, patch_len:]
    inverse_imag = back_spec[:, patch_len:, :, :patch_len] + back_spec[:, :patch_len, :, patch_len:]
    half_back = jnp.concatenate([inverse_real, inverse_imag], axis=1).astype(jnp.bfloat16)
    back_table = jnp.concatenate([cosine, -sine_table], axis=1).astype(jnp.float32)
    surface = jnp.einsum("xu,nubv->nxbv", back_table, half_back.astype(jnp.float32), precision=HIGHEST_PREC)
    surface = surface / float(patch_len * patch_len)
    power_map = surface * surface
    offsets = ((jnp.arange(patch_len, dtype=jnp.int32) + patch_len // 2) % patch_len - patch_len // 2).astype(jnp.float32)
    weight = jnp.sum(power_map, axis=(1, 3))
    weight_total = weight + SMALL_WEIGHT
    shift_depth = jnp.sum(power_map * offsets[None, :, None, None], axis=(1, 3)) / weight_total
    shift_along = jnp.sum(power_map * offsets[None, None, None, :], axis=(1, 3)) / weight_total
    return weight, shift_depth, shift_along


def edge_tents(offsets, node_count, blocks, patch_len):
    centres = offsets[..., None] + (patch_len * jnp.arange(blocks, dtype=jnp.int32) + patch_len // 2).astype(offsets.dtype)
    node_pos = (NODE_GAP * jnp.arange(node_count, dtype=jnp.int32).astype(offsets.dtype) + NODE_GAP / 2)
    return jnp.maximum(0.0, 1.0 - jnp.abs(centres[..., None] - node_pos) / NODE_GAP)


def spread(tent_table, weight, vectors):
    return jnp.einsum("...kn,...ck->...cn", tent_table * weight[..., None], vectors, precision=HIGHEST_PREC)


def edge_force(tent_table, weight, difference):
    projected = jnp.einsum("...kn,...cn->...ck", tent_table, difference, precision=HIGHEST_PREC)
    return spread(tent_table, weight, projected)


def intra_term(mesh_grid, stiffness, anchor_grid):
    count_y, count_x = mesh_grid.shape[-2], mesh_grid.shape[-1]
    widths = [(0, 0)] * (mesh_grid.ndim - 2) + [(1, 1), (1, 1)]
    padded = jnp.pad(mesh_grid, widths)
    beside = padded[..., :-2, 1:-1] + padded[..., 2:, 1:-1] + padded[..., 1:-1, :-2] + padded[..., 1:-1, 2:]
    row_ids = jnp.arange(count_y, dtype=jnp.int32)[:, None]
    col_ids = jnp.arange(count_x, dtype=jnp.int32)[None, :]
    degree = ((row_ids > 0).astype(mesh_grid.dtype) + (row_ids < count_y - 1).astype(mesh_grid.dtype)
              + (col_ids > 0).astype(mesh_grid.dtype) + (col_ids < count_x - 1).astype(mesh_grid.dtype))
    return stiffness * (degree * mesh_grid - beside) + anchor_grid * mesh_grid


def place_pairs(result, east_force, south_force):
    result = result.at[..., :, MESH_X - 1].add(east_force)
    pushed_east = jnp.concatenate([jnp.zeros_like(east_force[:, :1]), east_force[:, :-1]], axis=1)
    result = result.at[..., :, 0].add(-pushed_east)
    result = result.at[..., MESH_Y - 1, :].add(south_force)
    pushed_south = jnp.concatenate([jnp.zeros_like(south_force[:1]), south_force[:-1]], axis=0)
    result = result.at[..., 0, :].add(-pushed_south)
    return result


def operate(node_field, stiffness, anchor_grid, east_pair, south_pair):
    tile_rows, tile_cols = node_field.shape[0], node_field.shape[1]
    mesh_grid = node_field.reshape(tile_rows, tile_cols, 2, MESH_Y, MESH_X)
    result = intra_term(mesh_grid, stiffness, anchor_grid)
    right_col = mesh_grid[..., :, MESH_X - 1]
    left_col = mesh_grid[..., :, 0]
    partner_left = jnp.concatenate([left_col[:, 1:], jnp.zeros_like(left_col[:, :1])], axis=1)
    east_force = edge_force(east_pair[0], east_pair[1], right_col - partner_left)
    bottom_row = mesh_grid[..., MESH_Y - 1, :]
    top_row = mesh_grid[..., 0, :]
    partner_top = jnp.concatenate([top_row[1:], jnp.zeros_like(top_row[:1])], axis=0)
    south_force = edge_force(south_pair[0], south_pair[1], bottom_row - partner_top)
    result = place_pairs(result, east_force, south_force)
    return result.reshape(tile_rows, tile_cols, 2, MESH_Y * MESH_X)


def reference(strips, pair_counts, pair_offsets, tile_stiffness, anchor):
    tile_rows, tile_cols = strips.shape[0], strips.shape[1]
    patch_len = strips.shape[3]
    blocks = strips.shape[4] // patch_len
    cosine, sine_table = dft_tables(patch_len)

    def row_terms(row_index):
        here_row = lax.dynamic_index_in_dim(strips, row_index, 0, keepdims=False)
        below_row = lax.dynamic_index_in_dim(strips, jnp.minimum(row_index + 1, tile_rows - 1), 0, keepdims=False)
        east_left = jnp.concatenate([here_row[1:, 0], here_row[-1:, 0]], axis=0)
        first_blocks = jnp.concatenate([here_row[:, 3], here_row[:, 2]], axis=0)
        second_blocks = jnp.concatenate([east_left, below_row[:, 1]], axis=0)
        first_blocks = first_blocks.reshape(2 * tile_cols, patch_len, blocks, patch_len)
        second_blocks = second_blocks.reshape(2 * tile_cols, patch_len, blocks, patch_len)
        return correlate(first_blocks, second_blocks, cosine, sine_table)

    row_list = jnp.arange(tile_rows, dtype=jnp.int32)
    weight, shift_depth, shift_along = lax.map(row_terms, row_list)

    def by_tile(values):
        return values.reshape(tile_rows, 2, tile_cols, blocks).transpose(0, 2, 1, 3)

    is_valid = jnp.arange(blocks, dtype=jnp.int32)[None, None, None, :] < pair_counts[..., None]
    weight = jnp.where(is_valid, by_tile(weight), 0.0)
    shift_depth = jnp.where(is_valid, by_tile(shift_depth), 0.0)
    shift_along = jnp.where(is_valid, by_tile(shift_along), 0.0)
    shift_x = jnp.stack([shift_depth[:, :, 0], shift_along[:, :, 1]], axis=2)
    shift_y = jnp.stack([shift_along[:, :, 0], shift_depth[:, :, 1]], axis=2)
    match_terms = jnp.stack([weight, shift_x, shift_y], axis=3)

    offsets = pair_offsets.astype(jnp.float32)
    east_tent = edge_tents(offsets[:, :, 0], MESH_Y, blocks, patch_len)
    south_tent = edge_tents(offsets[:, :, 1], MESH_X, blocks, patch_len)
    east_pair = (east_tent, weight[:, :, 0])
    south_pair = (south_tent, weight[:, :, 1])
    east_shift = jnp.stack([shift_x[:, :, 0], shift_y[:, :, 0]], axis=2)
    south_shift = jnp.stack([shift_x[:, :, 1], shift_y[:, :, 1]], axis=2)
    zero_grid = jnp.zeros((tile_rows, tile_cols, 2, MESH_Y, MESH_X), jnp.float32)
    rhs_grid = place_pairs(zero_grid, spread(east_tent, weight[:, :, 0], east_shift),
                           spread(south_tent, weight[:, :, 1], south_shift))
    right_side = rhs_grid.reshape(tile_rows, tile_cols, 2, MESH_Y * MESH_X)

    stiffness = tile_stiffness[:, :, None, None, None]
    anchor_grid = anchor.reshape(tile_rows, tile_cols, 1, MESH_Y, MESH_X)
    positions = jnp.zeros_like(right_side)
    residual = right_side
    direction = right_side
    norm_now = jnp.sum(residual * residual)
    for iteration in range(ITERS):
        applied = operate(direction, stiffness, anchor_grid, east_pair, south_pair)
        step_size = norm_now / jnp.sum(direction * applied)
        positions = positions + step_size * direction
        residual = residual - step_size * applied
        norm_next = jnp.sum(residual * residual)
        direction = residual + (norm_next / norm_now) * direction
        norm_now = norm_next
    return match_terms, positions, residual
```

```python
import functools
import math

import jax
import jax.numpy as jnp
import numpy as np
from jax import lax
from jax.experimental import pallas as pl
from jax.experimental.pallas import tpu as pltpu
from jax.sharding import PartitionSpec as P

MESH_Y = 28
MESH_X = 32
NODES = MESH_Y * MESH_X
PATCH = 64
MOST = 5
WIDE = MOST * PATCH
HALF_ROWS = 40
LANES = 128
COMP = 64
GROUP = 4
SMALL_WEIGHT = 1e-06
GAP = 16.0
F32 = jnp.float32
BF16 = jnp.bfloat16
HIGHEST = lax.Precision.HIGHEST


def tables():
    index = np.arange(PATCH)
    angle = (index[:, None] * index[None, :] % PATCH) * (2.0 * math.pi / PATCH)
    bf = jnp.bfloat16
    cos = np.cos(angle).astype(bf).astype(np.float32)
    sin = np.sin(angle).astype(bf).astype(np.float32)
    half = PATCH // 2 + 1
    depth = np.zeros((2 * HALF_ROWS, PATCH), np.float32)
    depth[:half] = cos[:half]
    depth[HALF_ROWS : HALF_ROWS + half] = -sin[:half]
    pair = np.zeros((2, 2), np.float32)
    np.fill_diagonal(pair, 1.0)
    cos2, sin2 = np.kron(pair, cos), np.kron(pair, sin)
    forward = np.block([[cos2, -sin2], [sin2, cos2]])
    back = np.block([[cos2, sin2], [-sin2, cos2]])
    back_swapped = np.block([[cos2, sin2], [sin2, -cos2]])
    twice = np.full((half,), 2.0, np.float32)
    twice[0] = twice[-1] = 1.0
    final = np.zeros((PATCH, 2 * HALF_ROWS), np.float32)
    final[:, :half] = cos[:, :half] * twice
    final[:, HALF_ROWS : HALF_ROWS + half] = -sin[:, :half] * twice
    offset = ((index + PATCH // 2) % PATCH - PATCH // 2).astype(np.float32)
    pick = np.zeros((8, LANES), np.float32)
    pick[0, :PATCH] = 1.0
    pick[1, PATCH:] = 1.0
    pick[2, :PATCH] = offset
    pick[3, PATCH:] = offset
    rows = np.repeat(offset[:, None], LANES, axis=1)
    as_bf = lambda a: jnp.asarray(a, BF16)
    backs = np.stack([back, back_swapped])
    return as_bf(depth), as_bf(forward), as_bf(backs), as_bf(final), jnp.asarray(pick), jnp.asarray(rows)


def block_pairs(strips):
    one, two = strips
    return [
        one[:, 0:128],
        one[:, 128:256],
        two[:, 0:128],
        two[:, 128:256],
        jnp.concatenate([one[:, 256:320], two[:, 256:320]], axis=1),
    ]


def correlate_group(firsts, seconds, depth, forward, back, final, rows, r0, r1, at):
    cols = block_pairs(firsts) + block_pairs(seconds)
    count = len(cols)
    half = count // 2
    spec = jnp.dot(depth, jnp.concatenate(cols, axis=1), preferred_element_type=F32)
    stacked = jnp.concatenate(
        [
            jnp.concatenate(
                [
                    spec[0:HALF_ROWS, LANES * i : LANES * (i + 1)],
                    spec[HALF_ROWS:, LANES * i : LANES * (i + 1)],
                ],
                axis=1,
            )
            for i in range(count)
        ],
        axis=0,
    ).astype(BF16)
    full = jnp.dot(stacked, forward, preferred_element_type=F32)
    split = half * HALF_ROWS
    first_real, first_imag = full[:split, :LANES], full[:split, LANES:]
    second_real, second_imag = full[split:, :LANES], full[split:, LANES:]
    denominator = (
        0.5
        * (
            first_real * first_real
            + first_imag * first_imag
            + second_real * second_real
            + second_imag * second_imag
        )
        + 1.0
    )
    inverse = 1.0 / denominator
    cross_real = (first_real * second_real + first_imag * second_imag) * inverse
    cross_imag = (first_imag * second_real - first_real * second_imag) * inverse
    cross = jnp.concatenate([cross_real, cross_imag], axis=1).astype(BF16)
    back_half = jnp.dot(cross, back, preferred_element_type=F32)
    sides = jnp.concatenate(
        [
            jnp.concatenate(
                [
                    back_half[HALF_ROWS * i : HALF_ROWS * (i + 1), :LANES],
                    back_half[HALF_ROWS * i : HALF_ROWS * (i + 1), LANES:],
                ],
                axis=0,
            )
            for i in range(half)
        ],
        axis=1,
    ).astype(BF16)
    surface = jnp.dot(final, sides, preferred_element_type=F32)
    for i in range(half):
        part = surface[:, LANES * i : LANES * (i + 1)]
        power = part * part
        total = jnp.sum(power, axis=0, keepdims=True)
        moment = jnp.sum(power * rows, axis=0, keepdims=True)
        if i < 4:
            row = at + i // 2
            r0[i % 2, pl.ds(row, 1), :] = total
            r1[i % 2, pl.ds(row, 1), :] = moment
        else:
            for row in (at, at + 1):
                r0[2, pl.ds(row, 1), :] = total
                r1[2, pl.ds(row, 1), :] = moment


def lane_sums(pick, table):
    return lax.dot_general(
        pick, table, (((1,), (1,)), ((), ())), precision=HIGHEST, preferred_element_type=F32
    )


def finish_terms(pick, r0, r1, counts, offsets, out):
    scale = 1.0 / float(PATCH * PATCH) ** 2
    even = lax.broadcasted_iota(jnp.int32, (1, LANES), 1) % 2 == 0
    plain = [lane_sums(pick, r0[s]) for s in range(3)]
    tilted = [lane_sums(pick, r1[s]) for s in range(3)]
    out[...] = jnp.zeros_like(out)
    for k in range(MOST):
        slot, side = k // 2, k % 2
        if k < 4:
            weight = plain[slot][side : side + 1]
            along = plain[slot][2 + side : 3 + side]
            deep = tilted[slot][side : side + 1]
        else:
            weight = jnp.where(even, plain[2][0:1], plain[2][1:2])
            along = jnp.where(even, plain[2][2:3], plain[2][3:4])
            deep = jnp.where(even, tilted[2][0:1], tilted[2][1:2])
        valid = counts > float(k) + 0.5
        weight = weight * scale
        inverse = scale / (weight + SMALL_WEIGHT)
        out[k : k + 1, :] = jnp.where(valid, weight, 0.0)
        out[8 + k : 9 + k, :] = jnp.where(valid, deep * inverse, 0.0)
        out[16 + k : 17 + k, :] = jnp.where(valid, along * inverse, 0.0)
    out[24:25, :] = offsets


def south_kernel(first, sec0, sec1, sec2, sec3, nxt, info, depth, forward, back, final, pick, rows, out, r0, r1):
    step = pl.program_id(0)
    last = pl.num_programs(0) - 1

    @pl.when(step == 0)
    def _():
        r0[...] = jnp.zeros_like(r0)
        r1[...] = jnp.zeros_like(r1)

    seconds = [ref[0, 0, :, :WIDE] for ref in (sec0, sec1, sec2, sec3)]
    seconds[3] = jnp.where(step == last, nxt[0], seconds[3])
    for g in range(GROUP // 2):
        correlate_group(
            [first[2 * g + j, 0, :, :WIDE] for j in range(2)],
            seconds[2 * g : 2 * g + 2],
            depth[...], forward[...], back[0], final[...], rows[...], r0, r1, GROUP * step + 2 * g,
        )

    @pl.when(step == last)
    def _():
        finish_terms(pick[...], r0, r1, info[2:3, :], info[3:4, :], out)


def side_kernel(own, from_east, from_west, info, info_west, depth, forward, back, final, pick, rows, out, r0, r1):
    step = pl.program_id(0)
    steps = pl.num_programs(0)

    @pl.when(step == 0)
    def _():
        r0[...] = jnp.zeros_like(r0)
        r1[...] = jnp.zeros_like(r1)

    east_part = step < steps // 2
    for g in range(GROUP // 2):
        others = [jnp.where(east_part, from_east[2 * g + j], from_west[2 * g + j]) for j in range(2)]
        correlate_group(
            [own[2 * g + j, 0, :, :WIDE] for j in range(2)],
            others,
            depth[...], forward[...], back[0], final[...], rows[...], r0, r1, GROUP * step + 2 * g,
        )

    @pl.when(step == steps - 1)
    def _():
        lane = lax.broadcasted_iota(jnp.int32, (1, LANES), 1)
        east = lane < GROUP * (steps // 2)
        counts = jnp.where(east, info[0:1, :], info_west[0:1, :])
        offsets = jnp.where(east, info[1:2, :], info_west[1:2, :])
        finish_terms(pick[...], r0, r1, counts, offsets, out)


def const_spec(shape):
    return pl.BlockSpec(shape, lambda i: (0,) * len(shape))


SUMS = [pltpu.VMEM((3, LANES, LANES), F32), pltpu.VMEM((3, LANES, LANES), F32)]
VMEM_BYTES = 48 * 1024 * 1024


def table_specs(tabs, back_map):
    depth, forward, backs, final, pick, rows = tabs
    return [
        const_spec(depth.shape),
        const_spec(forward.shape),
        pl.BlockSpec((1, 2 * LANES, 2 * LANES), back_map),
        const_spec(final.shape),
        const_spec(pick.shape),
        const_spec(rows.shape),
    ]


def correlation_cost(pairs):
    return pl.CostEstimate(
        flops=pairs * MOST * 12_000_000, bytes_accessed=pairs * 2 * 64 * 384 * 2, transcendentals=0
    )


def south_terms(strips, nxt, info, tabs):
    tiles = strips.shape[0]
    steps = tiles // GROUP
    side = 384

    def second_spec(j):
        return pl.BlockSpec(
            (1, 1, PATCH, side), lambda i: (jnp.minimum(GROUP * i + 1 + j, tiles - 1), 1, 0, 0)
        )

    return pl.pallas_call(
        south_kernel,
        name="south_pairs",
        grid=(steps,),
        in_specs=[pl.BlockSpec((GROUP, 1, PATCH, side), lambda i: (i, 2, 0, 0))]
        + [second_spec(j) for j in range(GROUP)]
        + [const_spec(nxt.shape), const_spec(info.shape)]
        + table_specs(tabs, lambda i: (0, 0, 0)),
        out_specs=const_spec((32, LANES)),
        out_shape=jax.ShapeDtypeStruct((32, LANES), F32),
        scratch_shapes=SUMS,
        compiler_params=pltpu.CompilerParams(vmem_limit_bytes=VMEM_BYTES),
        cost_estimate=correlation_cost(tiles),
    )(strips, strips, strips, strips, strips, nxt, info, *tabs)


def side_terms(strips, from_east, from_west, info, info_west, tabs):
    tiles = strips.shape[0]
    steps = tiles // GROUP
    mid = steps // 2
    return pl.pallas_call(
        side_kernel,
        name="side_pairs",
        grid=(steps,),
        in_specs=[
            pl.BlockSpec((GROUP, 1, PATCH, 384), lambda i: (i, jnp.where(i < mid, 3, 0), 0, 0)),
            pl.BlockSpec((GROUP, PATCH, WIDE), lambda i: (jnp.minimum(i, mid - 1), 0, 0)),
            pl.BlockSpec((GROUP, PATCH, WIDE), lambda i: (jnp.maximum(i - mid, 0), 0, 0)),
            const_spec(info.shape),
            const_spec(info.shape),
        ]
        + table_specs(tabs, lambda i: (jnp.where(i < mid, 0, 1), 0, 0)),
        out_specs=const_spec((32, LANES)),
        out_shape=jax.ShapeDtypeStruct((32, LANES), F32),
        scratch_shapes=SUMS,
        compiler_params=pltpu.CompilerParams(vmem_limit_bytes=VMEM_BYTES),
        cost_estimate=correlation_cost(tiles),
    )(strips, from_east, from_west, info, info_west, *tabs)


def prepare_kernel(counts, offsets, stiffness, anchor, info, anchor_t, small, wide):
    tiles = anchor.shape[0]
    small[...] = jnp.zeros_like(small)
    small[0:tiles, 0:1] = counts[:, 0:1].astype(F32)
    small[0:tiles, 1:2] = offsets[:, 0:1].astype(F32)
    small[0:tiles, 2:3] = counts[:, 1:2].astype(F32)
    small[0:tiles, 3:4] = offsets[:, 1:2].astype(F32)
    small[0:tiles, 4:5] = stiffness[...]
    info[...] = small[...].T[0:8, :]
    wide[...] = jnp.zeros_like(wide)
    wide[0:tiles, :] = anchor[...]
    wide[COMP : COMP + tiles, :] = anchor[...]
    for i in range(NODES // LANES):
        anchor_t[LANES * i : LANES * (i + 1), :] = wide[:, LANES * i : LANES * (i + 1)].T


def whole(kernel, outs, name, scratch=()):
    vmem = pl.BlockSpec(memory_space=pltpu.VMEM)
    shapes = [jax.ShapeDtypeStruct(s, F32) for s in outs]

    def call(*args):
        return pl.pallas_call(
            kernel,
            name=name,
            in_specs=[vmem] * len(args),
            out_specs=[vmem] * len(outs),
            out_shape=shapes,
            scratch_shapes=list(scratch),
            compiler_params=pltpu.CompilerParams(vmem_limit_bytes=VMEM_BYTES),
            cost_estimate=pl.CostEstimate(
                flops=4_000_000, bytes_accessed=2_000_000, transcendentals=0
            ),
        )(*args)

    return call


def both(x):
    return x + pltpu.roll(x, COMP, axis=1)


def pair_tables(tiles, terms_south, terms_side, from_east, from_west, from_north, info, info_west):
    lane = lax.broadcasted_iota(jnp.int32, (1, LANES), 1)
    low = lane < tiles // 2
    inside = lane < tiles
    east = jnp.where(low, terms_side[...], from_east[...])
    west = jnp.where(low, from_west[...], terms_side[...])
    south = terms_south[...]
    north = jnp.where(
        lane == 0, pltpu.roll(from_north[...], LANES - (tiles - 1), axis=1), pltpu.roll(south, 1, axis=1)
    )
    east, west, south, north = [jnp.where(inside, a, 0.0) for a in (east, west, south, north)]

    def unpack(terms, offset, swapped):
        deep, along = terms[8:16], terms[16:24]
        x, y = (along, deep) if swapped else (deep, along)
        return terms[0:8], x, y, offset

    return (
        unpack(east, info[1:2, :], False),
        unpack(west, info_west[1:2, :], False),
        unpack(south, south[24:25], True),
        unpack(north, north[24:25], True),
    )


def tents(offset, count):
    offset = both(offset)
    node = lax.broadcasted_iota(jnp.int32, (count, LANES), 0).astype(F32) * GAP + GAP / 2
    out = []
    for k in range(MOST):
        centre = offset + float(PATCH * k + PATCH // 2)
        out.append(jnp.maximum(0.0, 1.0 - jnp.abs(centre - node) / GAP))
    return out


def load_force(table, count):
    weight, x, y, offset = table
    loads = weight * x + pltpu.roll(weight * y, COMP, axis=1)
    return sum(t * loads[k : k + 1] for k, t in enumerate(tents(offset, count)))


def edge_force(table, difference):
    weight, _, _, offset = table
    weight = both(weight)
    out = 0.0
    for k, t in enumerate(tents(offset, difference.shape[0])):
        projected = jnp.sum(t * difference, axis=0, keepdims=True)
        out = out + t * (projected * weight[k : k + 1])
    return out


LEFT = pl.ds(0, MESH_Y, stride=MESH_X)
RIGHT = pl.ds(MESH_X - 1, MESH_Y, stride=MESH_X)
TOP = pl.ds(0, MESH_X)
BOTTOM = pl.ds(NODES - MESH_X, MESH_X)


def apply_inside(v, out, stiffness, anchor_t):
    column = lax.broadcasted_iota(jnp.int32, (MESH_X, LANES), 0)
    inner = jnp.where((column == 0) | (column == MESH_X - 1), 1.0, 2.0)
    for i in range(MESH_Y):
        here = v[MESH_X * i : MESH_X * (i + 1), :]
        beside = jnp.where(column == 0, 0.0, pltpu.roll(here, 1, axis=0))
        beside += jnp.where(column == MESH_X - 1, 0.0, pltpu.roll(here, MESH_X - 1, axis=0))
        degree = inner
        if i > 0:
            beside += v[MESH_X * (i - 1) : MESH_X * i, :]
            degree = degree + 1.0
        if i < MESH_Y - 1:
            beside += v[MESH_X * (i + 1) : MESH_X * (i + 2), :]
            degree = degree + 1.0
        out[MESH_X * i : MESH_X * (i + 1), :] = (
            stiffness * (degree * here - beside) + anchor_t[MESH_X * i : MESH_X * (i + 1), :] * here
        )


def add_forces(out, east, west, south, north):
    out[RIGHT, :] += east
    out[LEFT, :] -= west
    out[BOTTOM, :] += south
    out[TOP, :] -= north


def inner_product(a, b):
    return jnp.sum(a[...] * b[...], axis=0, keepdims=True)


def apply_exchanged(v, out, tables_here, beyond, stiffness, anchor_t, tiles):
    from_east, from_west, from_south, from_north = beyond
    lane = lax.broadcasted_iota(jnp.int32, (1, LANES), 1) % COMP
    apply_inside(v, out, stiffness, anchor_t)
    top, bottom = v[TOP, :], v[BOTTOM, :]
    below = jnp.where(
        lane == tiles - 1,
        pltpu.roll(from_south[...], tiles - 1, axis=1),
        pltpu.roll(top, LANES - 1, axis=1),
    )
    above = jnp.where(
        lane == 0,
        pltpu.roll(from_north[...], LANES - (tiles - 1), axis=1),
        pltpu.roll(bottom, 1, axis=1),
    )
    east, west, south, north = tables_here
    add_forces(
        out,
        edge_force(east, v[RIGHT, :] - from_east[...]),
        edge_force(west, from_west[...] - v[LEFT, :]),
        edge_force(south, bottom - below),
        edge_force(north, above - top),
    )


def start_kernel(tiles, *refs):
    ins, outs = refs[:8], refs[8:]
    info, anchor_t = ins[5], ins[7]
    v0, v1, left, right, top, bottom, match, gram, flip = outs
    tabs = pair_tables(tiles, *ins[:7])
    east, west, south, north = tabs
    stiffness = both(info[4:5, :])
    force_e = load_force(east, MESH_Y)
    force_w = load_force(west, MESH_Y)
    force_s = load_force(south, MESH_X)
    force_n = load_force(north, MESH_X)
    v0[...] = jnp.zeros_like(v0)
    add_forces(v0, force_e, force_w, force_s, force_n)
    apply_inside(v0, v1, stiffness, anchor_t)
    add_forces(
        v1,
        edge_force(east, v0[RIGHT, :] + force_e),
        edge_force(west, force_w - v0[LEFT, :]),
        edge_force(south, v0[BOTTOM, :] + force_s),
        edge_force(north, force_n - v0[TOP, :]),
    )
    left[...] = v1[LEFT, :]
    right[...] = v1[RIGHT, :]
    top[...] = v1[TOP, :]
    bottom[...] = v1[BOTTOM, :]
    gram[...] = jnp.zeros_like(gram)
    gram[0:1, :] = inner_product(v0, v0)
    gram[1:2, :] = inner_product(v0, v1)
    gram[2:3, :] = inner_product(v1, v1)
    flip[...] = jnp.zeros_like(flip)
    for q, (weight, x, y, _) in enumerate((east, south)):
        for s, rows in enumerate((weight, x, y)):
            flip[24 * q + 8 * s : 24 * q + 8 * s + 8, :] = rows
    match[...] = flip[...].T[0:tiles, 0:48]


def next_kernel(tiles, want_edges, *refs):
    ins, outs = refs[:14], refs[14:]
    info, anchor_t, previous, v, gram_in, = ins[5], ins[7], ins[8], ins[9], None
    beyond = ins[10:14]
    tabs = pair_tables(tiles, *ins[:7])
    stiffness = both(info[4:5, :])
    out, gram = outs[0], outs[1]
    apply_exchanged(v, out, tabs, beyond, stiffness, anchor_t, tiles)
    gram[...] = jnp.zeros_like(gram)
    if want_edges:
        left, right, top, bottom = outs[2:6]
        left[...] = out[LEFT, :]
        right[...] = out[RIGHT, :]
        top[...] = out[TOP, :]
        bottom[...] = out[BOTTOM, :]
        gram[3:4, :] = inner_product(v, out)
        gram[4:5, :] = inner_product(out, out)
    else:
        gram[5:6, :] = inner_product(v, out)


def final_kernel(tiles, gram, v0, v1, v2, v3, positions, residual):
    moments = jnp.sum(gram[...], axis=1, keepdims=True)
    mu = [moments[k : k + 1, :] for k in range(6)]
    zero, one = jnp.zeros_like(mu[0]), jnp.ones_like(mu[0])

    def form(a, b, shift):
        out = zero
        for i, x in enumerate(a):
            for j, y in enumerate(b):
                out = out + x * y * mu[i + j + shift]
        return out

    res, direction, pos = [one], [one], []
    norm_now = mu[0]
    for iteration in range(3):
        step = norm_now / form(direction, direction, 1)
        pos = [p + step * d for p, d in zip(pos + [zero] * (len(direction) - len(pos)), direction)]
        res = [
            r - step * d for r, d in zip(res + [zero], [zero] + direction)
        ]
        if iteration == 2:
            break
        norm_next = form(res, res, 0)
        ratio = norm_next / norm_now
        direction = [r + ratio * d for r, d in zip(res, direction + [zero])]
        norm_now = norm_next
    for out, coefficients in ((positions, pos), (residual, res)):
        for i in range(NODES // LANES):
            rows = slice(LANES * i, LANES * (i + 1))
            part = sum(c * v[rows, :] for c, v in zip(coefficients, (v0, v1, v2, v3)))
            part = part.T
            for c in range(2):
                out[:, c, rows] = part[COMP * c : COMP * c + tiles, :]


def shifted(x, axis, by):
    peers = lax.axis_size(axis)
    return lax.ppermute(x, axis, [(i, i + by) for i in range(peers) if 0 <= i + by < peers])


def add_over(x, axis, stride, radix):
    peers = lax.axis_size(axis)
    got = []
    for k in range(1, radix):
        pairs = []
        for i in range(peers):
            digit = i // stride % radix
            pairs.append((i, i + ((digit + k) % radix - digit) * stride))
        got.append(lax.ppermute(x, axis, pairs))
    for other in got:
        x = x + other
    return x


def sum_everywhere(x):
    for axis, order in (("row", (2, 4, 4)), ("col", (4,))):
        left, stride = lax.axis_size(axis), 1
        for radix in order:
            radix = math.gcd(radix, left)
            if radix > 1:
                x = add_over(x, axis, stride, radix)
                stride, left = stride * radix, left // radix
        if left > 1:
            x = add_over(x, axis, stride, left)
    return x


def per_device(strips, pair_counts, pair_offsets, tile_stiffness, anchor):
    tiles = strips.shape[0]
    half = tiles // 2
    own = strips[:, 0]
    field, column, line = (NODES, LANES), (MESH_Y, LANES), (MESH_X, LANES)
    from_east_strips = shifted(own[:half, 0, :, :WIDE], "row", -1)
    from_west_strips = shifted(own[half:, 3, :, :WIDE], "row", 1)
    next_top = shifted(own[0:1, 1, :, :WIDE], "col", -1)
    info, anchor_t = whole(
        prepare_kernel,
        [(8, LANES), field],
        "prepare",
        [pltpu.VMEM((LANES, LANES), F32), pltpu.VMEM((LANES, NODES), F32)],
    )(pair_counts[:, 0], pair_offsets[:, 0], tile_stiffness, anchor[:, 0])
    info_west = shifted(info, "row", 1)
    tabs = tables()
    terms_south = south_terms(own, next_top, info, tabs)
    from_north = shifted(terms_south, "col", 1)
    terms_side = side_terms(own, from_east_strips, from_west_strips, info, info_west, tabs)
    from_east = shifted(terms_side, "row", -1)
    from_west = shifted(terms_side, "row", 1)
    common = (terms_south, terms_side, from_east, from_west, from_north, info, info_west, anchor_t)

    def exchanged(left, right, top, bottom):
        return (
            shifted(left, "row", -1),
            shifted(right, "row", 1),
            shifted(top, "col", -1),
            shifted(bottom, "col", 1),
        )

    v0, v1, *edges, match, gram_a = whole(
        functools.partial(start_kernel, tiles),
        [field, field, column, column, line, line, (tiles, 48), (8, LANES)],
        "start",
        [pltpu.VMEM((LANES, LANES), F32)],
    )(*common)
    v2, gram_b, *edges = whole(
        functools.partial(next_kernel, tiles, True),
        [field, (8, LANES), column, column, line, line],
        "second",
    )(*common, v0, v1, *exchanged(*edges))
    v3, gram_c = whole(
        functools.partial(next_kernel, tiles, False), [field, (8, LANES)], "third"
    )(*common, v1, v2, *exchanged(*edges))
    gram = sum_everywhere(gram_a + gram_b + gram_c)
    positions, residual = whole(
        functools.partial(final_kernel, tiles),
        [(tiles, 2, NODES), (tiles, 2, NODES)],
        "combine",
    )(gram, v0, v1, v2, v3)
    return match.reshape(tiles, 1, 2, 3, 8), positions[:, None], residual[:, None]


def solution(mesh):
    return jax.shard_map(
        per_device,
        mesh=mesh,
        in_specs=(
            P("col", "row", None, None, None),
            P("col", "row", None),
            P("col", "row", None),
            P("col", "row"),
            P("col", "row", None),
        ),
        out_specs=(
            P("col", "row", None, None, None),
            P("col", "row", None, None),
            P("col", "row", None, None),
        ),
        check_vma=False,
    )
```

```python
import functools
import math

import jax
import jax.numpy as jnp
import numpy as np
from jax import lax
from jax.experimental import pallas as pl
from jax.experimental.pallas import tpu as pltpu
from jax.sharding import PartitionSpec as P

MESH_Y = 28
MESH_X = 32
NODES = MESH_Y * MESH_X
PATCH = 64
MOST = 5
WIDE = MOST * PATCH
ROWS = 32
EXTRA = 40
LANES = 128
COMP = 64
GROUP = 10
TALL = MESH_X * MESH_X
SMALL_WEIGHT = 1e-06
GAP = 16.0
F32 = jnp.float32
BF16 = jnp.bfloat16
HIGHEST = lax.Precision.HIGHEST


def tables():
    index = np.arange(PATCH)
    angle = (index[:, None] * index[None, :] % PATCH) * (2.0 * math.pi / PATCH)
    bf = jnp.bfloat16
    cos = np.cos(angle).astype(bf).astype(np.float32)
    sin = np.sin(angle).astype(bf).astype(np.float32)
    half = PATCH // 2
    depth = np.concatenate([cos[: half + 1], -sin[1:half]])
    pair = np.eye(2, dtype=np.float32)
    cos2, sin2 = np.kron(pair, cos), np.kron(pair, sin)
    forward = np.block([[cos2, -sin2], [sin2, cos2]])
    ends = np.kron(pair, np.concatenate([cos2, -sin2], axis=1))
    back = np.block([[cos2, sin2], [-sin2, cos2]])
    back_swapped = np.block([[cos2, sin2], [sin2, -cos2]])
    twice = np.full((PATCH,), 2.0, np.float32)
    twice[0] = twice[half] = 1.0
    final = np.concatenate([cos[:, : half + 1], -sin[:, 1:half]], axis=1) * twice
    offset = ((index + PATCH // 2) % PATCH - PATCH // 2).astype(np.float32)
    pick = np.zeros((8, LANES), np.float32)
    pick[0, :PATCH] = 1.0
    pick[1, PATCH:] = 1.0
    pick[2, :PATCH] = offset
    pick[3, PATCH:] = offset
    rows = np.repeat(offset[:, None], LANES, axis=1)
    as_bf = lambda a: jnp.asarray(a, BF16)
    backs = np.stack([back, back_swapped])
    return as_bf(depth), as_bf(forward), as_bf(ends), as_bf(backs), as_bf(final), jnp.asarray(pick), jnp.asarray(rows)


def block_pairs(strips):
    out = []
    for one, two in zip(strips[0::2], strips[1::2]):
        out += [
            one[:, 0:128],
            one[:, 128:256],
            two[:, 0:128],
            two[:, 128:256],
            jnp.concatenate([one[:, 256:320], two[:, 256:320]], axis=1),
        ]
    return out


def cross_power(first_real, first_imag, second_real, second_imag):
    denominator = (
        0.5
        * (
            first_real * first_real
            + first_imag * first_imag
            + second_real * second_real
            + second_imag * second_imag
        )
        + 1.0
    )
    inverse = 1.0 / denominator
    real = (first_real * second_real + first_imag * second_imag) * inverse
    imag = (first_imag * second_real - first_real * second_imag) * inverse
    return real, imag


def correlate_group(cols, depth, forward, ends, back, final, rows, r0, r1, at):
    count = len(cols)
    half = count // 2
    lanes = [slice(LANES * i, LANES * (i + 1)) for i in range(count)]
    spec = jnp.dot(depth, jnp.concatenate(cols, axis=1), preferred_element_type=F32)
    stacked = jnp.concatenate(
        [jnp.concatenate([spec[:ROWS, s], spec[ROWS:, s]], axis=1) for s in lanes], axis=0
    ).astype(BF16)
    end_rows = jnp.concatenate(
        [
            jnp.concatenate([spec[0:1, s] for s in lanes], axis=0),
            jnp.concatenate([spec[ROWS : ROWS + 1, s] for s in lanes], axis=0),
        ],
        axis=1,
    ).astype(BF16)
    full = jnp.dot(stacked, forward, preferred_element_type=F32)
    end = jnp.dot(end_rows, ends, preferred_element_type=F32)
    split = half * ROWS
    cross_real, cross_imag = cross_power(
        full[:split, :LANES], full[:split, LANES:], full[split:, :LANES], full[split:, LANES:]
    )
    cross = jnp.concatenate([cross_real, cross_imag], axis=1).astype(BF16)
    end_cross = []
    for s in (0, 2 * LANES):
        end_cross.append(
            jnp.concatenate(
                cross_power(
                    end[:half, s : s + LANES],
                    end[:half, s + LANES : s + 2 * LANES],
                    end[half:, s : s + LANES],
                    end[half:, s + LANES : s + 2 * LANES],
                ),
                axis=1,
            )
        )
    end_back = [
        jnp.dot(c.astype(BF16), back[:, :LANES], preferred_element_type=F32) for c in end_cross
    ]
    back_half = jnp.dot(cross, back, preferred_element_type=F32)
    is_end = lax.broadcasted_iota(jnp.int32, (8, LANES), 0) == 0

    def side(i):
        parts = []
        for part in range(2):
            block = back_half[ROWS * i : ROWS * (i + 1), lanes[part]]
            parts.append(jnp.where(is_end, end_back[part][i : i + 1], block[:8]))
            parts.append(block[8:])
        return jnp.concatenate(parts, axis=0)

    sides = jnp.concatenate([side(i) for i in range(half)], axis=1).astype(BF16)
    surface = jnp.dot(final, sides, preferred_element_type=F32)
    for i in range(half):
        part = surface[:, lanes[i]]
        power = part * part
        total = jnp.sum(power, axis=0, keepdims=True)
        moment = jnp.sum(power * rows, axis=0, keepdims=True)
        place = i % 5
        if i == 5 * (half // 5):
            r0[0, EXTRA : EXTRA + 1, :] = total
            r1[0, EXTRA : EXTRA + 1, :] = moment
        elif place < 4:
            row = at + 2 * (i // 5) + place // 2
            r0[place % 2, pl.ds(row, 1), :] = total
            r1[place % 2, pl.ds(row, 1), :] = moment
        else:
            for row in (at + 2 * (i // 5), at + 2 * (i // 5) + 1):
                r0[2, pl.ds(row, 1), :] = total
                r1[2, pl.ds(row, 1), :] = moment


def lane_sums(pick, table):
    return lax.dot_general(
        pick, table, (((1,), (1,)), ((), ())), precision=HIGHEST, preferred_element_type=F32
    )


def finish_terms(pick, r0, r1, counts, offsets, out):
    scale = 1.0 / float(PATCH * PATCH) ** 2
    even = lax.broadcasted_iota(jnp.int32, (1, LANES), 1) % 2 == 0
    plain = [lane_sums(pick, r0[s]) for s in range(3)]
    tilted = [lane_sums(pick, r1[s]) for s in range(3)]
    out[...] = jnp.zeros_like(out)
    for k in range(MOST):
        slot, side = k // 2, k % 2
        if k < 4:
            weight = plain[slot][side : side + 1]
            along = plain[slot][2 + side : 3 + side]
            deep = tilted[slot][side : side + 1]
        else:
            weight = jnp.where(even, plain[2][0:1], plain[2][1:2])
            along = jnp.where(even, plain[2][2:3], plain[2][3:4])
            deep = jnp.where(even, tilted[2][0:1], tilted[2][1:2])
        valid = counts > float(k) + 0.5
        weight = weight * scale
        inverse = scale / (weight + SMALL_WEIGHT)
        out[k : k + 1, :] = jnp.where(valid, weight, 0.0)
        out[8 + k : 9 + k, :] = jnp.where(valid, deep * inverse, 0.0)
        out[16 + k : 17 + k, :] = jnp.where(valid, along * inverse, 0.0)
    out[24:25, :] = offsets


def south_kernel(*refs):
    first, seconds = refs[0], refs[1 : 1 + GROUP]
    nxt, info, anchor_t, depth, forward, ends, back, final, pick, rows, out, r0, r1 = refs[1 + GROUP :]
    step = pl.program_id(0)
    last = pl.num_programs(0) - 1

    @pl.when(step == 0)
    def _():
        r0[...] = jnp.zeros_like(r0)
        r1[...] = jnp.zeros_like(r1)

    seconds = [ref[0, 0, :, :WIDE] for ref in seconds]
    seconds[-1] = jnp.where(step == last, nxt[0, :, :WIDE], seconds[-1])
    firsts = [first[j, 0, :, :WIDE] for j in range(GROUP)]
    correlate_group(
        block_pairs(firsts) + block_pairs(seconds),
        depth[...], forward[...], ends[...], back[0], final[...], rows[...], r0, r1, GROUP * step,
    )

    @pl.when(step == last)
    def _():
        finish_terms(pick[...], r0, r1, info[2:3, :], info[3:4, :], out)
        out[25:26, :] = info[4:5, :]
        out[32:, :] = anchor_t[...]


def side_kernel(own, from_east, from_west, own_extra, extra, info, depth, forward, ends, back, final, pick, rows, out, r0, r1):
    step = pl.program_id(0)
    steps = pl.num_programs(0)

    @pl.when(step == 0)
    def _():
        r0[...] = jnp.zeros_like(r0)
        r1[...] = jnp.zeros_like(r1)

    east_part = step < steps // 2
    others = []
    for slot in range(GROUP // 2):
        packed = jnp.where(east_part, from_east[slot], from_west[slot])
        others += [packed[:, LANES * i : LANES * (i + 1)] for i in range(5)]
    owns = block_pairs([own[j, 0, :, :WIDE] for j in range(GROUP)])
    correlate_group(
        owns + [own_extra[0, 0]] + others + [extra[0, :, :LANES]],
        depth[...], forward[...], ends[...], back[0], final[...], rows[...], r0, r1, GROUP * step,
    )

    @pl.when(step == steps - 1)
    def _():
        lane = lax.broadcasted_iota(jnp.int32, (8, LANES), 1)
        info_west = extra[0, 0:16, 2 * LANES : 3 * LANES].astype(F32)[0:8]
        table = jnp.where(lane < GROUP * (steps // 2), info[...], info_west)
        table = jnp.where(lane == EXTRA, pltpu.roll(info_west, EXTRA, axis=1), table)
        finish_terms(pick[...], r0, r1, table[0:1], table[1:2], out)


def const_spec(shape):
    return pl.BlockSpec(shape, lambda i: (0,) * len(shape))


SUMS = [pltpu.VMEM((3, LANES, LANES), F32), pltpu.VMEM((3, LANES, LANES), F32)]
VMEM_BYTES = 48 * 1024 * 1024


def table_specs(tabs, back_map):
    depth, forward, ends, backs, final, pick, rows = tabs
    return [
        const_spec(depth.shape),
        const_spec(forward.shape),
        const_spec(ends.shape),
        pl.BlockSpec((1, 2 * LANES, 2 * LANES), back_map),
        const_spec(final.shape),
        const_spec(pick.shape),
        const_spec(rows.shape),
    ]


def correlation_cost(pairs):
    return pl.CostEstimate(
        flops=pairs * MOST * 12_000_000, bytes_accessed=pairs * 2 * 64 * 384 * 2, transcendentals=0
    )


def south_terms(strips, nxt, info, anchor_t, tabs):
    tiles = strips.shape[0]
    steps = tiles // GROUP
    side = 384

    def second_spec(j):
        return pl.BlockSpec(
            (1, 1, PATCH, side), lambda i: (jnp.minimum(GROUP * i + 1 + j, tiles - 1), 1, 0, 0)
        )

    return pl.pallas_call(
        south_kernel,
        name="south_pairs",
        grid=(steps,),
        in_specs=[pl.BlockSpec((GROUP, 1, PATCH, side), lambda i: (i, 2, 0, 0))]
        + [second_spec(j) for j in range(GROUP)]
        + [const_spec(nxt.shape), const_spec(info.shape)]
        + [pl.BlockSpec((MESH_X, LANES), lambda i: (MESH_Y - 1, 0))]
        + table_specs(tabs, lambda i: (0, 0, 0)),
        out_specs=const_spec((64, LANES)),
        out_shape=jax.ShapeDtypeStruct((64, LANES), F32),
        scratch_shapes=SUMS,
        compiler_params=pltpu.CompilerParams(vmem_limit_bytes=VMEM_BYTES),
        cost_estimate=correlation_cost(tiles),
    )(*[strips] * (1 + GROUP), nxt, info, anchor_t, *tabs)


def side_terms(strips, from_east, from_west, info, tabs):
    tiles = strips.shape[0]
    steps = tiles // GROUP
    mid = steps // 2
    packed = (GROUP // 2, PATCH, 2 * WIDE)
    return pl.pallas_call(
        side_kernel,
        name="side_pairs",
        grid=(steps,),
        in_specs=[
            pl.BlockSpec((GROUP, 1, PATCH, 384), lambda i: (i, jnp.where(i < mid, 3, 0), 0, 0)),
            pl.BlockSpec(packed, lambda i: (jnp.minimum(i, mid - 1), 0, 0)),
            pl.BlockSpec(packed, lambda i: (jnp.maximum(i - mid, 0), 0, 0)),
            pl.BlockSpec((1, 1, PATCH, LANES), lambda i: (0, 0, 0, 0)),
            pl.BlockSpec((1, PATCH, 2 * WIDE), lambda i: (tiles // 4, 0, 0)),
            const_spec(info.shape),
        ]
        + table_specs(tabs, lambda i: (jnp.where(i < mid, 0, 1), 0, 0)),
        out_specs=const_spec((32, LANES)),
        out_shape=jax.ShapeDtypeStruct((32, LANES), F32),
        scratch_shapes=SUMS,
        compiler_params=pltpu.CompilerParams(vmem_limit_bytes=VMEM_BYTES),
        cost_estimate=correlation_cost(tiles),
    )(strips, from_east, from_west, strips, from_west, info, *tabs)


def prepare_kernel(strips, counts, offsets, stiffness, anchor, west, east, north, info, anchor_t, left, right, small, wide, sems):
    tiles = anchor.shape[0]
    half = tiles // 2
    moves = [
        (strips.at[pl.ds(half, half), 3, :, pl.ds(0, 384)], right),
        (strips.at[pl.ds(0, half), 0, :, pl.ds(0, 384)], left),
        (strips.at[0, 3, :, pl.ds(0, LANES)], east.at[half // 2, :, pl.ds(0, LANES)]),
        (strips.at[0, 1, :, pl.ds(0, 384)], north.at[0]),
    ]
    moves = [pltpu.make_async_copy(a, b, sems.at[k]) for k, (a, b) in enumerate(moves)]
    for move in moves:
        move.start()
    small[...] = jnp.zeros_like(small)
    small[0:tiles, 0:1] = counts[:, 0:1].astype(F32)
    small[0:tiles, 1:2] = offsets[:, 0:1].astype(F32)
    small[0:tiles, 2:3] = counts[:, 1:2].astype(F32)
    small[0:tiles, 3:4] = offsets[:, 1:2].astype(F32)
    small[0:tiles, 4:5] = stiffness[...]
    flat = small[...].T
    info[...] = flat[0:8, :]
    wide[...] = jnp.zeros_like(wide)
    wide[0:tiles, :] = anchor[...]
    wide[COMP : COMP + tiles, :] = anchor[...]
    for i in range(NODES // LANES):
        anchor_t[LANES * i : LANES * (i + 1), :] = wide[:, LANES * i : LANES * (i + 1)].T
    east[half // 2, :, LANES:] = jnp.zeros((PATCH, 2 * WIDE - LANES), BF16)
    east[half // 2, 0:16, 2 * LANES : 3 * LANES] = flat[0:16, :].astype(BF16)
    for move, source, packed in ((moves[0], right, east), (moves[1], left, west)):
        move.wait()
        for slot in range(half // 2):
            columns = block_pairs([source[2 * slot + j, :, :WIDE] for j in range(2)])
            for i, x in enumerate(columns):
                packed[slot, :, LANES * i : LANES * (i + 1)] = x
    moves[2].wait()
    moves[3].wait()


def prepare(strips, counts, offsets, stiffness, anchor):
    tiles = anchor.shape[0]
    vmem = pl.BlockSpec(memory_space=pltpu.VMEM)
    slots = tiles // 4
    return pl.pallas_call(
        prepare_kernel,
        name="prepare",
        in_specs=[pl.BlockSpec(memory_space=pl.ANY)] + [vmem] * 4,
        out_specs=[vmem] * 5,
        out_shape=[
            jax.ShapeDtypeStruct((slots, PATCH, 2 * WIDE), BF16),
            jax.ShapeDtypeStruct((slots + 1, PATCH, 2 * WIDE), BF16),
            jax.ShapeDtypeStruct((1, PATCH, 384), BF16),
            jax.ShapeDtypeStruct((8, LANES), F32),
            jax.ShapeDtypeStruct((NODES, LANES), F32),
        ],
        scratch_shapes=[
            pltpu.VMEM((tiles // 2, PATCH, 384), BF16),
            pltpu.VMEM((tiles // 2, PATCH, 384), BF16),
            pltpu.VMEM((LANES, LANES), F32),
            pltpu.VMEM((LANES, NODES), F32),
            pltpu.SemaphoreType.DMA((4,)),
        ],
        compiler_params=pltpu.CompilerParams(vmem_limit_bytes=VMEM_BYTES),
    )(strips, counts, offsets, stiffness, anchor)


def whole(kernel, outs, name, scratch=()):
    vmem = pl.BlockSpec(memory_space=pltpu.VMEM)
    shapes = [jax.ShapeDtypeStruct(s, F32) for s in outs]

    def call(*args):
        return pl.pallas_call(
            kernel,
            name=name,
            in_specs=[vmem] * len(args),
            out_specs=[vmem] * len(outs),
            out_shape=shapes,
            scratch_shapes=list(scratch),
            compiler_params=pltpu.CompilerParams(vmem_limit_bytes=VMEM_BYTES),
            cost_estimate=pl.CostEstimate(
                flops=4_000_000, bytes_accessed=2_000_000, transcendentals=0
            ),
        )(*args)

    return call


def both(x):
    return x + pltpu.roll(x, COMP, axis=1)


def tents(offset, count):
    offset = both(offset)
    node = lax.broadcasted_iota(jnp.int32, (count, LANES), 0).astype(F32) * GAP + GAP / 2
    out = []
    for k in range(MOST):
        centre = offset + float(PATCH * k + PATCH // 2)
        out.append(jnp.maximum(0.0, 1.0 - jnp.abs(centre - node) / GAP))
    return out


def load_force(table):
    weight, x, y, shapes = table
    lane = lax.broadcasted_iota(jnp.int32, (1, LANES), 1)
    loads = weight * jnp.where(lane < COMP, x, pltpu.roll(y, COMP, axis=1))
    return sum(t * loads[k : k + 1] for k, t in enumerate(shapes))


def edge_force(table, difference):
    weight, _, _, shapes = table
    out = 0.0
    for k, t in enumerate(shapes):
        projected = jnp.sum(t * difference, axis=0, keepdims=True)
        out = out + t * (projected * weight[k : k + 1])
    return out


LEFT = pl.ds(0, MESH_X, stride=MESH_X)
RIGHT = pl.ds(MESH_X - 1, MESH_X, stride=MESH_X)
TOP = pl.ds(0, MESH_X)
BOTTOM = pl.ds(NODES - MESH_X, MESH_X)


def apply_inside(v, out, stiffness, anchor_t):
    column = lax.broadcasted_iota(jnp.int32, (MESH_X, LANES), 0)
    inner = jnp.where((column == 0) | (column == MESH_X - 1), 1.0, 2.0)
    for i in range(MESH_Y):
        here = v[MESH_X * i : MESH_X * (i + 1), :]
        beside = along_row(here, column)
        degree = inner
        if i > 0:
            beside += v[MESH_X * (i - 1) : MESH_X * i, :]
            degree = degree + 1.0
        if i < MESH_Y - 1:
            beside += v[MESH_X * (i + 1) : MESH_X * (i + 2), :]
            degree = degree + 1.0
        out[MESH_X * i : MESH_X * (i + 1), :] = (
            stiffness * (degree * here - beside) + anchor_t[MESH_X * i : MESH_X * (i + 1), :] * here
        )
    out[NODES:, :] = jnp.zeros((TALL - NODES, LANES), F32)


def along_row(x, node):
    before = jnp.where(node == 0, 0.0, pltpu.roll(x, 1, axis=0))
    return before + jnp.where(node == MESH_X - 1, 0.0, pltpu.roll(x, MESH_X - 1, axis=0))


def along_column(x, node):
    after = jnp.where(node >= MESH_Y - 1, 0.0, pltpu.roll(x, MESH_X - 1, axis=0))
    return after + jnp.where(node >= MESH_Y, 0.0, pltpu.roll(x, 1, axis=0))


def add_forces(out, east, west, south, north):
    out[RIGHT, :] += east
    out[LEFT, :] -= west
    out[BOTTOM, :] += south
    out[TOP, :] -= north


def inner_product(a, b):
    return jnp.sum(a[0:NODES, :] * b[0:NODES, :], axis=0, keepdims=True)


def message_kernel(tiles, terms_south, terms_side, from_north, info, anchor_t, to_west, to_east, to_north):
    lane = lax.broadcasted_iota(jnp.int32, (1, LANES), 1)
    side = terms_side[...]
    for out in (to_west, to_east, to_north):
        out[0:32, :] = side
        out[25:26, :] = info[4:5, :]
    south = terms_south[0:32, :]
    north = roll_tiles(south, 1, from_north[0:32, :], tiles)
    for q, terms in enumerate((south, north)):
        for k, row in enumerate((0, 8, 16, 24)):
            to_west[32 + 4 * q + k : 33 + 4 * q + k, :] = terms[row : row + 1]
    first = anchor_t[pl.ds(0, MESH_Y, stride=MESH_X), :]
    second = anchor_t[pl.ds(1, MESH_Y, stride=MESH_X), :]
    to_west[40 : 40 + MESH_Y, :] = jnp.where(lane < COMP, first, second)
    to_west[40 + MESH_Y :, :] = jnp.zeros((4, LANES), F32)
    to_east[32 : 32 + MESH_Y, :] = anchor_t[pl.ds(MESH_X - 1, MESH_Y, stride=MESH_X), :]
    to_east[32 + MESH_Y :, :] = jnp.zeros((4, LANES), F32)
    to_north[32:, :] = jnp.where(
        lane == 0, anchor_t[0:MESH_X, :], pltpu.roll(anchor_t[MESH_X : 2 * MESH_X, :], 1, axis=1)
    )


def roll_tiles(x, by, outside, tiles):
    lane = lax.broadcasted_iota(jnp.int32, (1, LANES), 1) % COMP
    if by == 1:
        edge, beyond = lane == 0, pltpu.roll(outside, LANES - (tiles - 1), axis=1)
    else:
        edge, beyond = lane == tiles - 1, pltpu.roll(outside, tiles - 1, axis=1)
    return jnp.where(edge, beyond, pltpu.roll(x, by % LANES, axis=1))


def pick_lane(x, source, target):
    lane = lax.broadcasted_iota(jnp.int32, (1, LANES), 1)
    return both(jnp.where(lane == target, pltpu.roll(x, (target - source) % LANES, axis=1), 0.0))


def near_tents(offset):
    return [
        jnp.maximum(0.0, 1.0 - jnp.abs(offset + (PATCH // 2 - GAP * n - GAP / 2)) / GAP) for n in (1, 2)
    ]


def near_pair(weight, x, y, offset):
    one, two = near_tents(offset)
    lane = lax.broadcasted_iota(jnp.int32, (1, LANES), 1)
    load = weight * jnp.where(lane < COMP, x, y)
    force = weight * one * (one * (2.0 * one * load) + two * (2.0 * two * load))
    return one * load, two * load, force


def mesh_kernel(tiles, *refs):
    terms_south, terms_side, from_east, from_west, from_south, from_north, info, anchor_t = refs[:8]
    v0, v1, v2, v3, match, gram, flip = refs[8:]
    lane = lax.broadcasted_iota(jnp.int32, (1, LANES), 1)
    node = lax.broadcasted_iota(jnp.int32, (MESH_X, LANES), 0)
    low, inside = lane < tiles // 2, lane < tiles
    side = terms_side[...]
    south_terms = terms_south[0:32, :]
    terms = [
        jnp.where(low, side, from_east[0:32, :]),
        jnp.where(low, from_west[0:32, :], side),
        south_terms,
        roll_tiles(south_terms, 1, from_north[0:32, :], tiles),
    ]
    tables_here = []
    for q, table in enumerate(terms):
        table = jnp.where(inside, table, 0.0)
        deep, along = table[8:16], table[16:24]
        x, y = (deep, along) if q < 2 else (along, deep)
        tables_here.append((both(table[0:8]), x, y, tents(table[24:25], MESH_X)))
    east, west, south, north = tables_here
    stiffness = both(info[4:5, :])

    flip[...] = jnp.zeros_like(flip)
    for q, (weight, x, y, _) in enumerate((east, south)):
        for s, rows in enumerate((jnp.where(lane < COMP, weight, 0.0), x, y)):
            flip[24 * q + 8 * s : 24 * q + 8 * s + 8, :] = rows
    match[...] = flip[...].T[0:tiles, 0:48]

    force_e, force_w, force_s, force_n = [load_force(t) for t in tables_here]
    v0[...] = jnp.zeros_like(v0)
    add_forces(v0, force_e, force_w, force_s, force_n)

    outside_east, outside_west = both(from_east[25:26, :]), both(from_west[25:26, :])
    packed = from_east[40:72, :]
    turned = pltpu.roll(packed, COMP, axis=1)
    anchor_e0 = jnp.where(lane < COMP, packed, turned)
    anchor_e1 = jnp.where(lane < COMP, turned, packed)
    anchor_w0 = from_west[32:64, :]
    last = tiles - 1
    outside_south = pick_lane(from_south[25:26, :], 0, last)
    anchor_s0 = pick_lane(from_south[32:64, :], 0, last)
    anchor_s1 = pick_lane(from_south[32:64, :], 1, last)
    outside_north = pick_lane(from_north[25:26, :], last, 0)
    anchor_n0 = pick_lane(from_north[32:64, :], last, 0)

    degree_c = jnp.where((node == 0) | (node == MESH_Y - 1), 2.0, 3.0)
    degree_r = jnp.where((node == 0) | (node == MESH_X - 1), 2.0, 3.0)

    near_s = near_pair(*[both(from_east[32 + k : 33 + k, :]) for k in (0, 2, 1, 3)])
    near_n = near_pair(*[both(from_east[36 + k : 37 + k, :]) for k in (0, 2, 1, 3)])
    at_ends = lambda a, b, x, y: jnp.where(node == a, x, 0.0) - jnp.where(node == b, y, 0.0)
    e0 = -force_e
    e1 = at_ends(MESH_Y - 1, 0, near_s[0], near_n[0])
    e2 = at_ends(MESH_Y - 1, 0, near_s[1], near_n[1])
    e1_pairs = at_ends(MESH_Y - 1, 0, near_s[2], near_n[2])
    w0 = force_w
    near_e = near_pair(*[pick_lane(from_south[k : k + 1, :], 0, last) for k in (0, 8, 16, 24)])
    near_w = near_pair(*[pick_lane(from_south[k : k + 1, :], EXTRA, last) for k in (0, 8, 16, 24)])
    s0 = -force_s
    s1 = at_ends(MESH_X - 1, 0, near_e[0], near_w[0])
    s2 = at_ends(MESH_X - 1, 0, near_e[1], near_w[1])
    s1_pairs = at_ends(MESH_X - 1, 0, near_e[2], near_w[2])
    n0 = force_n

    apply_inside(v0, v1, stiffness, anchor_t)
    pull_e = edge_force(east, v0[RIGHT, :] - e0)
    pull_w = edge_force(west, w0 - v0[LEFT, :])
    pull_s = edge_force(south, v0[BOTTOM, :] - s0)
    pull_n = edge_force(north, n0 - v0[TOP, :])
    add_forces(v1, pull_e, pull_w, pull_s, pull_n)
    e0, e1 = (
        outside_east * (degree_c * e0 - along_column(e0, node) - e1) + anchor_e0 * e0 - pull_e,
        outside_east * ((degree_c + 1.0) * e1 - along_column(e1, node) - e0 - e2) + anchor_e1 * e1 + e1_pairs,
    )
    w0, w1 = (
        outside_west * (degree_c * w0 - along_column(w0, node)) + anchor_w0 * w0 + pull_w,
        -outside_west * w0,
    )
    s0, s1 = (
        outside_south * (degree_r * s0 - along_row(s0, node) - s1) + anchor_s0 * s0 - pull_s,
        outside_south * ((degree_r + 1.0) * s1 - along_row(s1, node) - s0 - s2) + anchor_s1 * s1 + s1_pairs,
    )
    n0, n1 = (
        outside_north * (degree_r * n0 - along_row(n0, node)) + anchor_n0 * n0 + pull_n,
        -outside_north * n0,
    )

    def pulls(v, e0, w0, s0, n0):
        top, bottom = v[TOP, :], v[BOTTOM, :]
        spot = lane % COMP
        below = jnp.where(spot == last, s0, pltpu.roll(top, LANES - 1, axis=1))
        above = jnp.where(spot == 0, n0, pltpu.roll(bottom, 1, axis=1))
        return (
            edge_force(east, v[RIGHT, :] - e0),
            edge_force(west, w0 - v[LEFT, :]),
            edge_force(south, bottom - below),
            edge_force(north, above - top),
        )

    apply_inside(v1, v2, stiffness, anchor_t)
    pull_e, pull_w, pull_s, pull_n = pulls(v1, e0, w0, s0, n0)
    add_forces(v2, pull_e, pull_w, pull_s, pull_n)
    e0 = outside_east * (degree_c * e0 - along_column(e0, node) - e1) + anchor_e0 * e0 - pull_e
    w0 = outside_west * (degree_c * w0 - along_column(w0, node) - w1) + anchor_w0 * w0 + pull_w
    s0 = outside_south * (degree_r * s0 - along_row(s0, node) - s1) + anchor_s0 * s0 - pull_s
    n0 = outside_north * (degree_r * n0 - along_row(n0, node) - n1) + anchor_n0 * n0 + pull_n

    apply_inside(v2, v3, stiffness, anchor_t)
    add_forces(v3, *pulls(v2, e0, w0, s0, n0))

    gram[...] = jnp.zeros_like(gram)
    for k, (a, b) in enumerate(((v0, v0), (v0, v1), (v1, v1), (v1, v2), (v2, v2), (v2, v3))):
        gram[k : k + 1, :] = inner_product(a, b)


def final_kernel(tiles, gram, v0, v1, v2, v3, positions, residual):
    moments = jnp.sum(gram[...], axis=1, keepdims=True)
    mu = [moments[k : k + 1, :] for k in range(6)]
    zero, one = jnp.zeros_like(mu[0]), jnp.ones_like(mu[0])

    def form(a, b, shift):
        out = zero
        for i, x in enumerate(a):
            for j, y in enumerate(b):
                out = out + x * y * mu[i + j + shift]
        return out

    res, direction, pos = [one], [one], []
    norm_now = mu[0]
    for iteration in range(3):
        step = norm_now / form(direction, direction, 1)
        pos = [p + step * d for p, d in zip(pos + [zero] * (len(direction) - len(pos)), direction)]
        res = [
            r - step * d for r, d in zip(res + [zero], [zero] + direction)
        ]
        if iteration == 2:
            break
        norm_next = form(res, res, 0)
        ratio = norm_next / norm_now
        direction = [r + ratio * d for r, d in zip(res, direction + [zero])]
        norm_now = norm_next
    for out, coefficients in ((positions, pos), (residual, res)):
        for i in range(NODES // LANES):
            rows = slice(LANES * i, LANES * (i + 1))
            part = sum(c * v[rows, :] for c, v in zip(coefficients, (v0, v1, v2, v3)))
            part = part.T
            for c in range(2):
                out[:, c, rows] = part[COMP * c : COMP * c + tiles, :]


def shifted(x, axis, by):
    peers = lax.axis_size(axis)
    return lax.ppermute(x, axis, [(i, i + by) for i in range(peers) if 0 <= i + by < peers])


def add_over(x, axis, stride, radix):
    peers = lax.axis_size(axis)
    got = []
    for k in range(1, radix):
        pairs = []
        for i in range(peers):
            digit = i // stride % radix
            pairs.append((i, i + ((digit + k) % radix - digit) * stride))
        got.append(lax.ppermute(x, axis, pairs))
    for other in got:
        x = x + other
    return x


def sum_everywhere(x):
    for axis, order in (("row", (2, 4, 4)), ("col", (4,))):
        left, stride = lax.axis_size(axis), 1
        for radix in order:
            radix = math.gcd(radix, left)
            if radix > 1:
                x = add_over(x, axis, stride, radix)
                stride, left = stride * radix, left // radix
        if left > 1:
            x = add_over(x, axis, stride, left)
    return x


def per_device(strips, pair_counts, pair_offsets, tile_stiffness, anchor):
    tiles = strips.shape[0]
    own = strips[:, 0]
    field = (TALL, LANES)
    to_west, to_east, to_north, info, anchor_t = prepare(
        own, pair_counts[:, 0], pair_offsets[:, 0], tile_stiffness, anchor[:, 0]
    )
    strips_west = shifted(to_east, "row", 1)
    strips_east = shifted(to_west, "row", -1)
    next_top = shifted(to_north, "col", -1)
    tabs = tables()
    terms_south = south_terms(own, next_top, info, anchor_t, tabs)
    from_north = shifted(terms_south, "col", 1)
    terms_side = side_terms(own, strips_east, strips_west, info, tabs)
    to_west, to_east, to_north = whole(
        functools.partial(message_kernel, tiles),
        [(72, LANES), (64, LANES), (64, LANES)],
        "messages",
    )(terms_south, terms_side, from_north, info, anchor_t)
    from_east = shifted(to_west, "row", -1)
    from_west = shifted(to_east, "row", 1)
    from_south = shifted(to_north, "col", -1)
    v0, v1, v2, v3, match, gram = whole(
        functools.partial(mesh_kernel, tiles),
        [field, field, field, field, (tiles, 48), (8, LANES)],
        "powers",
        [pltpu.VMEM((LANES, LANES), F32)],
    )(terms_south, terms_side, from_east, from_west, from_south, from_north, info, anchor_t)
    gram = sum_everywhere(gram)
    positions, residual = whole(
        functools.partial(final_kernel, tiles),
        [(tiles, 2, NODES), (tiles, 2, NODES)],
        "combine",
    )(gram, v0, v1, v2, v3)
    return match.reshape(tiles, 1, 2, 3, 8), positions[:, None], residual[:, None]


def solution(mesh):
    return jax.shard_map(
        per_device,
        mesh=mesh,
        in_specs=(
            P("col", "row", None, None, None),
            P("col", "row", None),
            P("col", "row", None),
            P("col", "row"),
            P("col", "row", None),
        ),
        out_specs=(
            P("col", "row", None, None, None),
            P("col", "row", None, None),
            P("col", "row", None, None),
        ),
        check_vma=False,
    )
```

```python
import functools
import math

import jax
import jax.numpy as jnp
import numpy as np
from jax import lax
from jax.experimental import pallas as pl
from jax.experimental.pallas import tpu as pltpu
from jax.sharding import PartitionSpec as P

MESH_Y = 28
MESH_X = 32
NODES = MESH_Y * MESH_X
PATCH = 64
MOST = 5
WIDE = MOST * PATCH
SIDE = 384
ROWS = 32
EXTRA = 40
LANES = 128
COMP = 64
GROUP = 10
TALL = MESH_X * MESH_X
SMALL_WEIGHT = 1e-06
GAP = 16.0
F32 = jnp.float32
BF16 = jnp.bfloat16
HIGHEST = lax.Precision.HIGHEST


def tables():
    index = np.arange(PATCH)
    angle = (index[:, None] * index[None, :] % PATCH) * (2.0 * math.pi / PATCH)
    bf = jnp.bfloat16
    cos = np.cos(angle).astype(bf).astype(np.float32)
    sin = np.sin(angle).astype(bf).astype(np.float32)
    half = PATCH // 2
    depth = np.concatenate([cos[: half + 1], -sin[1:half]])
    pair = np.eye(2, dtype=np.float32)
    cos2, sin2 = np.kron(pair, cos), np.kron(pair, sin)
    forward = np.block([[cos2, -sin2], [sin2, cos2]])
    ends = np.kron(pair, np.concatenate([cos2, -sin2], axis=1))
    back = np.block([[cos2, sin2], [-sin2, cos2]])
    back_swapped = np.block([[cos2, sin2], [sin2, -cos2]])
    twice = np.full((PATCH,), 2.0, np.float32)
    twice[0] = twice[half] = 1.0
    final = np.concatenate([cos[:, : half + 1], -sin[:, 1:half]], axis=1) * twice
    offset = ((index + PATCH // 2) % PATCH - PATCH // 2).astype(np.float32)
    pick = np.zeros((8, LANES), np.float32)
    pick[0, :PATCH] = 1.0
    pick[1, PATCH:] = 1.0
    pick[2, :PATCH] = offset
    pick[3, PATCH:] = offset
    rows = np.repeat(offset[:, None], LANES, axis=1)
    as_bf = lambda a: jnp.asarray(a, BF16)
    backs = np.stack([back, back_swapped])
    return as_bf(depth), as_bf(forward), as_bf(ends), as_bf(backs), as_bf(final), jnp.asarray(pick), jnp.asarray(rows)


def block_pairs(strips):
    out = []
    for one, two in zip(strips[0::2], strips[1::2]):
        out += [
            one[:, 0:128],
            one[:, 128:256],
            two[:, 0:128],
            two[:, 128:256],
            jnp.concatenate([one[:, 256:320], two[:, 256:320]], axis=1),
        ]
    return out


def cross_power(first_real, first_imag, second_real, second_imag):
    denominator = (
        0.5
        * (
            first_real * first_real
            + first_imag * first_imag
            + second_real * second_real
            + second_imag * second_imag
        )
        + 1.0
    )
    inverse = 1.0 / denominator
    real = (first_real * second_real + first_imag * second_imag) * inverse
    imag = (first_imag * second_real - first_real * second_imag) * inverse
    return real, imag


def correlate_group(cols, depth, forward, ends, back, final, rows, r0, r1, at):
    count = len(cols)
    half = count // 2
    lanes = [slice(LANES * i, LANES * (i + 1)) for i in range(count)]
    spec = jnp.dot(depth, jnp.concatenate(cols, axis=1), preferred_element_type=F32)
    stacked = jnp.concatenate(
        [jnp.concatenate([spec[:ROWS, s], spec[ROWS:, s]], axis=1) for s in lanes], axis=0
    ).astype(BF16)
    end_rows = jnp.concatenate(
        [
            jnp.concatenate([spec[0:1, s] for s in lanes], axis=0),
            jnp.concatenate([spec[ROWS : ROWS + 1, s] for s in lanes], axis=0),
        ],
        axis=1,
    ).astype(BF16)
    full = jnp.dot(stacked, forward, preferred_element_type=F32)
    end = jnp.dot(end_rows, ends, preferred_element_type=F32)
    split = half * ROWS
    cross_real, cross_imag = cross_power(
        full[:split, :LANES], full[:split, LANES:], full[split:, :LANES], full[split:, LANES:]
    )
    cross = jnp.concatenate([cross_real, cross_imag], axis=1).astype(BF16)
    end_cross = []
    for s in (0, 2 * LANES):
        end_cross.append(
            jnp.concatenate(
                cross_power(
                    end[:half, s : s + LANES],
                    end[:half, s + LANES : s + 2 * LANES],
                    end[half:, s : s + LANES],
                    end[half:, s + LANES : s + 2 * LANES],
                ),
                axis=1,
            )
        )
    end_back = [
        jnp.dot(c.astype(BF16), back[:, :LANES], preferred_element_type=F32) for c in end_cross
    ]
    back_half = jnp.dot(cross, back, preferred_element_type=F32)
    is_end = lax.broadcasted_iota(jnp.int32, (8, LANES), 0) == 0

    def side(i):
        parts = []
        for part in range(2):
            block = back_half[ROWS * i : ROWS * (i + 1), lanes[part]]
            parts.append(jnp.where(is_end, end_back[part][i : i + 1], block[:8]))
            parts.append(block[8:])
        return jnp.concatenate(parts, axis=0)

    sides = jnp.concatenate([side(i) for i in range(half)], axis=1).astype(BF16)
    surface = jnp.dot(final, sides, preferred_element_type=F32)
    for i in range(half):
        part = surface[:, lanes[i]]
        power = part * part
        total = jnp.sum(power, axis=0, keepdims=True)
        moment = jnp.sum(power * rows, axis=0, keepdims=True)
        place = i % 5
        if i == 5 * (half // 5):
            r0[0, EXTRA : EXTRA + 1, :] = total
            r1[0, EXTRA : EXTRA + 1, :] = moment
        elif place < 4:
            row = at + 2 * (i // 5) + place // 2
            r0[place % 2, pl.ds(row, 1), :] = total
            r1[place % 2, pl.ds(row, 1), :] = moment
        else:
            for row in (at + 2 * (i // 5), at + 2 * (i // 5) + 1):
                r0[2, pl.ds(row, 1), :] = total
                r1[2, pl.ds(row, 1), :] = moment


def lane_sums(pick, table):
    return lax.dot_general(
        pick, table, (((1,), (1,)), ((), ())), precision=HIGHEST, preferred_element_type=F32
    )


def finish_terms(pick, r0, r1, counts, offsets, out):
    scale = 1.0 / float(PATCH * PATCH) ** 2
    even = lax.broadcasted_iota(jnp.int32, (1, LANES), 1) % 2 == 0
    plain = [lane_sums(pick, r0[s]) for s in range(3)]
    tilted = [lane_sums(pick, r1[s]) for s in range(3)]
    out[...] = jnp.zeros_like(out)
    for k in range(MOST):
        slot, side = k // 2, k % 2
        if k < 4:
            weight = plain[slot][side : side + 1]
            along = plain[slot][2 + side : 3 + side]
            deep = tilted[slot][side : side + 1]
        else:
            weight = jnp.where(even, plain[2][0:1], plain[2][1:2])
            along = jnp.where(even, plain[2][2:3], plain[2][3:4])
            deep = jnp.where(even, tilted[2][0:1], tilted[2][1:2])
        valid = counts > float(k) + 0.5
        weight = weight * scale
        inverse = scale / (weight + SMALL_WEIGHT)
        out[k : k + 1, :] = jnp.where(valid, weight, 0.0)
        out[8 + k : 9 + k, :] = jnp.where(valid, deep * inverse, 0.0)
        out[16 + k : 17 + k, :] = jnp.where(valid, along * inverse, 0.0)
    out[24:25, :] = offsets


def south_kernel(strips, nxt, info, anchor_t, depth, forward, ends, backs, final, pick, rows, out, first, second, r0, r1, sems, last_sem):
    tiles = first.shape[0]
    steps = tiles // GROUP
    side = pl.ds(0, SIDE)

    def first_copy(c):
        at = pl.ds(GROUP * c, GROUP)
        return pltpu.make_async_copy(strips.at[at, 2, :, side], first.at[at], sems.at[0, c])

    def second_copy(c, count=GROUP):
        below = strips.at[pl.ds(GROUP * c + 1, count), 1, :, side]
        return pltpu.make_async_copy(below, second.at[pl.ds(GROUP * c, count)], sems.at[1, c])

    last_copies = (
        second_copy(steps - 1, GROUP - 1),
        pltpu.make_async_copy(nxt.at[0], second.at[tiles - 1], last_sem),
    )
    for c in range(steps):
        first_copy(c).start()
        if c < steps - 1:
            second_copy(c).start()
        else:
            for copy in last_copies:
                copy.start()
    r0[...] = jnp.zeros_like(r0)
    r1[...] = jnp.zeros_like(r1)

    def step(c, carry):
        first_copy(c).wait()

        @pl.when(c < steps - 1)
        def _():
            second_copy(c).wait()

        @pl.when(c == steps - 1)
        def _():
            for copy in last_copies:
                copy.wait()

        columns = [
            block_pairs([ref[GROUP * c + j, :, :WIDE] for j in range(GROUP)]) for ref in (first, second)
        ]
        correlate_group(
            columns[0] + columns[1],
            depth[...], forward[...], ends[...], backs[0], final[...], rows[...], r0, r1, GROUP * c,
        )
        return carry

    lax.fori_loop(0, steps, step, 0)
    finish_terms(pick[...], r0, r1, info[2:3, :], info[3:4, :], out)
    out[25:26, :] = info[4:5, :]
    out[32:, :] = anchor_t[NODES - MESH_X : NODES, :]


def side_kernel(strips, from_east, from_west, info, depth, forward, ends, backs, final, pick, rows, out, own, other, own_extra, r0, r1, sems, extra_sems):
    steps = own.shape[0] // GROUP
    slots = GROUP // 2
    count = from_east.shape[0]
    side = pl.ds(0, SIDE)

    def own_copy(c, which):
        at = pl.ds(GROUP * c, GROUP)
        return pltpu.make_async_copy(strips.at[at, which, :, side], own.at[at], sems.at[0, c])

    def other_copy(c, source, start):
        return pltpu.make_async_copy(
            source.at[pl.ds(start, slots)], other.at[pl.ds(slots * c, slots)], sems.at[1, c]
        )

    extra_copies = (
        pltpu.make_async_copy(strips.at[0, 0, :, pl.ds(0, LANES)], own_extra, extra_sems.at[0]),
        pltpu.make_async_copy(from_west.at[count], other.at[2 * count], extra_sems.at[1]),
    )
    for c in range(steps):
        east = c < steps // 2
        own_copy(c, 3 if east else 0).start()
        other_copy(c, from_east if east else from_west, slots * (c % (steps // 2))).start()
        if c == 0:
            for copy in extra_copies:
                copy.start()
    r0[...] = jnp.zeros_like(r0)
    r1[...] = jnp.zeros_like(r1)
    for copy in extra_copies:
        copy.wait()

    def step(c, carry):
        own_copy(c, 0).wait()
        other_copy(c, from_east, 0).wait()
        owns = block_pairs([own[GROUP * c + j, :, :WIDE] for j in range(GROUP)])
        others = [
            other[slots * c + slot, :, LANES * i : LANES * (i + 1)] for slot in range(slots) for i in range(5)
        ]
        correlate_group(
            owns + [own_extra[...]] + others + [other[2 * count, :, :LANES]],
            depth[...], forward[...], ends[...], backs[c // (steps // 2)], final[...], rows[...], r0, r1, GROUP * c,
        )
        return carry

    lax.fori_loop(0, steps, step, 0)
    lane = lax.broadcasted_iota(jnp.int32, (8, LANES), 1)
    info_west = other[2 * count, 0:16, 2 * LANES : 3 * LANES].astype(F32)[0:8]
    table = jnp.where(lane < GROUP * (steps // 2), info[...], info_west)
    table = jnp.where(lane == EXTRA, pltpu.roll(info_west, EXTRA, axis=1), table)
    finish_terms(pick[...], r0, r1, table[0:1], table[1:2], out)


SUMS = [pltpu.VMEM((3, LANES, LANES), F32), pltpu.VMEM((3, LANES, LANES), F32)]
VMEM_BYTES = 48 * 1024 * 1024
ANY = pl.BlockSpec(memory_space=pl.ANY)
VMEM = pl.BlockSpec(memory_space=pltpu.VMEM)


def pair_call(kernel, name, tiles, rows, specs, buffers, semaphores):
    steps = tiles // GROUP
    return pl.pallas_call(
        kernel,
        name=name,
        in_specs=specs + [VMEM] * 7,
        out_specs=VMEM,
        out_shape=jax.ShapeDtypeStruct((rows, LANES), F32),
        scratch_shapes=buffers + SUMS + [pltpu.SemaphoreType.DMA((2, steps))] + semaphores,
        compiler_params=pltpu.CompilerParams(vmem_limit_bytes=VMEM_BYTES),
        cost_estimate=pl.CostEstimate(
            flops=tiles * MOST * 12_000_000,
            bytes_accessed=tiles * 2 * PATCH * SIDE * 2,
            transcendentals=0,
        ),
    )


def south_terms(strips, nxt, info, anchor_t, tabs):
    tiles = strips.shape[0]
    buffers = [pltpu.VMEM((tiles, PATCH, SIDE), BF16)] * 2
    return pair_call(
        south_kernel, "south_pairs", tiles, 64, [ANY, ANY, VMEM, VMEM], buffers, [pltpu.SemaphoreType.DMA]
    )(strips, nxt, info, anchor_t, *tabs)


def side_terms(strips, from_east, from_west, info, tabs):
    tiles = strips.shape[0]
    buffers = [
        pltpu.VMEM((tiles, PATCH, SIDE), BF16),
        pltpu.VMEM((tiles // 2 + 1, PATCH, 2 * WIDE), BF16),
        pltpu.VMEM((PATCH, LANES), BF16),
    ]
    return pair_call(
        side_kernel, "side_pairs", tiles, 32, [ANY, ANY, ANY, VMEM], buffers, [pltpu.SemaphoreType.DMA((2,))]
    )(strips, from_east, from_west, info, *tabs)


def edge_kernel(strips, north, sem):
    copy = pltpu.make_async_copy(strips.at[0, 1, :, pl.ds(0, SIDE)], north.at[0], sem)
    copy.start()
    copy.wait()


def prepare_kernel(strips, counts, offsets, stiffness, anchor, west, east, info, anchor_t, left, right, small, wide, sems):
    tiles = anchor.shape[0]
    half = tiles // 2
    moves = [
        (strips.at[pl.ds(half, half), 3, :, pl.ds(0, SIDE)], right),
        (strips.at[pl.ds(0, half), 0, :, pl.ds(0, SIDE)], left),
        (strips.at[0, 3, :, pl.ds(0, LANES)], east.at[half // 2, :, pl.ds(0, LANES)]),
    ]
    moves = [pltpu.make_async_copy(a, b, sems.at[k]) for k, (a, b) in enumerate(moves)]
    for move in moves:
        move.start()
    small[...] = jnp.zeros_like(small)
    here = pl.ds(0, tiles)
    small[0:1, here] = counts[0:1, :].astype(F32)
    small[1:2, here] = offsets[0:1, :].astype(F32)
    small[2:3, here] = counts[1:2, :].astype(F32)
    small[3:4, here] = offsets[1:2, :].astype(F32)
    small[4:5, here] = stiffness[...]
    info[...] = small[0:8, :]
    wide[...] = jnp.zeros_like(wide)
    for first in (0, COMP):
        wide[first : first + tiles, :] = anchor[:, 0, :]
    for i in range(NODES // LANES):
        anchor_t[LANES * i : LANES * (i + 1), :] = wide[:, LANES * i : LANES * (i + 1)].T
    east[half // 2, :, LANES:] = jnp.zeros((PATCH, 2 * WIDE - LANES), BF16)
    east[half // 2, 0:16, 2 * LANES : 3 * LANES] = small[...].astype(BF16)
    for move, source, packed in ((moves[0], right, east), (moves[1], left, west)):
        move.wait()
        for slot in range(half // 2):
            columns = block_pairs([source[2 * slot + j, :, :WIDE] for j in range(2)])
            for i, x in enumerate(columns):
                packed[slot, :, LANES * i : LANES * (i + 1)] = x
    moves[2].wait()


def prepare(strips, counts, offsets, stiffness, anchor):
    tiles = anchor.shape[0]
    vmem = pl.BlockSpec(memory_space=pltpu.VMEM)
    slots = tiles // 4
    return pl.pallas_call(
        prepare_kernel,
        name="prepare",
        in_specs=[pl.BlockSpec(memory_space=pl.ANY)] + [vmem] * 4,
        out_specs=[vmem] * 4,
        out_shape=[
            jax.ShapeDtypeStruct((slots, PATCH, 2 * WIDE), BF16),
            jax.ShapeDtypeStruct((slots + 1, PATCH, 2 * WIDE), BF16),
            jax.ShapeDtypeStruct((8, LANES), F32),
            jax.ShapeDtypeStruct((NODES, LANES), F32),
        ],
        scratch_shapes=[
            pltpu.VMEM((tiles // 2, PATCH, SIDE), BF16),
            pltpu.VMEM((tiles // 2, PATCH, SIDE), BF16),
            pltpu.VMEM((16, LANES), F32),
            pltpu.VMEM((LANES, NODES), F32),
            pltpu.SemaphoreType.DMA((3,)),
        ],
        compiler_params=pltpu.CompilerParams(vmem_limit_bytes=VMEM_BYTES),
    )(strips, counts, offsets, stiffness, anchor)


def whole(kernel, outs, name, scratch=()):
    vmem = pl.BlockSpec(memory_space=pltpu.VMEM)
    shapes = [jax.ShapeDtypeStruct(s, F32) for s in outs]

    def call(*args):
        return pl.pallas_call(
            kernel,
            name=name,
            in_specs=[vmem] * len(args),
            out_specs=[vmem] * len(outs),
            out_shape=shapes,
            scratch_shapes=list(scratch),
            compiler_params=pltpu.CompilerParams(vmem_limit_bytes=VMEM_BYTES),
            cost_estimate=pl.CostEstimate(
                flops=4_000_000, bytes_accessed=2_000_000, transcendentals=0
            ),
        )(*args)

    return call


def both(x):
    return x + pltpu.roll(x, COMP, axis=1)


def tents(offset, count):
    offset = both(offset)
    node = lax.broadcasted_iota(jnp.int32, (count, LANES), 0).astype(F32) * GAP + GAP / 2
    out = []
    for k in range(MOST):
        centre = offset + float(PATCH * k + PATCH // 2)
        out.append(jnp.maximum(0.0, 1.0 - jnp.abs(centre - node) / GAP))
    return out


def load_force(table):
    weight, x, y, shapes = table
    lane = lax.broadcasted_iota(jnp.int32, (1, LANES), 1)
    loads = weight * jnp.where(lane < COMP, x, pltpu.roll(y, COMP, axis=1))
    return sum(t * loads[k : k + 1] for k, t in enumerate(shapes))


def edge_force(table, difference):
    weight, _, _, shapes = table
    out = 0.0
    for k, t in enumerate(shapes):
        projected = jnp.sum(t * difference, axis=0, keepdims=True)
        out = out + t * (projected * weight[k : k + 1])
    return out


LEFT = pl.ds(0, MESH_X, stride=MESH_X)
RIGHT = pl.ds(MESH_X - 1, MESH_X, stride=MESH_X)
TOP = pl.ds(0, MESH_X)
BOTTOM = pl.ds(NODES - MESH_X, MESH_X)


def apply_inside(v, out, stiffness, anchor_t):
    column = lax.broadcasted_iota(jnp.int32, (MESH_X, LANES), 0)
    inner = jnp.where((column == 0) | (column == MESH_X - 1), 1.0, 2.0)
    for i in range(MESH_Y):
        here = v[MESH_X * i : MESH_X * (i + 1), :]
        beside = along_row(here, column)
        degree = inner
        if i > 0:
            beside += v[MESH_X * (i - 1) : MESH_X * i, :]
            degree = degree + 1.0
        if i < MESH_Y - 1:
            beside += v[MESH_X * (i + 1) : MESH_X * (i + 2), :]
            degree = degree + 1.0
        out[MESH_X * i : MESH_X * (i + 1), :] = (
            stiffness * (degree * here - beside) + anchor_t[MESH_X * i : MESH_X * (i + 1), :] * here
        )
    out[NODES:, :] = jnp.zeros((TALL - NODES, LANES), F32)


def along_row(x, node):
    before = jnp.where(node == 0, 0.0, pltpu.roll(x, 1, axis=0))
    return before + jnp.where(node == MESH_X - 1, 0.0, pltpu.roll(x, MESH_X - 1, axis=0))


def along_column(x, node):
    after = jnp.where(node >= MESH_Y - 1, 0.0, pltpu.roll(x, MESH_X - 1, axis=0))
    return after + jnp.where(node >= MESH_Y, 0.0, pltpu.roll(x, 1, axis=0))


def add_forces(out, east, west, south, north):
    out[RIGHT, :] += east
    out[LEFT, :] -= west
    out[BOTTOM, :] += south
    out[TOP, :] -= north


def inner_product(a, b):
    return jnp.sum(a[0:NODES, :] * b[0:NODES, :], axis=0, keepdims=True)


def message_kernel(tiles, terms_south, terms_side, from_north, info, anchor_t, to_west, to_east, to_north):
    lane = lax.broadcasted_iota(jnp.int32, (1, LANES), 1)
    side = terms_side[...]
    for out in (to_west, to_east, to_north):
        out[0:32, :] = side
        out[25:26, :] = info[4:5, :]
    south = terms_south[0:32, :]
    north = roll_tiles(south, 1, from_north[0:32, :], tiles)
    for q, terms in enumerate((south, north)):
        for k, row in enumerate((0, 8, 16, 24)):
            to_west[32 + 4 * q + k : 33 + 4 * q + k, :] = terms[row : row + 1]
    first = anchor_t[pl.ds(0, MESH_Y, stride=MESH_X), :]
    second = anchor_t[pl.ds(1, MESH_Y, stride=MESH_X), :]
    to_west[40 : 40 + MESH_Y, :] = jnp.where(lane < COMP, first, second)
    to_west[40 + MESH_Y :, :] = jnp.zeros((4, LANES), F32)
    to_east[32 : 32 + MESH_Y, :] = anchor_t[pl.ds(MESH_X - 1, MESH_Y, stride=MESH_X), :]
    to_east[32 + MESH_Y :, :] = jnp.zeros((4, LANES), F32)
    to_north[32:, :] = jnp.where(
        lane == 0, anchor_t[0:MESH_X, :], pltpu.roll(anchor_t[MESH_X : 2 * MESH_X, :], 1, axis=1)
    )


def roll_tiles(x, by, outside, tiles):
    lane = lax.broadcasted_iota(jnp.int32, (1, LANES), 1) % COMP
    if by == 1:
        edge, beyond = lane == 0, pltpu.roll(outside, LANES - (tiles - 1), axis=1)
    else:
        edge, beyond = lane == tiles - 1, pltpu.roll(outside, tiles - 1, axis=1)
    return jnp.where(edge, beyond, pltpu.roll(x, by % LANES, axis=1))


def pick_lane(x, source, target):
    lane = lax.broadcasted_iota(jnp.int32, (1, LANES), 1)
    return both(jnp.where(lane == target, pltpu.roll(x, (target - source) % LANES, axis=1), 0.0))


def near_tents(offset):
    return [
        jnp.maximum(0.0, 1.0 - jnp.abs(offset + (PATCH // 2 - GAP * n - GAP / 2)) / GAP) for n in (1, 2)
    ]


def near_pair(weight, x, y, offset):
    one, two = near_tents(offset)
    lane = lax.broadcasted_iota(jnp.int32, (1, LANES), 1)
    load = weight * jnp.where(lane < COMP, x, y)
    force = weight * one * (one * (2.0 * one * load) + two * (2.0 * two * load))
    return one * load, two * load, force


def mesh_kernel(tiles, *refs):
    terms_south, terms_side, from_east, from_west, from_south, from_north, info, anchor_t = refs[:8]
    v0, v1, v2, v3, match, gram, flip = refs[8:]
    lane = lax.broadcasted_iota(jnp.int32, (1, LANES), 1)
    node = lax.broadcasted_iota(jnp.int32, (MESH_X, LANES), 0)
    low, inside = lane < tiles // 2, lane < tiles
    side = terms_side[...]
    south_terms = terms_south[0:32, :]
    terms = [
        jnp.where(low, side, from_east[0:32, :]),
        jnp.where(low, from_west[0:32, :], side),
        south_terms,
        roll_tiles(south_terms, 1, from_north[0:32, :], tiles),
    ]
    tables_here = []
    for q, table in enumerate(terms):
        table = jnp.where(inside, table, 0.0)
        deep, along = table[8:16], table[16:24]
        x, y = (deep, along) if q < 2 else (along, deep)
        tables_here.append((both(table[0:8]), x, y, tents(table[24:25], MESH_X)))
    east, west, south, north = tables_here
    stiffness = both(info[4:5, :])

    flip[...] = jnp.zeros_like(flip)
    for q, (weight, x, y, _) in enumerate((east, south)):
        for s, rows in enumerate((jnp.where(lane < COMP, weight, 0.0), x, y)):
            flip[24 * q + 8 * s : 24 * q + 8 * s + 8, :] = rows
    match[...] = flip[...].T[0:tiles, 0:48]

    force_e, force_w, force_s, force_n = [load_force(t) for t in tables_here]
    v0[...] = jnp.zeros_like(v0)
    add_forces(v0, force_e, force_w, force_s, force_n)

    outside_east, outside_west = both(from_east[25:26, :]), both(from_west[25:26, :])
    packed = from_east[40:72, :]
    turned = pltpu.roll(packed, COMP, axis=1)
    anchor_e0 = jnp.where(lane < COMP, packed, turned)
    anchor_e1 = jnp.where(lane < COMP, turned, packed)
    anchor_w0 = from_west[32:64, :]
    last = tiles - 1
    outside_south = pick_lane(from_south[25:26, :], 0, last)
    anchor_s0 = pick_lane(from_south[32:64, :], 0, last)
    anchor_s1 = pick_lane(from_south[32:64, :], 1, last)
    outside_north = pick_lane(from_north[25:26, :], last, 0)
    anchor_n0 = pick_lane(from_north[32:64, :], last, 0)

    degree_c = jnp.where((node == 0) | (node == MESH_Y - 1), 2.0, 3.0)
    degree_r = jnp.where((node == 0) | (node == MESH_X - 1), 2.0, 3.0)

    near_s = near_pair(*[both(from_east[32 + k : 33 + k, :]) for k in (0, 2, 1, 3)])
    near_n = near_pair(*[both(from_east[36 + k : 37 + k, :]) for k in (0, 2, 1, 3)])
    at_ends = lambda a, b, x, y: jnp.where(node == a, x, 0.0) - jnp.where(node == b, y, 0.0)
    e0 = -force_e
    e1 = at_ends(MESH_Y - 1, 0, near_s[0], near_n[0])
    e2 = at_ends(MESH_Y - 1, 0, near_s[1], near_n[1])
    e1_pairs = at_ends(MESH_Y - 1, 0, near_s[2], near_n[2])
    w0 = force_w
    near_e = near_pair(*[pick_lane(from_south[k : k + 1, :], 0, last) for k in (0, 8, 16, 24)])
    near_w = near_pair(*[pick_lane(from_south[k : k + 1, :], EXTRA, last) for k in (0, 8, 16, 24)])
    s0 = -force_s
    s1 = at_ends(MESH_X - 1, 0, near_e[0], near_w[0])
    s2 = at_ends(MESH_X - 1, 0, near_e[1], near_w[1])
    s1_pairs = at_ends(MESH_X - 1, 0, near_e[2], near_w[2])
    n0 = force_n

    apply_inside(v0, v1, stiffness, anchor_t)
    pull_e = edge_force(east, v0[RIGHT, :] - e0)
    pull_w = edge_force(west, w0 - v0[LEFT, :])
    pull_s = edge_force(south, v0[BOTTOM, :] - s0)
    pull_n = edge_force(north, n0 - v0[TOP, :])
    add_forces(v1, pull_e, pull_w, pull_s, pull_n)
    e0, e1 = (
        outside_east * (degree_c * e0 - along_column(e0, node) - e1) + anchor_e0 * e0 - pull_e,
        outside_east * ((degree_c + 1.0) * e1 - along_column(e1, node) - e0 - e2) + anchor_e1 * e1 + e1_pairs,
    )
    w0, w1 = (
        outside_west * (degree_c * w0 - along_column(w0, node)) + anchor_w0 * w0 + pull_w,
        -outside_west * w0,
    )
    s0, s1 = (
        outside_south * (degree_r * s0 - along_row(s0, node) - s1) + anchor_s0 * s0 - pull_s,
        outside_south * ((degree_r + 1.0) * s1 - along_row(s1, node) - s0 - s2) + anchor_s1 * s1 + s1_pairs,
    )
    n0, n1 = (
        outside_north * (degree_r * n0 - along_row(n0, node)) + anchor_n0 * n0 + pull_n,
        -outside_north * n0,
    )

    def pulls(v, e0, w0, s0, n0):
        top, bottom = v[TOP, :], v[BOTTOM, :]
        spot = lane % COMP
        below = jnp.where(spot == last, s0, pltpu.roll(top, LANES - 1, axis=1))
        above = jnp.where(spot == 0, n0, pltpu.roll(bottom, 1, axis=1))
        return (
            edge_force(east, v[RIGHT, :] - e0),
            edge_force(west, w0 - v[LEFT, :]),
            edge_force(south, bottom - below),
            edge_force(north, above - top),
        )

    apply_inside(v1, v2, stiffness, anchor_t)
    pull_e, pull_w, pull_s, pull_n = pulls(v1, e0, w0, s0, n0)
    add_forces(v2, pull_e, pull_w, pull_s, pull_n)
    e0 = outside_east * (degree_c * e0 - along_column(e0, node) - e1) + anchor_e0 * e0 - pull_e
    w0 = outside_west * (degree_c * w0 - along_column(w0, node) - w1) + anchor_w0 * w0 + pull_w
    s0 = outside_south * (degree_r * s0 - along_row(s0, node) - s1) + anchor_s0 * s0 - pull_s
    n0 = outside_north * (degree_r * n0 - along_row(n0, node) - n1) + anchor_n0 * n0 + pull_n

    apply_inside(v2, v3, stiffness, anchor_t)
    add_forces(v3, *pulls(v2, e0, w0, s0, n0))

    gram[...] = jnp.zeros_like(gram)
    for k, (a, b) in enumerate(((v0, v0), (v0, v1), (v1, v1), (v1, v2), (v2, v2), (v2, v3))):
        gram[k : k + 1, :] = inner_product(a, b)


def final_kernel(tiles, gram, v0, v1, v2, v3, positions, residual):
    moments = jnp.sum(gram[...], axis=1, keepdims=True)
    mu = [moments[k : k + 1, :] for k in range(6)]
    zero, one = jnp.zeros_like(mu[0]), jnp.ones_like(mu[0])

    def form(a, b, shift):
        out = zero
        for i, x in enumerate(a):
            for j, y in enumerate(b):
                out = out + x * y * mu[i + j + shift]
        return out

    res, direction, pos = [one], [one], []
    norm_now = mu[0]
    for iteration in range(3):
        step = norm_now / form(direction, direction, 1)
        pos = [p + step * d for p, d in zip(pos + [zero] * (len(direction) - len(pos)), direction)]
        res = [
            r - step * d for r, d in zip(res + [zero], [zero] + direction)
        ]
        if iteration == 2:
            break
        norm_next = form(res, res, 0)
        ratio = norm_next / norm_now
        direction = [r + ratio * d for r, d in zip(res, direction + [zero])]
        norm_now = norm_next
    for out, coefficients in ((positions, pos), (residual, res)):
        for i in range(NODES // LANES):
            rows = slice(LANES * i, LANES * (i + 1))
            part = sum(c * v[rows, :] for c, v in zip(coefficients, (v0, v1, v2, v3)))
            part = part.T
            for c in range(2):
                out[:, c, rows] = part[COMP * c : COMP * c + tiles, :]


def shifted(x, axis, by):
    peers = lax.axis_size(axis)
    return lax.ppermute(x, axis, [(i, i + by) for i in range(peers) if 0 <= i + by < peers])


def add_over(x, axis, stride, radix):
    peers = lax.axis_size(axis)
    got = []
    for k in range(1, radix):
        pairs = []
        for i in range(peers):
            digit = i // stride % radix
            pairs.append((i, i + ((digit + k) % radix - digit) * stride))
        got.append(lax.ppermute(x, axis, pairs))
    for other in got:
        x = x + other
    return x


def sum_everywhere(x):
    for axis, order in (("row", (2, 4, 4)), ("col", (4,))):
        left, stride = lax.axis_size(axis), 1
        for radix in order:
            radix = math.gcd(radix, left)
            if radix > 1:
                x = add_over(x, axis, stride, radix)
                stride, left = stride * radix, left // radix
        if left > 1:
            x = add_over(x, axis, stride, left)
    return x


def per_device(strips, pair_counts, pair_offsets, tile_stiffness, anchor):
    tiles = strips.shape[0]
    own = strips[:, 0]
    field = (TALL, LANES)
    to_north = pl.pallas_call(
        edge_kernel,
        name="edge",
        in_specs=[ANY],
        out_specs=VMEM,
        out_shape=jax.ShapeDtypeStruct((1, PATCH, SIDE), BF16),
        scratch_shapes=[pltpu.SemaphoreType.DMA],
    )(own)
    next_top = shifted(to_north, "col", -1)
    to_west, to_east, info, anchor_t = prepare(
        own, pair_counts[:, 0].T, pair_offsets[:, 0].T, tile_stiffness.T, anchor
    )
    to_west, to_east, next_top = lax.optimization_barrier((to_west, to_east, next_top))
    strips_west = shifted(to_east, "row", 1)
    strips_east = shifted(to_west, "row", -1)
    tabs = tables()
    terms_south = south_terms(own, next_top, info, anchor_t, tabs)
    from_north = shifted(terms_south, "col", 1)
    terms_side = side_terms(own, strips_east, strips_west, info, tabs)
    to_west, to_east, to_north = whole(
        functools.partial(message_kernel, tiles),
        [(72, LANES), (64, LANES), (64, LANES)],
        "messages",
    )(terms_south, terms_side, from_north, info, anchor_t)
    from_east = shifted(to_west, "row", -1)
    from_west = shifted(to_east, "row", 1)
    from_south = shifted(to_north, "col", -1)
    v0, v1, v2, v3, match, gram = whole(
        functools.partial(mesh_kernel, tiles),
        [field, field, field, field, (tiles, 48), (8, LANES)],
        "powers",
        [pltpu.VMEM((LANES, LANES), F32)],
    )(terms_south, terms_side, from_east, from_west, from_south, from_north, info, anchor_t)
    gram = sum_everywhere(gram)
    positions, residual = whole(
        functools.partial(final_kernel, tiles),
        [(tiles, 2, NODES), (tiles, 2, NODES)],
        "combine",
    )(gram, v0, v1, v2, v3)
    return match.reshape(tiles, 1, 2, 3, 8), positions[:, None], residual[:, None]


def solution(mesh):
    return jax.shard_map(
        per_device,
        mesh=mesh,
        in_specs=(
            P("col", "row", None, None, None),
            P("col", "row", None),
            P("col", "row", None),
            P("col", "row"),
            P("col", "row", None),
        ),
        out_specs=(
            P("col", "row", None, None, None),
            P("col", "row", None, None),
            P("col", "row", None, None),
        ),
        check_vma=False,
    )
```

```python
import functools
import math

import jax
import jax.numpy as jnp
import numpy as np
from jax import lax
from jax.experimental import pallas as pl
from jax.experimental.pallas import tpu as pltpu
from jax.sharding import PartitionSpec as P

MESH_Y = 28
MESH_X = 32
NODES = MESH_Y * MESH_X
PATCH = 64
MOST = 5
WIDE = MOST * PATCH
SIDE = 384
ROWS = 32
EXTRA = 40
LANES = 128
COMP = 64
GROUP = 10
TALL = MESH_X * MESH_X
SMALL_WEIGHT = 1e-06
GAP = 16.0
F32 = jnp.float32
BF16 = jnp.bfloat16
HIGHEST = lax.Precision.HIGHEST


def tables():
    index = np.arange(PATCH)
    angle = (index[:, None] * index[None, :] % PATCH) * (2.0 * math.pi / PATCH)
    bf = jnp.bfloat16
    cos = np.cos(angle).astype(bf).astype(np.float32)
    sin = np.sin(angle).astype(bf).astype(np.float32)
    half = PATCH // 2
    depth = np.concatenate([cos[: half + 1], -sin[1:half]])
    pair = np.eye(2, dtype=np.float32)
    cos2, sin2 = np.kron(pair, cos), np.kron(pair, sin)
    forward = np.block([[cos2, -sin2], [sin2, cos2]])
    ends = np.kron(pair, np.concatenate([cos2, -sin2], axis=1))
    back = np.block([[cos2, sin2], [-sin2, cos2]])
    back_swapped = np.block([[cos2, sin2], [sin2, -cos2]])
    twice = np.full((PATCH,), 2.0, np.float32)
    twice[0] = twice[half] = 1.0
    final = np.concatenate([cos[:, : half + 1], -sin[:, 1:half]], axis=1) * twice
    offset = ((index + PATCH // 2) % PATCH - PATCH // 2).astype(np.float32)
    pick = np.zeros((8, LANES), np.float32)
    pick[0, :PATCH] = 1.0
    pick[1, PATCH:] = 1.0
    pick[2, :PATCH] = offset
    pick[3, PATCH:] = offset
    rows = np.repeat(offset[:, None], LANES, axis=1)
    as_bf = lambda a: jnp.asarray(a, BF16)
    backs = np.stack([back, back_swapped])
    return as_bf(depth), as_bf(forward), as_bf(ends), as_bf(backs), as_bf(final), jnp.asarray(pick), jnp.asarray(rows)


def block_pairs(strips):
    out = []
    for one, two in zip(strips[0::2], strips[1::2]):
        out += [
            one[:, 0:128],
            one[:, 128:256],
            two[:, 0:128],
            two[:, 128:256],
            jnp.concatenate([one[:, 256:320], two[:, 256:320]], axis=1),
        ]
    return out


def cross_power(first_real, first_imag, second_real, second_imag):
    denominator = (
        0.5
        * (
            first_real * first_real
            + first_imag * first_imag
            + second_real * second_real
            + second_imag * second_imag
        )
        + 1.0
    )
    inverse = 1.0 / denominator
    real = (first_real * second_real + first_imag * second_imag) * inverse
    imag = (first_imag * second_real - first_real * second_imag) * inverse
    return real, imag


def correlate_group(cols, depth, forward, ends, back, final, rows, r0, r1, at):
    count = len(cols)
    half = count // 2
    lanes = [slice(LANES * i, LANES * (i + 1)) for i in range(count)]
    spec = jnp.dot(depth, jnp.concatenate(cols, axis=1), preferred_element_type=F32)
    stacked = jnp.concatenate(
        [jnp.concatenate([spec[:ROWS, s], spec[ROWS:, s]], axis=1) for s in lanes], axis=0
    ).astype(BF16)
    end_rows = jnp.concatenate(
        [
            jnp.concatenate([spec[0:1, s] for s in lanes], axis=0),
            jnp.concatenate([spec[ROWS : ROWS + 1, s] for s in lanes], axis=0),
        ],
        axis=1,
    ).astype(BF16)
    full = jnp.dot(stacked, forward, preferred_element_type=F32)
    end = jnp.dot(end_rows, ends, preferred_element_type=F32)
    split = half * ROWS
    cross_real, cross_imag = cross_power(
        full[:split, :LANES], full[:split, LANES:], full[split:, :LANES], full[split:, LANES:]
    )
    cross = jnp.concatenate([cross_real, cross_imag], axis=1).astype(BF16)
    end_cross = []
    for s in (0, 2 * LANES):
        end_cross.append(
            jnp.concatenate(
                cross_power(
                    end[:half, s : s + LANES],
                    end[:half, s + LANES : s + 2 * LANES],
                    end[half:, s : s + LANES],
                    end[half:, s + LANES : s + 2 * LANES],
                ),
                axis=1,
            )
        )
    end_back = [
        jnp.dot(c.astype(BF16), back[:, :LANES], preferred_element_type=F32) for c in end_cross
    ]
    back_half = jnp.dot(cross, back, preferred_element_type=F32)
    is_end = lax.broadcasted_iota(jnp.int32, (8, LANES), 0) == 0

    def side(i):
        parts = []
        for part in range(2):
            block = back_half[ROWS * i : ROWS * (i + 1), lanes[part]]
            parts.append(jnp.where(is_end, end_back[part][i : i + 1], block[:8]))
            parts.append(block[8:])
        return jnp.concatenate(parts, axis=0)

    sides = jnp.concatenate([side(i) for i in range(half)], axis=1).astype(BF16)
    surface = jnp.dot(final, sides, preferred_element_type=F32)
    for i in range(half):
        part = surface[:, lanes[i]]
        power = part * part
        total = jnp.sum(power, axis=0, keepdims=True)
        moment = jnp.sum(power * rows, axis=0, keepdims=True)
        place = i % 5
        if i == 5 * (half // 5):
            r0[0, EXTRA : EXTRA + 1, :] = total
            r1[0, EXTRA : EXTRA + 1, :] = moment
        elif place < 4:
            row = at + 2 * (i // 5) + place // 2
            r0[place % 2, pl.ds(row, 1), :] = total
            r1[place % 2, pl.ds(row, 1), :] = moment
        else:
            for row in (at + 2 * (i // 5), at + 2 * (i // 5) + 1):
                r0[2, pl.ds(row, 1), :] = total
                r1[2, pl.ds(row, 1), :] = moment


def lane_sums(pick, table):
    return lax.dot_general(
        pick, table, (((1,), (1,)), ((), ())), precision=HIGHEST, preferred_element_type=F32
    )


def finish_terms(pick, r0, r1, counts, offsets, out):
    scale = 1.0 / float(PATCH * PATCH) ** 2
    even = lax.broadcasted_iota(jnp.int32, (1, LANES), 1) % 2 == 0
    plain = [lane_sums(pick, r0[s]) for s in range(3)]
    tilted = [lane_sums(pick, r1[s]) for s in range(3)]
    out[...] = jnp.zeros_like(out)
    for k in range(MOST):
        slot, side = k // 2, k % 2
        if k < 4:
            weight = plain[slot][side : side + 1]
            along = plain[slot][2 + side : 3 + side]
            deep = tilted[slot][side : side + 1]
        else:
            weight = jnp.where(even, plain[2][0:1], plain[2][1:2])
            along = jnp.where(even, plain[2][2:3], plain[2][3:4])
            deep = jnp.where(even, tilted[2][0:1], tilted[2][1:2])
        valid = counts > float(k) + 0.5
        weight = weight * scale
        inverse = scale / (weight + SMALL_WEIGHT)
        out[k : k + 1, :] = jnp.where(valid, weight, 0.0)
        out[8 + k : 9 + k, :] = jnp.where(valid, deep * inverse, 0.0)
        out[16 + k : 17 + k, :] = jnp.where(valid, along * inverse, 0.0)
    out[24:25, :] = offsets


def south_kernel(strips, nxt, info, anchor_t, depth, forward, ends, backs, final, pick, rows, out, first, second, r0, r1, sems, last_sem):
    tiles = first.shape[0]
    steps = tiles // GROUP
    side = pl.ds(0, SIDE)

    def first_copy(c):
        at = pl.ds(GROUP * c, GROUP)
        return pltpu.make_async_copy(strips.at[at, 2, :, side], first.at[at], sems.at[0, c])

    def second_copy(c, count=GROUP):
        below = strips.at[pl.ds(GROUP * c + 1, count), 1, :, side]
        return pltpu.make_async_copy(below, second.at[pl.ds(GROUP * c, count)], sems.at[1, c])

    last_copies = (
        second_copy(steps - 1, GROUP - 1),
        pltpu.make_async_copy(nxt.at[0], second.at[tiles - 1], last_sem),
    )
    for c in range(steps):
        first_copy(c).start()
        if c < steps - 1:
            second_copy(c).start()
        else:
            for copy in last_copies:
                copy.start()
    r0[...] = jnp.zeros_like(r0)
    r1[...] = jnp.zeros_like(r1)

    def step(c, carry):
        first_copy(c).wait()

        @pl.when(c < steps - 1)
        def _():
            second_copy(c).wait()

        @pl.when(c == steps - 1)
        def _():
            for copy in last_copies:
                copy.wait()

        columns = [
            block_pairs([ref[GROUP * c + j, :, :WIDE] for j in range(GROUP)]) for ref in (first, second)
        ]
        correlate_group(
            columns[0] + columns[1],
            depth[...], forward[...], ends[...], backs[0], final[...], rows[...], r0, r1, GROUP * c,
        )
        return carry

    lax.fori_loop(0, steps, step, 0)
    finish_terms(pick[...], r0, r1, info[2:3, :], info[3:4, :], out)
    out[25:26, :] = info[4:5, :]
    out[32:, :] = anchor_t[NODES - MESH_X : NODES, :]


def side_kernel(role, strips, received, info, depth, forward, ends, backs, final, pick, rows, out, own, other, own_extra, r0, r1, sems, extra_sems):
    half = own.shape[0]
    steps = half // GROUP
    slots = GROUP // 2
    spare = half // 2
    west = role[0]
    base = west * half

    def own_copy(c):
        source = strips.at[pl.ds(base + GROUP * c, GROUP), 3 - 3 * west, :, pl.ds(0, SIDE)]
        return pltpu.make_async_copy(source, own.at[pl.ds(GROUP * c, GROUP)], sems.at[0, c])

    def other_copy(c):
        at = pl.ds(slots * c, slots)
        return pltpu.make_async_copy(received.at[at], other.at[at], sems.at[1, c])

    extra_copies = (
        pltpu.make_async_copy(strips.at[0, 0, :, pl.ds(0, LANES)], own_extra, extra_sems.at[0]),
        pltpu.make_async_copy(received.at[spare], other.at[spare], extra_sems.at[1]),
    )
    for c in range(steps):
        own_copy(c).start()
        other_copy(c).start()
        if c == 0:
            for copy in extra_copies:
                copy.start()
    r0[...] = jnp.zeros_like(r0)
    r1[...] = jnp.zeros_like(r1)
    for copy in extra_copies:
        copy.wait()

    def step(c, carry):
        own_copy(c).wait()
        other_copy(c).wait()
        owns = block_pairs([own[GROUP * c + j, :, :WIDE] for j in range(GROUP)])
        others = [
            other[slots * c + slot, :, LANES * i : LANES * (i + 1)] for slot in range(slots) for i in range(5)
        ]
        correlate_group(
            owns + [own_extra[...]] + others + [other[spare, :, :LANES]],
            depth[...], forward[...], ends[...], backs[west], final[...], rows[...], r0, r1, base + GROUP * c,
        )
        return carry

    lax.fori_loop(0, steps, step, 0)
    lane = lax.broadcasted_iota(jnp.int32, (8, LANES), 1)
    info_west = other[spare, 0:16, 2 * LANES : 3 * LANES].astype(F32)[0:8]
    table = jnp.where(west == 1, info_west, info[0:8, :])
    mine = (lane >= base) & (lane < base + half)
    table = jnp.where(mine, table, 0.0)
    table = jnp.where((lane == EXTRA) & (west == 1), pltpu.roll(info_west, EXTRA, axis=1), table)
    finish_terms(pick[...], r0, r1, table[0:1], table[1:2], out)


SUMS = [pltpu.VMEM((3, LANES, LANES), F32), pltpu.VMEM((3, LANES, LANES), F32)]
VMEM_BYTES = 48 * 1024 * 1024
ANY = pl.BlockSpec(memory_space=pl.ANY)
VMEM = pl.BlockSpec(memory_space=pltpu.VMEM)
SMEM = pl.BlockSpec(memory_space=pltpu.SMEM)


def pair_call(kernel, name, tiles, rows, specs, buffers, semaphores):
    steps = tiles // GROUP
    return pl.pallas_call(
        kernel,
        name=name,
        in_specs=specs + [VMEM] * 7,
        out_specs=VMEM,
        out_shape=jax.ShapeDtypeStruct((rows, LANES), F32),
        scratch_shapes=buffers + SUMS + [pltpu.SemaphoreType.DMA((2, steps))] + semaphores,
        compiler_params=pltpu.CompilerParams(vmem_limit_bytes=VMEM_BYTES),
        cost_estimate=pl.CostEstimate(
            flops=tiles * MOST * 12_000_000,
            bytes_accessed=tiles * 2 * PATCH * SIDE * 2,
            transcendentals=0,
        ),
    )


def south_terms(strips, nxt, info, anchor_t, tabs):
    tiles = strips.shape[0]
    buffers = [pltpu.VMEM((tiles, PATCH, SIDE), BF16)] * 2
    return pair_call(
        south_kernel, "south_pairs", tiles, 64, [ANY, ANY, VMEM, VMEM], buffers, [pltpu.SemaphoreType.DMA]
    )(strips, nxt, info, anchor_t, *tabs)


def side_terms(name, role, strips, received, info, tabs):
    half = strips.shape[0] // 2
    buffers = [
        pltpu.VMEM((half, PATCH, SIDE), BF16),
        pltpu.VMEM((half // 2 + 1, PATCH, 2 * WIDE), BF16),
        pltpu.VMEM((PATCH, LANES), BF16),
    ]
    return pair_call(
        side_kernel, name, half, 32, [SMEM, ANY, ANY, VMEM], buffers, [pltpu.SemaphoreType.DMA((2,))]
    )(role, strips, received, info, *tabs)


def pack(role, strips, info, packed, buffer, sems):
    half = buffer.shape[0]
    east = 1 - role[0]
    moves = [
        pltpu.make_async_copy(
            strips.at[pl.ds(east * half, half), 3 * east, :, pl.ds(0, SIDE)], buffer, sems.at[0]
        ),
        pltpu.make_async_copy(
            strips.at[0, 3, :, pl.ds(0, LANES)], packed.at[half // 2, :, pl.ds(0, LANES)], sems.at[1]
        ),
    ]
    for move in moves:
        move.start()
    packed[half // 2, :, LANES:] = jnp.zeros((PATCH, 2 * WIDE - LANES), BF16)
    packed[half // 2, 0:16, 2 * LANES : 3 * LANES] = info.astype(BF16)
    yield
    moves[0].wait()
    for slot in range(half // 2):
        columns = block_pairs([buffer[2 * slot + j, :, :WIDE] for j in range(2)])
        for i, x in enumerate(columns):
            packed[slot, :, LANES * i : LANES * (i + 1)] = x
    moves[1].wait()


def pack_across_kernel(role, strips, counts, offsets, stiffness, packed, north, info, buffer, sems, edge_sem):
    tiles = counts.shape[1]
    edge = pltpu.make_async_copy(strips.at[0, 1, :, pl.ds(0, SIDE)], north.at[0], edge_sem)
    edge.start()
    here = pl.ds(0, tiles)
    info[...] = jnp.zeros_like(info)
    info[0:1, here] = counts[0:1, :].astype(F32)
    info[1:2, here] = offsets[0:1, :].astype(F32)
    info[2:3, here] = counts[1:2, :].astype(F32)
    info[3:4, here] = offsets[1:2, :].astype(F32)
    info[4:5, here] = stiffness[...]
    for _ in pack(role, strips, info[...], packed, buffer, sems):
        pass
    edge.wait()


def pack_within_kernel(role, strips, info, anchor, packed, anchor_t, buffer, sems, wide):
    tiles = anchor.shape[0]
    for _ in pack(role, strips, info[...], packed, buffer, sems):
        wide[...] = jnp.zeros_like(wide)
        for first in (0, COMP):
            wide[first : first + tiles, :] = anchor[:, 0, :]
        for i in range(NODES // LANES):
            anchor_t[LANES * i : LANES * (i + 1), :] = wide[:, LANES * i : LANES * (i + 1)].T


def pack_across(role, strips, counts, offsets, stiffness):
    tiles = strips.shape[0]
    return pl.pallas_call(
        pack_across_kernel,
        name="pack_across",
        in_specs=[SMEM, ANY] + [VMEM] * 3,
        out_specs=[VMEM] * 3,
        out_shape=[
            jax.ShapeDtypeStruct((tiles // 4 + 1, PATCH, 2 * WIDE), BF16),
            jax.ShapeDtypeStruct((1, PATCH, SIDE), BF16),
            jax.ShapeDtypeStruct((16, LANES), F32),
        ],
        scratch_shapes=[
            pltpu.VMEM((tiles // 2, PATCH, SIDE), BF16),
            pltpu.SemaphoreType.DMA((2,)),
            pltpu.SemaphoreType.DMA,
        ],
        compiler_params=pltpu.CompilerParams(vmem_limit_bytes=VMEM_BYTES),
    )(role, strips, counts, offsets, stiffness)


def pack_within(role, strips, info, anchor):
    tiles = strips.shape[0]
    return pl.pallas_call(
        pack_within_kernel,
        name="pack_within",
        in_specs=[SMEM, ANY, VMEM, VMEM],
        out_specs=[VMEM] * 2,
        out_shape=[
            jax.ShapeDtypeStruct((tiles // 4 + 1, PATCH, 2 * WIDE), BF16),
            jax.ShapeDtypeStruct((NODES, LANES), F32),
        ],
        scratch_shapes=[
            pltpu.VMEM((tiles // 2, PATCH, SIDE), BF16),
            pltpu.SemaphoreType.DMA((2,)),
            pltpu.VMEM((LANES, NODES), F32),
        ],
        compiler_params=pltpu.CompilerParams(vmem_limit_bytes=VMEM_BYTES),
    )(role, strips, info, anchor)


def whole(kernel, outs, name, scratch=(), with_role=True):
    shapes = [jax.ShapeDtypeStruct(s, F32) for s in outs]

    def call(*args):
        return pl.pallas_call(
            kernel,
            name=name,
            in_specs=[SMEM] + [VMEM] * (len(args) - 1) if with_role else [VMEM] * len(args),
            out_specs=[VMEM] * len(outs),
            out_shape=shapes,
            scratch_shapes=list(scratch),
            compiler_params=pltpu.CompilerParams(vmem_limit_bytes=VMEM_BYTES),
            cost_estimate=pl.CostEstimate(
                flops=4_000_000, bytes_accessed=2_000_000, transcendentals=0
            ),
        )(*args)

    return call


def both(x):
    return x + pltpu.roll(x, COMP, axis=1)


def tents(offset, count):
    offset = both(offset)
    node = lax.broadcasted_iota(jnp.int32, (count, LANES), 0).astype(F32) * GAP + GAP / 2
    out = []
    for k in range(MOST):
        centre = offset + float(PATCH * k + PATCH // 2)
        out.append(jnp.maximum(0.0, 1.0 - jnp.abs(centre - node) / GAP))
    return out


def load_force(table):
    weight, x, y, shapes = table
    lane = lax.broadcasted_iota(jnp.int32, (1, LANES), 1)
    loads = weight * jnp.where(lane < COMP, x, pltpu.roll(y, COMP, axis=1))
    return sum(t * loads[k : k + 1] for k, t in enumerate(shapes))


def edge_force(table, difference):
    weight, _, _, shapes = table
    out = 0.0
    for k, t in enumerate(shapes):
        projected = jnp.sum(t * difference, axis=0, keepdims=True)
        out = out + t * (projected * weight[k : k + 1])
    return out


LEFT = pl.ds(0, MESH_X, stride=MESH_X)
RIGHT = pl.ds(MESH_X - 1, MESH_X, stride=MESH_X)
TOP = pl.ds(0, MESH_X)
BOTTOM = pl.ds(NODES - MESH_X, MESH_X)


def apply_inside(v, out, stiffness, anchor_t):
    column = lax.broadcasted_iota(jnp.int32, (MESH_X, LANES), 0)
    inner = jnp.where((column == 0) | (column == MESH_X - 1), 1.0, 2.0)
    for i in range(MESH_Y):
        here = v[MESH_X * i : MESH_X * (i + 1), :]
        beside = along_row(here, column)
        degree = inner
        if i > 0:
            beside += v[MESH_X * (i - 1) : MESH_X * i, :]
            degree = degree + 1.0
        if i < MESH_Y - 1:
            beside += v[MESH_X * (i + 1) : MESH_X * (i + 2), :]
            degree = degree + 1.0
        out[MESH_X * i : MESH_X * (i + 1), :] = (
            stiffness * (degree * here - beside) + anchor_t[MESH_X * i : MESH_X * (i + 1), :] * here
        )
    out[NODES:, :] = jnp.zeros((TALL - NODES, LANES), F32)


def along_row(x, node):
    before = jnp.where(node == 0, 0.0, pltpu.roll(x, 1, axis=0))
    return before + jnp.where(node == MESH_X - 1, 0.0, pltpu.roll(x, MESH_X - 1, axis=0))


def along_column(x, node):
    after = jnp.where(node >= MESH_Y - 1, 0.0, pltpu.roll(x, MESH_X - 1, axis=0))
    return after + jnp.where(node >= MESH_Y, 0.0, pltpu.roll(x, 1, axis=0))


def add_forces(out, east, west, south, north):
    out[RIGHT, :] += east
    out[LEFT, :] -= west
    out[BOTTOM, :] += south
    out[TOP, :] -= north


def inner_product(a, b):
    return jnp.sum(a[0:NODES, :] * b[0:NODES, :], axis=0, keepdims=True)


def write_message(role, terms, terms_south, from_north, info, anchor_t, tiles, out):
    lane = lax.broadcasted_iota(jnp.int32, (1, LANES), 1)
    out[0:32, :] = terms[...]
    out[25:26, :] = info[4:5, :]
    south = terms_south[0:32, :]
    north = roll_tiles(south, 1, from_north[0:32, :], tiles)
    for q, table in enumerate((south, north)):
        for k, row in enumerate((0, 8, 16, 24)):
            out[32 + 4 * q + k : 33 + 4 * q + k, :] = table[row : row + 1]
    first, second, edge = [
        anchor_t[pl.ds(j, MESH_Y, stride=MESH_X), :] for j in (0, 1, MESH_X - 1)
    ]
    to_west = jnp.where(lane < COMP, first, second)
    out[40 : 40 + MESH_Y, :] = jnp.where(role[0] == 1, to_west, edge)
    out[40 + MESH_Y :, :] = jnp.zeros((MESH_X - MESH_Y, LANES), F32)


def message_kernel(tiles, role, terms, terms_south, from_north, info, anchor_t, out):
    write_message(role, terms, terms_south, from_north, info, anchor_t, tiles, out)


def last_message_kernel(tiles, role, terms, other_terms, terms_south, from_north, info, anchor_t, out, to_north):
    lane = lax.broadcasted_iota(jnp.int32, (1, LANES), 1)
    write_message(role, terms, terms_south, from_north, info, anchor_t, tiles, out)
    to_north[0:32, :] = terms[...] + other_terms[...]
    to_north[25:26, :] = info[4:5, :]
    to_north[32:, :] = jnp.where(
        lane == 0, anchor_t[0:MESH_X, :], pltpu.roll(anchor_t[MESH_X : 2 * MESH_X, :], 1, axis=1)
    )


def roll_tiles(x, by, outside, tiles):
    lane = lax.broadcasted_iota(jnp.int32, (1, LANES), 1) % COMP
    if by == 1:
        edge, beyond = lane == 0, pltpu.roll(outside, LANES - (tiles - 1), axis=1)
    else:
        edge, beyond = lane == tiles - 1, pltpu.roll(outside, tiles - 1, axis=1)
    return jnp.where(edge, beyond, pltpu.roll(x, by % LANES, axis=1))


def pick_lane(x, source, target):
    lane = lax.broadcasted_iota(jnp.int32, (1, LANES), 1)
    return both(jnp.where(lane == target, pltpu.roll(x, (target - source) % LANES, axis=1), 0.0))


def near_tents(offset):
    return [
        jnp.maximum(0.0, 1.0 - jnp.abs(offset + (PATCH // 2 - GAP * n - GAP / 2)) / GAP) for n in (1, 2)
    ]


def near_pair(weight, x, y, offset):
    one, two = near_tents(offset)
    lane = lax.broadcasted_iota(jnp.int32, (1, LANES), 1)
    load = weight * jnp.where(lane < COMP, x, y)
    force = weight * one * (one * (2.0 * one * load) + two * (2.0 * two * load))
    return one * load, two * load, force


def mesh_kernel(tiles, *refs):
    role, terms_south, terms_within, terms_across, within, across, from_south, from_north, info, anchor_t = refs[:10]
    v0, v1, v2, v3, match, gram, flip = refs[10:]
    within_is_east = role[0] == 0
    from_east = jnp.where(within_is_east, within[...], across[...])
    from_west = jnp.where(within_is_east, across[...], within[...])
    lane = lax.broadcasted_iota(jnp.int32, (1, LANES), 1)
    node = lax.broadcasted_iota(jnp.int32, (MESH_X, LANES), 0)
    low, inside = lane < tiles // 2, lane < tiles
    side = terms_within[...] + terms_across[...]
    south_terms = terms_south[0:32, :]
    terms = [
        jnp.where(low, side, from_east[0:32, :]),
        jnp.where(low, from_west[0:32, :], side),
        south_terms,
        roll_tiles(south_terms, 1, from_north[0:32, :], tiles),
    ]
    tables_here = []
    for q, table in enumerate(terms):
        table = jnp.where(inside, table, 0.0)
        deep, along = table[8:16], table[16:24]
        x, y = (deep, along) if q < 2 else (along, deep)
        tables_here.append((both(table[0:8]), x, y, tents(table[24:25], MESH_X)))
    east, west, south, north = tables_here
    stiffness = both(info[4:5, :])

    flip[...] = jnp.zeros_like(flip)
    for q, (weight, x, y, _) in enumerate((east, south)):
        for s, rows in enumerate((jnp.where(lane < COMP, weight, 0.0), x, y)):
            flip[24 * q + 8 * s : 24 * q + 8 * s + 8, :] = rows
    match[...] = flip[...].T[0:tiles, 0:48]

    force_e, force_w, force_s, force_n = [load_force(t) for t in tables_here]
    v0[...] = jnp.zeros_like(v0)
    add_forces(v0, force_e, force_w, force_s, force_n)

    outside_east, outside_west = both(from_east[25:26, :]), both(from_west[25:26, :])
    packed = from_east[40:72, :]
    turned = pltpu.roll(packed, COMP, axis=1)
    anchor_e0 = jnp.where(lane < COMP, packed, turned)
    anchor_e1 = jnp.where(lane < COMP, turned, packed)
    anchor_w0 = from_west[40:72, :]
    last = tiles - 1
    outside_south = pick_lane(from_south[25:26, :], 0, last)
    anchor_s0 = pick_lane(from_south[32:64, :], 0, last)
    anchor_s1 = pick_lane(from_south[32:64, :], 1, last)
    outside_north = pick_lane(from_north[25:26, :], last, 0)
    anchor_n0 = pick_lane(from_north[32:64, :], last, 0)

    degree_c = jnp.where((node == 0) | (node == MESH_Y - 1), 2.0, 3.0)
    degree_r = jnp.where((node == 0) | (node == MESH_X - 1), 2.0, 3.0)

    near_s = near_pair(*[both(from_east[32 + k : 33 + k, :]) for k in (0, 2, 1, 3)])
    near_n = near_pair(*[both(from_east[36 + k : 37 + k, :]) for k in (0, 2, 1, 3)])
    at_ends = lambda a, b, x, y: jnp.where(node == a, x, 0.0) - jnp.where(node == b, y, 0.0)
    e0 = -force_e
    e1 = at_ends(MESH_Y - 1, 0, near_s[0], near_n[0])
    e2 = at_ends(MESH_Y - 1, 0, near_s[1], near_n[1])
    e1_pairs = at_ends(MESH_Y - 1, 0, near_s[2], near_n[2])
    w0 = force_w
    near_e = near_pair(*[pick_lane(from_south[k : k + 1, :], 0, last) for k in (0, 8, 16, 24)])
    near_w = near_pair(*[pick_lane(from_south[k : k + 1, :], EXTRA, last) for k in (0, 8, 16, 24)])
    s0 = -force_s
    s1 = at_ends(MESH_X - 1, 0, near_e[0], near_w[0])
    s2 = at_ends(MESH_X - 1, 0, near_e[1], near_w[1])
    s1_pairs = at_ends(MESH_X - 1, 0, near_e[2], near_w[2])
    n0 = force_n

    apply_inside(v0, v1, stiffness, anchor_t)
    pull_e = edge_force(east, v0[RIGHT, :] - e0)
    pull_w = edge_force(west, w0 - v0[LEFT, :])
    pull_s = edge_force(south, v0[BOTTOM, :] - s0)
    pull_n = edge_force(north, n0 - v0[TOP, :])
    add_forces(v1, pull_e, pull_w, pull_s, pull_n)
    e0, e1 = (
        outside_east * (degree_c * e0 - along_column(e0, node) - e1) + anchor_e0 * e0 - pull_e,
        outside_east * ((degree_c + 1.0) * e1 - along_column(e1, node) - e0 - e2) + anchor_e1 * e1 + e1_pairs,
    )
    w0, w1 = (
        outside_west * (degree_c * w0 - along_column(w0, node)) + anchor_w0 * w0 + pull_w,
        -outside_west * w0,
    )
    s0, s1 = (
        outside_south * (degree_r * s0 - along_row(s0, node) - s1) + anchor_s0 * s0 - pull_s,
        outside_south * ((degree_r + 1.0) * s1 - along_row(s1, node) - s0 - s2) + anchor_s1 * s1 + s1_pairs,
    )
    n0, n1 = (
        outside_north * (degree_r * n0 - along_row(n0, node)) + anchor_n0 * n0 + pull_n,
        -outside_north * n0,
    )

    def pulls(v, e0, w0, s0, n0):
        top, bottom = v[TOP, :], v[BOTTOM, :]
        spot = lane % COMP
        below = jnp.where(spot == last, s0, pltpu.roll(top, LANES - 1, axis=1))
        above = jnp.where(spot == 0, n0, pltpu.roll(bottom, 1, axis=1))
        return (
            edge_force(east, v[RIGHT, :] - e0),
            edge_force(west, w0 - v[LEFT, :]),
            edge_force(south, bottom - below),
            edge_force(north, above - top),
        )

    apply_inside(v1, v2, stiffness, anchor_t)
    pull_e, pull_w, pull_s, pull_n = pulls(v1, e0, w0, s0, n0)
    add_forces(v2, pull_e, pull_w, pull_s, pull_n)
    e0 = outside_east * (degree_c * e0 - along_column(e0, node) - e1) + anchor_e0 * e0 - pull_e
    w0 = outside_west * (degree_c * w0 - along_column(w0, node) - w1) + anchor_w0 * w0 + pull_w
    s0 = outside_south * (degree_r * s0 - along_row(s0, node) - s1) + anchor_s0 * s0 - pull_s
    n0 = outside_north * (degree_r * n0 - along_row(n0, node) - n1) + anchor_n0 * n0 + pull_n

    apply_inside(v2, v3, stiffness, anchor_t)
    add_forces(v3, *pulls(v2, e0, w0, s0, n0))

    gram[...] = jnp.zeros_like(gram)
    for k, (a, b) in enumerate(((v0, v0), (v0, v1), (v1, v1), (v1, v2), (v2, v2), (v2, v3))):
        gram[k : k + 1, :] = inner_product(a, b)


def final_kernel(tiles, gram, v0, v1, v2, v3, positions, residual):
    moments = jnp.sum(gram[...], axis=1, keepdims=True)
    mu = [moments[k : k + 1, :] for k in range(6)]
    zero, one = jnp.zeros_like(mu[0]), jnp.ones_like(mu[0])

    def form(a, b, shift):
        out = zero
        for i, x in enumerate(a):
            for j, y in enumerate(b):
                out = out + x * y * mu[i + j + shift]
        return out

    res, direction, pos = [one], [one], []
    norm_now = mu[0]
    for iteration in range(3):
        step = norm_now / form(direction, direction, 1)
        pos = [p + step * d for p, d in zip(pos + [zero] * (len(direction) - len(pos)), direction)]
        res = [
            r - step * d for r, d in zip(res + [zero], [zero] + direction)
        ]
        if iteration == 2:
            break
        norm_next = form(res, res, 0)
        ratio = norm_next / norm_now
        direction = [r + ratio * d for r, d in zip(res, direction + [zero])]
        norm_now = norm_next
    for out, coefficients in ((positions, pos), (residual, res)):
        for i in range(NODES // LANES):
            rows = slice(LANES * i, LANES * (i + 1))
            part = sum(c * v[rows, :] for c, v in zip(coefficients, (v0, v1, v2, v3)))
            part = part.T
            for c in range(2):
                out[:, c, rows] = part[COMP * c : COMP * c + tiles, :]


def shifted(x, axis, by):
    peers = lax.axis_size(axis)
    return lax.ppermute(x, axis, [(i, i + by) for i in range(peers) if 0 <= i + by < peers])


def swapped(x, axis, first):
    peers = lax.axis_size(axis)
    pairs = [(i, i + 1) for i in range(first, peers - 1, 2)]
    return lax.ppermute(x, axis, pairs + [(b, a) for a, b in pairs])


def add_over(x, axis, stride, radix):
    peers = lax.axis_size(axis)
    got = []
    for k in range(1, radix):
        pairs = []
        for i in range(peers):
            digit = i // stride % radix
            pairs.append((i, i + ((digit + k) % radix - digit) * stride))
        got.append(lax.ppermute(x, axis, pairs))
    for other in got:
        x = x + other
    return x


def sum_everywhere(x):
    for axis, order in (("row", (2, 4, 4)), ("col", (4,))):
        left, stride = lax.axis_size(axis), 1
        for radix in order:
            radix = math.gcd(radix, left)
            if radix > 1:
                x = add_over(x, axis, stride, radix)
                stride, left = stride * radix, left // radix
        if left > 1:
            x = add_over(x, axis, stride, left)
    return x


def per_device(strips, pair_counts, pair_offsets, tile_stiffness, anchor):
    tiles = strips.shape[0]
    own = strips[:, 0]
    field = (TALL, LANES)
    within_role = (lax.axis_index("row") % 2).astype(jnp.int32).reshape(1)
    across_role = 1 - within_role
    packed_across, to_north, info = pack_across(
        across_role, own, pair_counts[:, 0].T, pair_offsets[:, 0].T, tile_stiffness.T
    )
    strips_across = swapped(packed_across, "row", 1)
    next_top = shifted(to_north, "col", -1)
    packed_within, anchor_t = pack_within(within_role, own, info, anchor)
    packed_within, next_top = lax.optimization_barrier((packed_within, next_top))
    strips_within = swapped(packed_within, "row", 0)
    tabs = tables()
    terms_south = south_terms(own, next_top, info, anchor_t, tabs)
    from_north = shifted(terms_south, "col", 1)
    terms_within = side_terms("within_pairs", within_role, own, strips_within, info, tabs)
    message = (72, LANES)
    (to_within,) = whole(functools.partial(message_kernel, tiles), [message], "message")(
        within_role, terms_within, terms_south, from_north, info, anchor_t
    )
    to_within, strips_across = lax.optimization_barrier((to_within, strips_across))
    within = swapped(to_within, "row", 0)
    terms_across = side_terms("across_pairs", across_role, own, strips_across, info, tabs)
    to_across, to_north = whole(
        functools.partial(last_message_kernel, tiles), [message, (64, LANES)], "last_message"
    )(across_role, terms_across, terms_within, terms_south, from_north, info, anchor_t)
    across = swapped(to_across, "row", 1)
    from_south = shifted(to_north, "col", -1)
    v0, v1, v2, v3, match, gram = whole(
        functools.partial(mesh_kernel, tiles),
        [field, field, field, field, (tiles, 48), (8, LANES)],
        "powers",
        [pltpu.VMEM((LANES, LANES), F32)],
    )(within_role, terms_south, terms_within, terms_across, within, across, from_south, from_north, info, anchor_t)
    gram = sum_everywhere(gram)
    positions, residual = whole(
        functools.partial(final_kernel, tiles),
        [(tiles, 2, NODES), (tiles, 2, NODES)],
        "combine",
        with_role=False,
    )(gram, v0, v1, v2, v3)
    return match.reshape(tiles, 1, 2, 3, 8), positions[:, None], residual[:, None]


def solution(mesh):
    return jax.shard_map(
        per_device,
        mesh=mesh,
        in_specs=(
            P("col", "row", None, None, None),
            P("col", "row", None),
            P("col", "row", None),
            P("col", "row"),
            P("col", "row", None),
        ),
        out_specs=(
            P("col", "row", None, None, None),
            P("col", "row", None, None),
            P("col", "row", None, None),
        ),
        check_vma=False,
    )
```

```python
import functools
import math

import jax
import jax.numpy as jnp
import numpy as np
from jax import lax
from jax.experimental import pallas as pl
from jax.experimental.pallas import tpu as pltpu
from jax.sharding import PartitionSpec as P

MESH_Y = 28
MESH_X = 32
NODES = MESH_Y * MESH_X
PATCH = 64
MOST = 5
WIDE = MOST * PATCH
SIDE = 384
ROWS = 32
EXTRA = 40
LANES = 128
COMP = 64
GROUP = 10
TALL = MESH_X * MESH_X
SMALL_WEIGHT = 1e-06
GAP = 16.0
F32 = jnp.float32
BF16 = jnp.bfloat16
HIGHEST = lax.Precision.HIGHEST


def tables():
    index = np.arange(PATCH)
    angle = (index[:, None] * index[None, :] % PATCH) * (2.0 * math.pi / PATCH)
    bf = jnp.bfloat16
    cos = np.cos(angle).astype(bf).astype(np.float32)
    sin = np.sin(angle).astype(bf).astype(np.float32)
    half = PATCH // 2
    depth = np.concatenate([cos[: half + 1], -sin[1:half]])
    pair = np.eye(2, dtype=np.float32)
    cos2, sin2 = np.kron(pair, cos), np.kron(pair, sin)
    forward = np.block([[cos2, -sin2], [sin2, cos2]])
    ends = np.kron(pair, np.concatenate([cos2, -sin2], axis=1))
    back = np.block([[cos2, sin2], [-sin2, cos2]])
    back_swapped = np.block([[cos2, sin2], [sin2, -cos2]])
    twice = np.full((PATCH,), 2.0, np.float32)
    twice[0] = twice[half] = 1.0
    final = np.concatenate([cos[:, : half + 1], -sin[:, 1:half]], axis=1) * twice
    offset = ((index + PATCH // 2) % PATCH - PATCH // 2).astype(np.float32)
    pick = np.zeros((8, LANES), np.float32)
    pick[0, :PATCH] = 1.0
    pick[1, PATCH:] = 1.0
    pick[2, :PATCH] = offset
    pick[3, PATCH:] = offset
    rows = np.repeat(offset[:, None], LANES, axis=1)
    as_bf = lambda a: jnp.asarray(a, BF16)
    backs = np.stack([back, back_swapped])
    return as_bf(depth), as_bf(forward), as_bf(ends), as_bf(backs), as_bf(final), jnp.asarray(pick), jnp.asarray(rows)


def block_pairs(strips):
    out = []
    for one, two in zip(strips[0::2], strips[1::2]):
        out += [
            one[:, 0:128],
            one[:, 128:256],
            two[:, 0:128],
            two[:, 128:256],
            jnp.concatenate([one[:, 256:320], two[:, 256:320]], axis=1),
        ]
    return out


def cross_power(first_real, first_imag, second_real, second_imag):
    denominator = (
        0.5
        * (
            first_real * first_real
            + first_imag * first_imag
            + second_real * second_real
            + second_imag * second_imag
        )
        + 1.0
    )
    inverse = 1.0 / denominator
    real = (first_real * second_real + first_imag * second_imag) * inverse
    imag = (first_imag * second_real - first_real * second_imag) * inverse
    return real, imag


def correlate_group(cols, depth, forward, ends, back, final, rows, r0, r1, at):
    count = len(cols)
    half = count // 2
    lanes = [slice(LANES * i, LANES * (i + 1)) for i in range(count)]
    spec = jnp.dot(depth, jnp.concatenate(cols, axis=1), preferred_element_type=F32)
    stacked = jnp.concatenate(
        [jnp.concatenate([spec[:ROWS, s], spec[ROWS:, s]], axis=1) for s in lanes], axis=0
    ).astype(BF16)
    end_rows = jnp.concatenate(
        [
            jnp.concatenate([spec[0:1, s] for s in lanes], axis=0),
            jnp.concatenate([spec[ROWS : ROWS + 1, s] for s in lanes], axis=0),
        ],
        axis=1,
    ).astype(BF16)
    full = jnp.dot(stacked, forward, preferred_element_type=F32)
    end = jnp.dot(end_rows, ends, preferred_element_type=F32)
    split = half * ROWS
    cross_real, cross_imag = cross_power(
        full[:split, :LANES], full[:split, LANES:], full[split:, :LANES], full[split:, LANES:]
    )
    cross = jnp.concatenate([cross_real, cross_imag], axis=1).astype(BF16)
    end_cross = []
    for s in (0, 2 * LANES):
        end_cross.append(
            jnp.concatenate(
                cross_power(
                    end[:half, s : s + LANES],
                    end[:half, s + LANES : s + 2 * LANES],
                    end[half:, s : s + LANES],
                    end[half:, s + LANES : s + 2 * LANES],
                ),
                axis=1,
            )
        )
    end_back = [
        jnp.dot(c.astype(BF16), back[:, :LANES], preferred_element_type=F32) for c in end_cross
    ]
    back_half = jnp.dot(cross, back, preferred_element_type=F32)
    is_end = lax.broadcasted_iota(jnp.int32, (8, LANES), 0) == 0

    def side(i):
        parts = []
        for part in range(2):
            block = back_half[ROWS * i : ROWS * (i + 1), lanes[part]]
            parts.append(jnp.where(is_end, end_back[part][i : i + 1], block[:8]))
            parts.append(block[8:])
        return jnp.concatenate(parts, axis=0)

    sides = jnp.concatenate([side(i) for i in range(half)], axis=1).astype(BF16)
    surface = jnp.dot(final, sides, preferred_element_type=F32)
    for i in range(half):
        part = surface[:, lanes[i]]
        power = part * part
        total = jnp.sum(power, axis=0, keepdims=True)
        moment = jnp.sum(power * rows, axis=0, keepdims=True)
        place = i % 5
        if i == 5 * (half // 5):
            r0[0, EXTRA : EXTRA + 1, :] = total
            r1[0, EXTRA : EXTRA + 1, :] = moment
        elif place < 4:
            row = at + 2 * (i // 5) + place // 2
            r0[place % 2, pl.ds(row, 1), :] = total
            r1[place % 2, pl.ds(row, 1), :] = moment
        else:
            for row in (at + 2 * (i // 5), at + 2 * (i // 5) + 1):
                r0[2, pl.ds(row, 1), :] = total
                r1[2, pl.ds(row, 1), :] = moment


def lane_sums(pick, table):
    return lax.dot_general(
        pick, table, (((1,), (1,)), ((), ())), precision=HIGHEST, preferred_element_type=F32
    )


def finish_terms(pick, r0, r1, counts, offsets, out):
    scale = 1.0 / float(PATCH * PATCH) ** 2
    even = lax.broadcasted_iota(jnp.int32, (1, LANES), 1) % 2 == 0
    plain = [lane_sums(pick, r0[s]) for s in range(3)]
    tilted = [lane_sums(pick, r1[s]) for s in range(3)]
    out[...] = jnp.zeros_like(out)
    for k in range(MOST):
        slot, side = k // 2, k % 2
        if k < 4:
            weight = plain[slot][side : side + 1]
            along = plain[slot][2 + side : 3 + side]
            deep = tilted[slot][side : side + 1]
        else:
            weight = jnp.where(even, plain[2][0:1], plain[2][1:2])
            along = jnp.where(even, plain[2][2:3], plain[2][3:4])
            deep = jnp.where(even, tilted[2][0:1], tilted[2][1:2])
        valid = counts > float(k) + 0.5
        weight = weight * scale
        inverse = scale / (weight + SMALL_WEIGHT)
        out[k : k + 1, :] = jnp.where(valid, weight, 0.0)
        out[8 + k : 9 + k, :] = jnp.where(valid, deep * inverse, 0.0)
        out[16 + k : 17 + k, :] = jnp.where(valid, along * inverse, 0.0)
    out[24:25, :] = offsets


def south_kernel(strips, nxt, info, anchor_t, depth, forward, ends, backs, final, pick, rows, out, first, second, r0, r1, sems, last_sem):
    tiles = first.shape[0]
    steps = tiles // GROUP
    side = pl.ds(0, SIDE)

    def first_copy(c):
        at = pl.ds(GROUP * c, GROUP)
        return pltpu.make_async_copy(strips.at[at, 2, :, side], first.at[at], sems.at[0, c])

    def second_copy(c, count=GROUP):
        below = strips.at[pl.ds(GROUP * c + 1, count), 1, :, side]
        return pltpu.make_async_copy(below, second.at[pl.ds(GROUP * c, count)], sems.at[1, c])

    last_copies = (
        second_copy(steps - 1, GROUP - 1),
        pltpu.make_async_copy(nxt.at[0, :, side], second.at[tiles - 1], last_sem),
    )
    for c in range(steps):
        first_copy(c).start()
        if c < steps - 1:
            second_copy(c).start()
        else:
            for copy in last_copies:
                copy.start()
    r0[...] = jnp.zeros_like(r0)
    r1[...] = jnp.zeros_like(r1)

    def step(c, carry):
        first_copy(c).wait()

        @pl.when(c < steps - 1)
        def _():
            second_copy(c).wait()

        @pl.when(c == steps - 1)
        def _():
            for copy in last_copies:
                copy.wait()

        columns = [
            block_pairs([ref[GROUP * c + j, :, :WIDE] for j in range(GROUP)]) for ref in (first, second)
        ]
        correlate_group(
            columns[0] + columns[1],
            depth[...], forward[...], ends[...], backs[0], final[...], rows[...], r0, r1, GROUP * c,
        )
        return carry

    lax.fori_loop(0, steps, step, 0)
    finish_terms(pick[...], r0, r1, info[2:3, :], info[3:4, :], out)
    out[25:26, :] = info[4:5, :]
    out[32:, :] = anchor_t[NODES - MESH_X : NODES, :]


def side_kernel(role, strips, received, next_top, info, depth, forward, ends, backs, final, pick, rows, out, own, other, r0, r1, sems, extra_sem):
    half = own.shape[0]
    steps = half // GROUP
    slots = GROUP // 2
    spare = half // 2
    west = role[0]
    base = west * half

    def own_copy(c):
        source = strips.at[pl.ds(base + GROUP * c, GROUP), 3 - 3 * west, :, pl.ds(0, SIDE)]
        return pltpu.make_async_copy(source, own.at[pl.ds(GROUP * c, GROUP)], sems.at[0, c])

    def other_copy(c):
        at = pl.ds(slots * c, slots)
        return pltpu.make_async_copy(received.at[at], other.at[at], sems.at[1, c])

    extra_copy = pltpu.make_async_copy(received.at[spare], other.at[spare], extra_sem)
    for c in range(steps):
        own_copy(c).start()
        other_copy(c).start()
        if c == 0:
            extra_copy.start()
    r0[...] = jnp.zeros_like(r0)
    r1[...] = jnp.zeros_like(r1)
    extra_copy.wait()

    def step(c, carry):
        own_copy(c).wait()
        other_copy(c).wait()
        owns = block_pairs([own[GROUP * c + j, :, :WIDE] for j in range(GROUP)])
        others = [
            other[slots * c + slot, :, LANES * i : LANES * (i + 1)] for slot in range(slots) for i in range(5)
        ]
        correlate_group(
            owns + [next_top[0, :, SIDE : SIDE + LANES]] + others + [other[spare, :, :LANES]],
            depth[...], forward[...], ends[...], backs[west], final[...], rows[...], r0, r1, base + GROUP * c,
        )
        return carry

    lax.fori_loop(0, steps, step, 0)
    lane = lax.broadcasted_iota(jnp.int32, (8, LANES), 1)
    info_west = other[spare, 0:16, 2 * LANES : 3 * LANES].astype(F32)[0:8]
    table = jnp.where(west == 1, info_west, info[0:8, :])
    mine = (lane >= base) & (lane < base + half) | (lane == EXTRA) & (west == 1)
    table = jnp.where(mine, table, 0.0)
    finish_terms(pick[...], r0, r1, table[0:1], table[1:2], out)


SUMS = [pltpu.VMEM((3, LANES, LANES), F32), pltpu.VMEM((3, LANES, LANES), F32)]
VMEM_BYTES = 48 * 1024 * 1024
ANY = pl.BlockSpec(memory_space=pl.ANY)
VMEM = pl.BlockSpec(memory_space=pltpu.VMEM)
SMEM = pl.BlockSpec(memory_space=pltpu.SMEM)


def pair_call(kernel, name, tiles, rows, specs, buffers, semaphores):
    steps = tiles // GROUP
    return pl.pallas_call(
        kernel,
        name=name,
        in_specs=specs + [VMEM] * 7,
        out_specs=VMEM,
        out_shape=jax.ShapeDtypeStruct((rows, LANES), F32),
        scratch_shapes=buffers + SUMS + [pltpu.SemaphoreType.DMA((2, steps))] + semaphores,
        compiler_params=pltpu.CompilerParams(vmem_limit_bytes=VMEM_BYTES),
        cost_estimate=pl.CostEstimate(
            flops=tiles * MOST * 12_000_000,
            bytes_accessed=tiles * 2 * PATCH * SIDE * 2,
            transcendentals=0,
        ),
    )


def south_terms(strips, nxt, info, anchor_t, tabs):
    tiles = strips.shape[0]
    buffers = [pltpu.VMEM((tiles, PATCH, SIDE), BF16)] * 2
    return pair_call(
        south_kernel, "south_pairs", tiles, 64, [ANY, ANY, VMEM, VMEM], buffers, [pltpu.SemaphoreType.DMA]
    )(strips, nxt, info, anchor_t, *tabs)


def side_terms(name, role, strips, received, next_top, info, tabs):
    half = strips.shape[0] // 2
    buffers = [
        pltpu.VMEM((half, PATCH, SIDE), BF16),
        pltpu.VMEM((half // 2 + 1, PATCH, 2 * WIDE), BF16),
    ]
    return pair_call(
        side_kernel, name, half, 32, [SMEM, ANY, ANY, VMEM, VMEM], buffers, [pltpu.SemaphoreType.DMA]
    )(role, strips, received, next_top, info, *tabs)


STATICS = COMP


def pieces(x):
    high = x.astype(BF16).astype(F32)
    middle = (x - high).astype(BF16).astype(F32)
    return high, middle, x - high - middle


def edge_kernel(strips, counts, offsets, stiffness, anchor, north, info, left, count_s, offset_s, stiff_s, anchor_s, turn, sems):
    tiles = counts.shape[1]
    lanes = pl.ds(0, LANES)
    copies = [
        (strips.at[0, 1, :, pl.ds(0, SIDE)], north.at[0, :, pl.ds(0, SIDE)]),
        (strips.at[0, 3, :, lanes], north.at[0, :, pl.ds(4 * LANES, LANES)]),
        (strips.at[0, 0, :, lanes], left),
        (counts, count_s),
        (offsets, offset_s),
        (stiffness, stiff_s),
        (anchor.at[0], anchor_s),
    ]
    copies = [pltpu.make_async_copy(a, b, sems.at[k]) for k, (a, b) in enumerate(copies)]
    for copy in copies:
        copy.start()
    turn[...] = jnp.zeros_like(turn)
    info[...] = jnp.zeros_like(info)
    for copy in copies:
        copy.wait()
    here = pl.ds(0, tiles)
    info[0:1, here] = count_s[0:1, :].astype(F32)
    info[1:2, here] = offset_s[0:1, :].astype(F32)
    info[2:3, here] = count_s[1:2, :].astype(F32)
    info[3:4, here] = offset_s[1:2, :].astype(F32)
    info[4:5, here] = stiff_s[...]
    turn[0:1, :] = anchor_s[0:1, lanes]
    columns = list(pieces(turn[...].T[0:PATCH, 0:1])) + list(pieces(info[4:5, 0:1]))
    columns += [info[0:1, 0:1], info[1:2, 0:1]]
    lane = lax.broadcasted_iota(jnp.int32, (PATCH, LANES), 1)
    block = jnp.where(lane < COMP, left[...].astype(F32), 0.0)
    for k, x in enumerate(columns):
        block = jnp.where(lane == STATICS + k, x, block)
    north[0, :, SIDE : SIDE + LANES] = block.astype(BF16)


def pack_kernel(role, strips, anchor, across, within, anchor_t, buffers, wide, sems):
    tiles = anchor.shape[0]
    half = tiles // 2
    moves = []
    for k, east in enumerate((role[0], 1 - role[0])):
        source = strips.at[pl.ds(east * half, half), 3 * east, :, pl.ds(0, SIDE)]
        moves.append(pltpu.make_async_copy(source, buffers.at[k], sems.at[k]))
        moves[k].start()
    wide[...] = jnp.zeros_like(wide)
    for first in (0, COMP):
        wide[first : first + tiles, :] = anchor[:, 0, :]
    for i in range(NODES // LANES):
        anchor_t[LANES * i : LANES * (i + 1), :] = wide[:, LANES * i : LANES * (i + 1)].T
    for k, packed in enumerate((across, within)):
        moves[k].wait()
        for slot in range(half // 2):
            columns = block_pairs([buffers[k, 2 * slot + j, :, :WIDE] for j in range(2)])
            for i, x in enumerate(columns):
                packed[slot, :, LANES * i : LANES * (i + 1)] = x
        packed[half // 2] = jnp.zeros((PATCH, 2 * WIDE), BF16)


def fill_kernel(next_top, info, across_in, within_in, across, within, slot, sems):
    spare = across.shape[0] - 1
    lane = lax.broadcasted_iota(jnp.int32, (16, LANES), 1)
    row = lax.broadcasted_iota(jnp.int32, (16, LANES), 0)
    statics = next_top[0, 0:16, SIDE : SIDE + LANES].astype(F32)
    count = pltpu.roll(statics, (EXTRA - STATICS - 6) % LANES, axis=1)
    offset = pltpu.roll(statics, (EXTRA - STATICS - 7) % LANES, axis=1)
    facts = jnp.where(lane == EXTRA, jnp.where(row == 0, count, offset), info[...])
    slot[...] = jnp.zeros_like(slot)
    slot[:, 0:LANES] = next_top[0, :, 4 * LANES :]
    slot[0:16, 2 * LANES : 3 * LANES] = facts.astype(BF16)
    copies = [
        pltpu.make_async_copy(slot, packed.at[spare, :, pl.ds(0, SIDE)], sems.at[k])
        for k, packed in enumerate((across, within))
    ]
    for copy in copies:
        copy.start()
    for copy in copies:
        copy.wait()


def edge(strips, counts, offsets, stiffness, anchor):
    tiles = strips.shape[0]
    dma = pltpu.SemaphoreType.DMA
    return pl.pallas_call(
        edge_kernel,
        name="edge",
        in_specs=[ANY] * 5,
        out_specs=[VMEM] * 2,
        out_shape=[
            jax.ShapeDtypeStruct((1, PATCH, 2 * WIDE), BF16),
            jax.ShapeDtypeStruct((16, LANES), F32),
        ],
        scratch_shapes=[
            pltpu.VMEM((PATCH, LANES), BF16),
            pltpu.VMEM((2, tiles), jnp.int32),
            pltpu.VMEM((2, tiles), jnp.int32),
            pltpu.VMEM((1, tiles), F32),
            pltpu.VMEM((1, NODES), F32),
            pltpu.VMEM((LANES, LANES), F32),
            dma((7,)),
        ],
    )(strips, counts, offsets, stiffness, anchor)


def pack(role, strips, anchor):
    tiles = strips.shape[0]
    packed = jax.ShapeDtypeStruct((tiles // 4 + 1, PATCH, 2 * WIDE), BF16)
    return pl.pallas_call(
        pack_kernel,
        name="pack",
        in_specs=[SMEM, ANY, VMEM],
        out_specs=[VMEM] * 3,
        out_shape=[packed, packed, jax.ShapeDtypeStruct((NODES, LANES), F32)],
        scratch_shapes=[
            pltpu.VMEM((2, tiles // 2, PATCH, SIDE), BF16),
            pltpu.VMEM((LANES, NODES), F32),
            pltpu.SemaphoreType.DMA((2,)),
        ],
        compiler_params=pltpu.CompilerParams(vmem_limit_bytes=VMEM_BYTES),
        cost_estimate=pl.CostEstimate(flops=0, bytes_accessed=6_000_000, transcendentals=0),
    )(role, strips, anchor)


def fill(next_top, info, across, within):
    packed = jax.ShapeDtypeStruct(across.shape, BF16)
    return pl.pallas_call(
        fill_kernel,
        name="fill",
        in_specs=[VMEM, VMEM, ANY, ANY],
        out_specs=[ANY, ANY],
        out_shape=[packed, packed],
        input_output_aliases={2: 0, 3: 1},
        scratch_shapes=[pltpu.VMEM((PATCH, SIDE), BF16), pltpu.SemaphoreType.DMA((2,))],
    )(next_top, info, across, within)


def whole(kernel, outs, name, scratch=(), with_role=True):
    shapes = [jax.ShapeDtypeStruct(s, F32) for s in outs]

    def call(*args):
        return pl.pallas_call(
            kernel,
            name=name,
            in_specs=[SMEM] + [VMEM] * (len(args) - 1) if with_role else [VMEM] * len(args),
            out_specs=[VMEM] * len(outs),
            out_shape=shapes,
            scratch_shapes=list(scratch),
            compiler_params=pltpu.CompilerParams(vmem_limit_bytes=VMEM_BYTES),
            cost_estimate=pl.CostEstimate(
                flops=4_000_000, bytes_accessed=2_000_000, transcendentals=0
            ),
        )(*args)

    return call


def both(x):
    return x + pltpu.roll(x, COMP, axis=1)


def tents(offset, count):
    offset = both(offset)
    node = lax.broadcasted_iota(jnp.int32, (count, LANES), 0).astype(F32) * GAP + GAP / 2
    out = []
    for k in range(MOST):
        centre = offset + float(PATCH * k + PATCH // 2)
        out.append(jnp.maximum(0.0, 1.0 - jnp.abs(centre - node) / GAP))
    return out


def load_force(table):
    weight, x, y, shapes = table
    lane = lax.broadcasted_iota(jnp.int32, (1, LANES), 1)
    loads = weight * jnp.where(lane < COMP, x, pltpu.roll(y, COMP, axis=1))
    return sum(t * loads[k : k + 1] for k, t in enumerate(shapes))


def edge_force(table, difference):
    weight, _, _, shapes = table
    out = 0.0
    for k, t in enumerate(shapes):
        projected = jnp.sum(t * difference, axis=0, keepdims=True)
        out = out + t * (projected * weight[k : k + 1])
    return out


LEFT = pl.ds(0, MESH_X, stride=MESH_X)
RIGHT = pl.ds(MESH_X - 1, MESH_X, stride=MESH_X)
TOP = pl.ds(0, MESH_X)
BOTTOM = pl.ds(NODES - MESH_X, MESH_X)


def apply_inside(v, out, stiffness, anchor_t):
    column = lax.broadcasted_iota(jnp.int32, (MESH_X, LANES), 0)
    inner = jnp.where((column == 0) | (column == MESH_X - 1), 1.0, 2.0)
    for i in range(MESH_Y):
        here = v[MESH_X * i : MESH_X * (i + 1), :]
        beside = along_row(here, column)
        degree = inner
        if i > 0:
            beside += v[MESH_X * (i - 1) : MESH_X * i, :]
            degree = degree + 1.0
        if i < MESH_Y - 1:
            beside += v[MESH_X * (i + 1) : MESH_X * (i + 2), :]
            degree = degree + 1.0
        out[MESH_X * i : MESH_X * (i + 1), :] = (
            stiffness * (degree * here - beside) + anchor_t[MESH_X * i : MESH_X * (i + 1), :] * here
        )
    out[NODES:, :] = jnp.zeros((TALL - NODES, LANES), F32)


def along_row(x, node):
    before = jnp.where(node == 0, 0.0, pltpu.roll(x, 1, axis=0))
    return before + jnp.where(node == MESH_X - 1, 0.0, pltpu.roll(x, MESH_X - 1, axis=0))


def along_column(x, node):
    after = jnp.where(node >= MESH_Y - 1, 0.0, pltpu.roll(x, MESH_X - 1, axis=0))
    return after + jnp.where(node >= MESH_Y, 0.0, pltpu.roll(x, 1, axis=0))


def add_forces(out, east, west, south, north):
    out[RIGHT, :] += east
    out[LEFT, :] -= west
    out[BOTTOM, :] += south
    out[TOP, :] -= north


def inner_product(a, b):
    return jnp.sum(a[0:NODES, :] * b[0:NODES, :], axis=0, keepdims=True)


def message_kernel(tiles, role, terms, terms_south, from_north, info, anchor_t, out):
    lane = lax.broadcasted_iota(jnp.int32, (1, LANES), 1)
    out[0:32, :] = terms[...]
    out[25:26, :] = info[4:5, :]
    north = roll_tiles(terms_south[0:32, :], 1, from_north[0:32, :], tiles)
    out[32:40, :] = jnp.zeros((8, LANES), F32)
    for k, row in enumerate((0, 8, 16, 24)):
        out[32 + k : 33 + k, :] = north[row : row + 1]
    first, second, last = [anchor_t[pl.ds(j, MESH_Y, stride=MESH_X), :] for j in (0, 1, MESH_X - 1)]
    to_west = jnp.where(lane < COMP, first, second)
    out[40 : 40 + MESH_Y, :] = jnp.where(role[0] == 1, to_west, last)
    out[40 + MESH_Y :, :] = jnp.zeros((MESH_X - MESH_Y, LANES), F32)


def roll_tiles(x, by, outside, tiles):
    lane = lax.broadcasted_iota(jnp.int32, (1, LANES), 1) % COMP
    if by == 1:
        edge, beyond = lane == 0, pltpu.roll(outside, LANES - (tiles - 1), axis=1)
    else:
        edge, beyond = lane == tiles - 1, pltpu.roll(outside, tiles - 1, axis=1)
    return jnp.where(edge, beyond, pltpu.roll(x, by % LANES, axis=1))


def pick_lane(x, source, target):
    lane = lax.broadcasted_iota(jnp.int32, (1, LANES), 1)
    return both(jnp.where(lane == target, pltpu.roll(x, (target - source) % LANES, axis=1), 0.0))


def near_tents(offset):
    return [
        jnp.maximum(0.0, 1.0 - jnp.abs(offset + (PATCH // 2 - GAP * n - GAP / 2)) / GAP) for n in (1, 2)
    ]


def near_pair(weight, x, y, offset):
    one, two = near_tents(offset)
    lane = lax.broadcasted_iota(jnp.int32, (1, LANES), 1)
    load = weight * jnp.where(lane < COMP, x, y)
    force = weight * one * (one * (2.0 * one * load) + two * (2.0 * two * load))
    return one * load, two * load, force


def mesh_kernel(tiles, *refs):
    role, terms_south, terms_within, terms_across, within, across, next_top, from_north, info, anchor_t = refs[:10]
    v0, v1, v2, v3, match, gram, flip = refs[10:]
    within_is_east = role[0] == 0
    from_east = jnp.where(within_is_east, within[...], across[...])
    from_west = jnp.where(within_is_east, across[...], within[...])
    lane = lax.broadcasted_iota(jnp.int32, (1, LANES), 1)
    node = lax.broadcasted_iota(jnp.int32, (MESH_X, LANES), 0)
    low, inside = lane < tiles // 2, lane < tiles
    side = terms_within[...] + terms_across[...]
    south_terms = terms_south[0:32, :]
    terms = [
        jnp.where(low, side, from_east[0:32, :]),
        jnp.where(low, from_west[0:32, :], side),
        south_terms,
        roll_tiles(south_terms, 1, from_north[0:32, :], tiles),
    ]
    tables_here = []
    for q, table in enumerate(terms):
        table = jnp.where(inside, table, 0.0)
        deep, along = table[8:16], table[16:24]
        x, y = (deep, along) if q < 2 else (along, deep)
        tables_here.append((both(table[0:8]), x, y, tents(table[24:25], MESH_X)))
    east, west, south, north = tables_here
    stiffness = both(info[4:5, :])

    flip[...] = jnp.zeros_like(flip)
    for q, (weight, x, y, _) in enumerate((east, south)):
        for s, rows in enumerate((jnp.where(lane < COMP, weight, 0.0), x, y)):
            flip[24 * q + 8 * s : 24 * q + 8 * s + 8, :] = rows
    match[...] = flip[...].T[0:tiles, 0:48]

    force_e, force_w, force_s, force_n = [load_force(t) for t in tables_here]
    v0[...] = jnp.zeros_like(v0)
    add_forces(v0, force_e, force_w, force_s, force_n)

    outside_east, outside_west = both(from_east[25:26, :]), both(from_west[25:26, :])
    packed = from_east[40:72, :]
    turned = pltpu.roll(packed, COMP, axis=1)
    anchor_e0 = jnp.where(lane < COMP, packed, turned)
    anchor_e1 = jnp.where(lane < COMP, turned, packed)
    anchor_w0 = from_west[40:72, :]
    last = tiles - 1
    statics = next_top[0, :, SIDE : SIDE + LANES].astype(F32)
    outside_south = sum(pick_lane(statics[0:1], STATICS + k, last) for k in (3, 4, 5))
    anchor_south = sum(pick_lane(statics, STATICS + k, last) for k in (0, 1, 2))
    anchor_s0, anchor_s1 = anchor_south[:MESH_X], anchor_south[MESH_X:]
    outside_north = pick_lane(from_north[25:26, :], last, 0)
    anchor_n0 = pick_lane(from_north[32:64, :], last, 0)

    degree_c = jnp.where((node == 0) | (node == MESH_Y - 1), 2.0, 3.0)
    degree_r = jnp.where((node == 0) | (node == MESH_X - 1), 2.0, 3.0)

    near_n = near_pair(*[both(from_east[32 + k : 33 + k, :]) for k in (0, 2, 1, 3)])
    e0 = -force_e
    e1, e2, e1_pairs = [-jnp.where(node == 0, x, 0.0) for x in near_n]
    w0 = force_w
    near_w = near_pair(*[pick_lane(side[k : k + 1, :], EXTRA, last) for k in (0, 8, 16, 24)])
    s0 = -force_s
    s1, s2, s1_pairs = [-jnp.where(node == 0, x, 0.0) for x in near_w]
    n0 = force_n

    apply_inside(v0, v1, stiffness, anchor_t)
    pull_e = edge_force(east, v0[RIGHT, :] - e0)
    pull_w = edge_force(west, w0 - v0[LEFT, :])
    pull_s = edge_force(south, v0[BOTTOM, :] - s0)
    pull_n = edge_force(north, n0 - v0[TOP, :])
    add_forces(v1, pull_e, pull_w, pull_s, pull_n)
    e0, e1 = (
        outside_east * (degree_c * e0 - along_column(e0, node) - e1) + anchor_e0 * e0 - pull_e,
        outside_east * ((degree_c + 1.0) * e1 - along_column(e1, node) - e0 - e2) + anchor_e1 * e1 + e1_pairs,
    )
    w0, w1 = (
        outside_west * (degree_c * w0 - along_column(w0, node)) + anchor_w0 * w0 + pull_w,
        -outside_west * w0,
    )
    s0, s1 = (
        outside_south * (degree_r * s0 - along_row(s0, node) - s1) + anchor_s0 * s0 - pull_s,
        outside_south * ((degree_r + 1.0) * s1 - along_row(s1, node) - s0 - s2) + anchor_s1 * s1 + s1_pairs,
    )
    n0, n1 = (
        outside_north * (degree_r * n0 - along_row(n0, node)) + anchor_n0 * n0 + pull_n,
        -outside_north * n0,
    )

    def pulls(v, e0, w0, s0, n0):
        top, bottom = v[TOP, :], v[BOTTOM, :]
        spot = lane % COMP
        below = jnp.where(spot == last, s0, pltpu.roll(top, LANES - 1, axis=1))
        above = jnp.where(spot == 0, n0, pltpu.roll(bottom, 1, axis=1))
        return (
            edge_force(east, v[RIGHT, :] - e0),
            edge_force(west, w0 - v[LEFT, :]),
            edge_force(south, bottom - below),
            edge_force(north, above - top),
        )

    apply_inside(v1, v2, stiffness, anchor_t)
    pull_e, pull_w, pull_s, pull_n = pulls(v1, e0, w0, s0, n0)
    add_forces(v2, pull_e, pull_w, pull_s, pull_n)
    e0 = outside_east * (degree_c * e0 - along_column(e0, node) - e1) + anchor_e0 * e0 - pull_e
    w0 = outside_west * (degree_c * w0 - along_column(w0, node) - w1) + anchor_w0 * w0 + pull_w
    s0 = outside_south * (degree_r * s0 - along_row(s0, node) - s1) + anchor_s0 * s0 - pull_s
    n0 = outside_north * (degree_r * n0 - along_row(n0, node) - n1) + anchor_n0 * n0 + pull_n

    apply_inside(v2, v3, stiffness, anchor_t)
    add_forces(v3, *pulls(v2, e0, w0, s0, n0))

    gram[...] = jnp.zeros_like(gram)
    for k, (a, b) in enumerate(((v0, v0), (v0, v1), (v1, v1), (v1, v2), (v2, v2), (v2, v3))):
        gram[k : k + 1, :] = inner_product(a, b)


def final_kernel(tiles, gram, v0, v1, v2, v3, positions, residual):
    moments = jnp.sum(gram[...], axis=1, keepdims=True)
    mu = [moments[k : k + 1, :] for k in range(6)]
    zero, one = jnp.zeros_like(mu[0]), jnp.ones_like(mu[0])

    def form(a, b, shift):
        out = zero
        for i, x in enumerate(a):
            for j, y in enumerate(b):
                out = out + x * y * mu[i + j + shift]
        return out

    res, direction, pos = [one], [one], []
    norm_now = mu[0]
    for iteration in range(3):
        step = norm_now / form(direction, direction, 1)
        pos = [p + step * d for p, d in zip(pos + [zero] * (len(direction) - len(pos)), direction)]
        res = [
            r - step * d for r, d in zip(res + [zero], [zero] + direction)
        ]
        if iteration == 2:
            break
        norm_next = form(res, res, 0)
        ratio = norm_next / norm_now
        direction = [r + ratio * d for r, d in zip(res, direction + [zero])]
        norm_now = norm_next
    for out, coefficients in ((positions, pos), (residual, res)):
        for i in range(NODES // LANES):
            rows = slice(LANES * i, LANES * (i + 1))
            part = sum(c * v[rows, :] for c, v in zip(coefficients, (v0, v1, v2, v3)))
            part = part.T
            for c in range(2):
                out[:, c, rows] = part[COMP * c : COMP * c + tiles, :]


def shifted(x, axis, by):
    peers = lax.axis_size(axis)
    return lax.ppermute(x, axis, [(i, i + by) for i in range(peers) if 0 <= i + by < peers])


def swapped(x, axis, first):
    peers = lax.axis_size(axis)
    pairs = [(i, i + 1) for i in range(first, peers - 1, 2)]
    return lax.ppermute(x, axis, pairs + [(b, a) for a, b in pairs])


def add_over(x, axis, stride, radix):
    peers = lax.axis_size(axis)
    got = [
        lax.ppermute(x, axis, [(i, i ^ (k * stride)) for i in range(peers)]) for k in range(1, radix)
    ]
    for other in got:
        x = x + other
    return x


def sum_everywhere(x):
    for axis, order in (("row", (2, 4, 4)), ("col", (4,))):
        left, stride = lax.axis_size(axis), 1
        for radix in order:
            radix = math.gcd(radix, left)
            if radix > 1:
                x = add_over(x, axis, stride, radix)
                stride, left = stride * radix, left // radix
        if left > 1:
            x = add_over(x, axis, stride, left)
    return x


def per_device(strips, pair_counts, pair_offsets, tile_stiffness, anchor):
    tiles = strips.shape[0]
    own = strips[:, 0]
    field = (TALL, LANES)
    within_role = (lax.axis_index("row") % 2).astype(jnp.int32).reshape(1)
    across_role = 1 - within_role
    to_north, info = edge(
        own, pair_counts[:, 0].T, pair_offsets[:, 0].T, tile_stiffness.T, anchor
    )
    next_top = shifted(to_north, "col", -1)
    packed_across, packed_within, anchor_t = pack(within_role, own, anchor)
    packed_across, packed_within = fill(next_top, info, packed_across, packed_within)
    strips_across = swapped(packed_across, "row", 1)
    strips_within = swapped(packed_within, "row", 0)
    tabs = tables()
    terms_south = south_terms(own, next_top, info, anchor_t, tabs)
    from_north = shifted(terms_south, "col", 1)
    message = whole(functools.partial(message_kernel, tiles), [(72, LANES)], "message")
    terms_within = side_terms("within_pairs", within_role, own, strips_within, next_top, info, tabs)
    (to_within,) = message(within_role, terms_within, terms_south, from_north, info, anchor_t)
    to_within, strips_across = lax.optimization_barrier((to_within, strips_across))
    within = swapped(to_within, "row", 0)
    terms_across = side_terms("across_pairs", across_role, own, strips_across, next_top, info, tabs)
    terms_across, within = lax.optimization_barrier((terms_across, within))
    (to_across,) = message(across_role, terms_across, terms_south, from_north, info, anchor_t)
    across = swapped(to_across, "row", 1)
    v0, v1, v2, v3, match, gram = whole(
        functools.partial(mesh_kernel, tiles),
        [field, field, field, field, (tiles, 48), (8, LANES)],
        "powers",
        [pltpu.VMEM((LANES, LANES), F32)],
    )(within_role, terms_south, terms_within, terms_across, within, across, next_top, from_north, info, anchor_t)
    gram = sum_everywhere(gram)
    positions, residual = whole(
        functools.partial(final_kernel, tiles),
        [(tiles, 2, NODES), (tiles, 2, NODES)],
        "combine",
        with_role=False,
    )(gram, v0, v1, v2, v3)
    return match.reshape(tiles, 1, 2, 3, 8), positions[:, None], residual[:, None]


def solution(mesh):
    return jax.shard_map(
        per_device,
        mesh=mesh,
        in_specs=(
            P("col", "row", None, None, None),
            P("col", "row", None),
            P("col", "row", None),
            P("col", "row"),
            P("col", "row", None),
        ),
        out_specs=(
            P("col", "row", None, None, None),
            P("col", "row", None, None),
            P("col", "row", None, None),
        ),
        check_vma=False,
    )
```

```python
import functools
import math

import jax
import jax.numpy as jnp
import numpy as np
from jax import lax
from jax.experimental import pallas as pl
from jax.experimental.pallas import tpu as pltpu
from jax.sharding import PartitionSpec as P

MESH_Y = 28
MESH_X = 32
NODES = MESH_Y * MESH_X
PATCH = 64
MOST = 5
WIDE = MOST * PATCH
SIDE = 384
ROWS = 32
EXTRA = 40
LANES = 128
COMP = 64
GROUP = 10
TALL = MESH_X * MESH_X
SMALL_WEIGHT = 1e-06
GAP = 16.0
F32 = jnp.float32
BF16 = jnp.bfloat16
HIGHEST = lax.Precision.HIGHEST


def tables():
    index = np.arange(PATCH)
    angle = (index[:, None] * index[None, :] % PATCH) * (2.0 * math.pi / PATCH)
    bf = jnp.bfloat16
    cos = np.cos(angle).astype(bf).astype(np.float32)
    sin = np.sin(angle).astype(bf).astype(np.float32)
    half = PATCH // 2
    depth = np.concatenate([cos[: half + 1], -sin[1:half]])
    pair = np.eye(2, dtype=np.float32)
    cos2, sin2 = np.kron(pair, cos), np.kron(pair, sin)
    forward = np.block([[cos2, -sin2], [sin2, cos2]])
    ends = np.kron(pair, np.concatenate([cos2, -sin2], axis=1))
    back = np.block([[cos2, sin2], [-sin2, cos2]])
    back_swapped = np.block([[cos2, sin2], [sin2, -cos2]])
    twice = np.full((PATCH,), 2.0, np.float32)
    twice[0] = twice[half] = 1.0
    final = np.concatenate([cos[:, : half + 1], -sin[:, 1:half]], axis=1) * twice
    offset = ((index + PATCH // 2) % PATCH - PATCH // 2).astype(np.float32)
    pick = np.zeros((8, LANES), np.float32)
    pick[0, :PATCH] = 1.0
    pick[1, PATCH:] = 1.0
    pick[2, :PATCH] = offset
    pick[3, PATCH:] = offset
    rows = np.repeat(offset[:, None], LANES, axis=1)
    as_bf = lambda a: jnp.asarray(a, BF16)
    backs = np.stack([back, back_swapped])
    return as_bf(depth), as_bf(forward), as_bf(ends), as_bf(backs), as_bf(final), jnp.asarray(pick), jnp.asarray(rows)


def block_pairs(strips):
    out = []
    for one, two in zip(strips[0::2], strips[1::2]):
        out += [
            one[:, 0:128],
            one[:, 128:256],
            two[:, 0:128],
            two[:, 128:256],
            jnp.concatenate([one[:, 256:320], two[:, 256:320]], axis=1),
        ]
    return out


def cross_power(first_real, first_imag, second_real, second_imag):
    denominator = (
        0.5
        * (
            first_real * first_real
            + first_imag * first_imag
            + second_real * second_real
            + second_imag * second_imag
        )
        + 1.0
    )
    inverse = 1.0 / denominator
    real = (first_real * second_real + first_imag * second_imag) * inverse
    imag = (first_imag * second_real - first_real * second_imag) * inverse
    return real, imag


def correlate_group(cols, depth, forward, ends, back, final, rows, r0, r1, at):
    count = len(cols)
    half = count // 2
    lanes = [slice(LANES * i, LANES * (i + 1)) for i in range(count)]
    spec = jnp.dot(depth, jnp.concatenate(cols, axis=1), preferred_element_type=F32)
    stacked = jnp.concatenate(
        [jnp.concatenate([spec[:ROWS, s], spec[ROWS:, s]], axis=1) for s in lanes], axis=0
    ).astype(BF16)
    end_rows = jnp.concatenate(
        [
            jnp.concatenate([spec[0:1, s] for s in lanes], axis=0),
            jnp.concatenate([spec[ROWS : ROWS + 1, s] for s in lanes], axis=0),
        ],
        axis=1,
    ).astype(BF16)
    full = jnp.dot(stacked, forward, preferred_element_type=F32)
    end = jnp.dot(end_rows, ends, preferred_element_type=F32)
    split = half * ROWS
    cross_real, cross_imag = cross_power(
        full[:split, :LANES], full[:split, LANES:], full[split:, :LANES], full[split:, LANES:]
    )
    cross = jnp.concatenate([cross_real, cross_imag], axis=1).astype(BF16)
    end_cross = []
    for s in (0, 2 * LANES):
        end_cross.append(
            jnp.concatenate(
                cross_power(
                    end[:half, s : s + LANES],
                    end[:half, s + LANES : s + 2 * LANES],
                    end[half:, s : s + LANES],
                    end[half:, s + LANES : s + 2 * LANES],
                ),
                axis=1,
            )
        )
    end_back = [
        jnp.dot(c.astype(BF16), back[:, :LANES], preferred_element_type=F32) for c in end_cross
    ]
    back_half = jnp.dot(cross, back, preferred_element_type=F32)
    is_end = lax.broadcasted_iota(jnp.int32, (8, LANES), 0) == 0

    def side(i):
        parts = []
        for part in range(2):
            block = back_half[ROWS * i : ROWS * (i + 1), lanes[part]]
            parts.append(jnp.where(is_end, end_back[part][i : i + 1], block[:8]))
            parts.append(block[8:])
        return jnp.concatenate(parts, axis=0)

    sides = jnp.concatenate([side(i) for i in range(half)], axis=1).astype(BF16)
    surface = jnp.dot(final, sides, preferred_element_type=F32)
    for i in range(half):
        part = surface[:, lanes[i]]
        power = part * part
        total = jnp.sum(power, axis=0, keepdims=True)
        moment = jnp.sum(power * rows, axis=0, keepdims=True)
        place = i % 5
        if i == 5 * (half // 5):
            r0[0, EXTRA : EXTRA + 1, :] = total
            r1[0, EXTRA : EXTRA + 1, :] = moment
        elif place < 4:
            row = at + 2 * (i // 5) + place // 2
            r0[place % 2, pl.ds(row, 1), :] = total
            r1[place % 2, pl.ds(row, 1), :] = moment
        else:
            for row in (at + 2 * (i // 5), at + 2 * (i // 5) + 1):
                r0[2, pl.ds(row, 1), :] = total
                r1[2, pl.ds(row, 1), :] = moment


def lane_sums(pick, table):
    return lax.dot_general(
        pick, table, (((1,), (1,)), ((), ())), precision=HIGHEST, preferred_element_type=F32
    )


def finish_terms(pick, r0, r1, counts, offsets, out):
    scale = 1.0 / float(PATCH * PATCH) ** 2
    even = lax.broadcasted_iota(jnp.int32, (1, LANES), 1) % 2 == 0
    plain = [lane_sums(pick, r0[s]) for s in range(3)]
    tilted = [lane_sums(pick, r1[s]) for s in range(3)]
    out[...] = jnp.zeros_like(out)
    for k in range(MOST):
        slot, side = k // 2, k % 2
        if k < 4:
            weight = plain[slot][side : side + 1]
            along = plain[slot][2 + side : 3 + side]
            deep = tilted[slot][side : side + 1]
        else:
            weight = jnp.where(even, plain[2][0:1], plain[2][1:2])
            along = jnp.where(even, plain[2][2:3], plain[2][3:4])
            deep = jnp.where(even, tilted[2][0:1], tilted[2][1:2])
        valid = counts > float(k) + 0.5
        weight = weight * scale
        inverse = scale / (weight + SMALL_WEIGHT)
        out[k : k + 1, :] = jnp.where(valid, weight, 0.0)
        out[8 + k : 9 + k, :] = jnp.where(valid, deep * inverse, 0.0)
        out[16 + k : 17 + k, :] = jnp.where(valid, along * inverse, 0.0)
    out[24:25, :] = offsets


def south_kernel(strips, nxt, info, anchor_t, depth, forward, ends, backs, final, pick, rows, out, first, second, r0, r1, sems, last_sem):
    tiles = first.shape[0]
    steps = tiles // GROUP
    side = pl.ds(0, SIDE)

    def first_copy(c):
        at = pl.ds(GROUP * c, GROUP)
        return pltpu.make_async_copy(strips.at[at, 2, :, side], first.at[at], sems.at[0, c])

    def second_copy(c, count=GROUP):
        below = strips.at[pl.ds(GROUP * c + 1, count), 1, :, side]
        return pltpu.make_async_copy(below, second.at[pl.ds(GROUP * c, count)], sems.at[1, c])

    last_copies = (
        second_copy(steps - 1, GROUP - 1),
        pltpu.make_async_copy(nxt.at[0, :, side], second.at[tiles - 1], last_sem),
    )
    for c in range(steps):
        first_copy(c).start()
        if c < steps - 1:
            second_copy(c).start()
        else:
            for copy in last_copies:
                copy.start()
    r0[...] = jnp.zeros_like(r0)
    r1[...] = jnp.zeros_like(r1)

    def step(c, carry):
        first_copy(c).wait()

        @pl.when(c < steps - 1)
        def _():
            second_copy(c).wait()

        @pl.when(c == steps - 1)
        def _():
            for copy in last_copies:
                copy.wait()

        columns = [
            block_pairs([ref[GROUP * c + j, :, :WIDE] for j in range(GROUP)]) for ref in (first, second)
        ]
        correlate_group(
            columns[0] + columns[1],
            depth[...], forward[...], ends[...], backs[0], final[...], rows[...], r0, r1, GROUP * c,
        )
        return carry

    lax.fori_loop(0, steps, step, 0)
    finish_terms(pick[...], r0, r1, info[2:3, :], info[3:4, :], out)
    out[25:26, :] = info[4:5, :]
    out[32:, :] = anchor_t[NODES - MESH_X : NODES, :]


def side_kernel(role, strips, received, next_top, corner, info, depth, forward, ends, backs, final, pick, rows, out, own, other, r0, r1, sems, extra_sem):
    half = own.shape[0]
    steps = half // GROUP
    slots = GROUP // 2
    spare = half // 2
    west = role[0]
    base = west * half

    def own_copy(c):
        source = strips.at[pl.ds(base + GROUP * c, GROUP), 3 - 3 * west, :, pl.ds(0, SIDE)]
        return pltpu.make_async_copy(source, own.at[pl.ds(GROUP * c, GROUP)], sems.at[0, c])

    def other_copy(c):
        at = pl.ds(slots * c, slots)
        return pltpu.make_async_copy(received.at[at], other.at[at], sems.at[1, c])

    extra_copy = pltpu.make_async_copy(received.at[spare], other.at[spare], extra_sem)
    for c in range(steps):
        own_copy(c).start()
        other_copy(c).start()
        if c == 0:
            extra_copy.start()
    r0[...] = jnp.zeros_like(r0)
    r1[...] = jnp.zeros_like(r1)
    extra_copy.wait()

    def step(c, carry):
        own_copy(c).wait()
        other_copy(c).wait()
        owns = block_pairs([own[GROUP * c + j, :, :WIDE] for j in range(GROUP)])
        others = [
            other[slots * c + slot, :, LANES * i : LANES * (i + 1)] for slot in range(slots) for i in range(5)
        ]
        correlate_group(
            owns + [next_top[0, :, SIDE:]] + others + [corner[0, :, :LANES]],
            depth[...], forward[...], ends[...], backs[west], final[...], rows[...], r0, r1, base + GROUP * c,
        )
        return carry

    lax.fori_loop(0, steps, step, 0)
    lane = lax.broadcasted_iota(jnp.int32, (8, LANES), 1)
    info_west = other[spare, 0:16, 0:LANES].astype(F32)[0:8]
    corner_facts = corner[0, 0:16, LANES:].astype(F32)[0:8]
    info_west = jnp.where(lane == EXTRA, corner_facts, info_west)
    table = jnp.where(west == 1, info_west, info[0:8, :])
    mine = (lane >= base) & (lane < base + half) | (lane == EXTRA) & (west == 1)
    table = jnp.where(mine, table, 0.0)
    finish_terms(pick[...], r0, r1, table[0:1], table[1:2], out)


SUMS = [pltpu.VMEM((3, LANES, LANES), F32), pltpu.VMEM((3, LANES, LANES), F32)]
VMEM_BYTES = 48 * 1024 * 1024
ANY = pl.BlockSpec(memory_space=pl.ANY)
VMEM = pl.BlockSpec(memory_space=pltpu.VMEM)
SMEM = pl.BlockSpec(memory_space=pltpu.SMEM)


def pair_call(kernel, name, tiles, rows, specs, buffers, semaphores):
    steps = tiles // GROUP
    return pl.pallas_call(
        kernel,
        name=name,
        in_specs=specs + [VMEM] * 7,
        out_specs=VMEM,
        out_shape=jax.ShapeDtypeStruct((rows, LANES), F32),
        scratch_shapes=buffers + SUMS + [pltpu.SemaphoreType.DMA((2, steps))] + semaphores,
        compiler_params=pltpu.CompilerParams(vmem_limit_bytes=VMEM_BYTES),
        cost_estimate=pl.CostEstimate(
            flops=tiles * MOST * 12_000_000,
            bytes_accessed=tiles * 2 * PATCH * SIDE * 2,
            transcendentals=0,
        ),
    )


def south_terms(strips, nxt, info, anchor_t, tabs):
    tiles = strips.shape[0]
    buffers = [pltpu.VMEM((tiles, PATCH, SIDE), BF16)] * 2
    return pair_call(
        south_kernel, "south_pairs", tiles, 64, [ANY, ANY, VMEM, VMEM], buffers, [pltpu.SemaphoreType.DMA]
    )(strips, nxt, info, anchor_t, *tabs)


def side_terms(name, role, strips, received, next_top, corner, info, tabs):
    half = strips.shape[0] // 2
    buffers = [
        pltpu.VMEM((half, PATCH, SIDE), BF16),
        pltpu.VMEM((half // 2 + 1, PATCH, 2 * WIDE), BF16),
    ]
    return pair_call(
        side_kernel, name, half, 32, [SMEM, ANY, ANY, VMEM, VMEM, VMEM], buffers, [pltpu.SemaphoreType.DMA]
    )(role, strips, received, next_top, corner, info, *tabs)


STATICS = COMP


def pieces(x):
    high = x.astype(BF16).astype(F32)
    middle = (x - high).astype(BF16).astype(F32)
    return high, middle, x - high - middle


def edge_kernel(strips, counts, offsets, stiffness, anchor, north, corner, info, left, count_s, offset_s, stiff_s, anchor_s, turn, sems):
    tiles = counts.shape[1]
    lanes = pl.ds(0, LANES)
    copies = [
        (strips.at[0, 1, :, pl.ds(0, SIDE)], north.at[0, :, pl.ds(0, SIDE)]),
        (strips.at[0, 3, :, lanes], corner.at[0, :, lanes]),
        (strips.at[0, 0, :, lanes], left),
        (counts, count_s),
        (offsets, offset_s),
        (stiffness, stiff_s),
        (anchor.at[0], anchor_s),
    ]
    copies = [pltpu.make_async_copy(a, b, sems.at[k]) for k, (a, b) in enumerate(copies)]
    for copy in copies:
        copy.start()
    turn[...] = jnp.zeros_like(turn)
    info[...] = jnp.zeros_like(info)
    for copy in copies:
        copy.wait()
    here = pl.ds(0, tiles)
    info[0:1, here] = count_s[0:1, :].astype(F32)
    info[1:2, here] = offset_s[0:1, :].astype(F32)
    info[2:3, here] = count_s[1:2, :].astype(F32)
    info[3:4, here] = offset_s[1:2, :].astype(F32)
    info[4:5, here] = stiff_s[...]
    turn[0:1, :] = anchor_s[0:1, lanes]
    columns = list(pieces(turn[...].T[0:PATCH, 0:1])) + list(pieces(info[4:5, 0:1]))
    columns += [info[0:1, 0:1], info[1:2, 0:1]]
    lane = lax.broadcasted_iota(jnp.int32, (PATCH, LANES), 1)
    block = jnp.where(lane < COMP, left[...].astype(F32), 0.0)
    for k, x in enumerate(columns):
        block = jnp.where(lane == STATICS + k, x, block)
    north[0, :, SIDE:] = block.astype(BF16)
    row = lax.broadcasted_iota(jnp.int32, (PATCH, LANES), 0)
    facts = jnp.where(row == 0, columns[-2], jnp.where(row == 1, columns[-1], 0.0))
    corner[0, :, LANES:] = jnp.where(lane == EXTRA, facts, 0.0).astype(BF16)


def pack_kernel(role, strips, info, anchor, across, within, anchor_t, buffers, wide, sems):
    tiles = anchor.shape[0]
    half = tiles // 2
    moves = []
    for k, east in enumerate((role[0], 1 - role[0])):
        source = strips.at[pl.ds(east * half, half), 3 * east, :, pl.ds(0, SIDE)]
        moves.append(pltpu.make_async_copy(source, buffers.at[k], sems.at[k]))
        moves[k].start()
    wide[...] = jnp.zeros_like(wide)
    for first in (0, COMP):
        wide[first : first + tiles, :] = anchor[:, 0, :]
    for i in range(NODES // LANES):
        anchor_t[LANES * i : LANES * (i + 1), :] = wide[:, LANES * i : LANES * (i + 1)].T
    for k, packed in enumerate((across, within)):
        moves[k].wait()
        for slot in range(half // 2):
            columns = block_pairs([buffers[k, 2 * slot + j, :, :WIDE] for j in range(2)])
            for i, x in enumerate(columns):
                packed[slot, :, LANES * i : LANES * (i + 1)] = x
        packed[half // 2] = jnp.zeros((PATCH, 2 * WIDE), BF16)
        packed[half // 2, 0:16, 0:LANES] = info[...].astype(BF16)


def edge(strips, counts, offsets, stiffness, anchor):
    tiles = strips.shape[0]
    dma = pltpu.SemaphoreType.DMA
    return pl.pallas_call(
        edge_kernel,
        name="edge",
        in_specs=[ANY] * 5,
        out_specs=[VMEM] * 3,
        out_shape=[
            jax.ShapeDtypeStruct((1, PATCH, SIDE + LANES), BF16),
            jax.ShapeDtypeStruct((1, PATCH, 2 * LANES), BF16),
            jax.ShapeDtypeStruct((16, LANES), F32),
        ],
        scratch_shapes=[
            pltpu.VMEM((PATCH, LANES), BF16),
            pltpu.VMEM((2, tiles), jnp.int32),
            pltpu.VMEM((2, tiles), jnp.int32),
            pltpu.VMEM((1, tiles), F32),
            pltpu.VMEM((1, NODES), F32),
            pltpu.VMEM((LANES, LANES), F32),
            dma((7,)),
        ],
    )(strips, counts, offsets, stiffness, anchor)


def pack(role, strips, info, anchor):
    tiles = strips.shape[0]
    packed = jax.ShapeDtypeStruct((tiles // 4 + 1, PATCH, 2 * WIDE), BF16)
    return pl.pallas_call(
        pack_kernel,
        name="pack",
        in_specs=[SMEM, ANY, VMEM, VMEM],
        out_specs=[VMEM] * 3,
        out_shape=[packed, packed, jax.ShapeDtypeStruct((NODES, LANES), F32)],
        scratch_shapes=[
            pltpu.VMEM((2, tiles // 2, PATCH, SIDE), BF16),
            pltpu.VMEM((LANES, NODES), F32),
            pltpu.SemaphoreType.DMA((2,)),
        ],
        compiler_params=pltpu.CompilerParams(vmem_limit_bytes=VMEM_BYTES),
        cost_estimate=pl.CostEstimate(flops=0, bytes_accessed=6_000_000, transcendentals=0),
    )(role, strips, info, anchor)


def whole(kernel, outs, name, scratch=(), with_role=True):
    shapes = [jax.ShapeDtypeStruct(s, F32) for s in outs]

    def call(*args):
        return pl.pallas_call(
            kernel,
            name=name,
            in_specs=[SMEM] + [VMEM] * (len(args) - 1) if with_role else [VMEM] * len(args),
            out_specs=[VMEM] * len(outs),
            out_shape=shapes,
            scratch_shapes=list(scratch),
            compiler_params=pltpu.CompilerParams(vmem_limit_bytes=VMEM_BYTES),
            cost_estimate=pl.CostEstimate(
                flops=4_000_000, bytes_accessed=2_000_000, transcendentals=0
            ),
        )(*args)

    return call


def both(x):
    return x + pltpu.roll(x, COMP, axis=1)


def tents(offset, count):
    offset = both(offset)
    node = lax.broadcasted_iota(jnp.int32, (count, LANES), 0).astype(F32) * GAP + GAP / 2
    out = []
    for k in range(MOST):
        centre = offset + float(PATCH * k + PATCH // 2)
        out.append(jnp.maximum(0.0, 1.0 - jnp.abs(centre - node) / GAP))
    return out


def load_force(table):
    weight, x, y, shapes = table
    lane = lax.broadcasted_iota(jnp.int32, (1, LANES), 1)
    loads = weight * jnp.where(lane < COMP, x, pltpu.roll(y, COMP, axis=1))
    return sum(t * loads[k : k + 1] for k, t in enumerate(shapes))


def edge_force(table, difference):
    weight, _, _, shapes = table
    out = 0.0
    for k, t in enumerate(shapes):
        projected = jnp.sum(t * difference, axis=0, keepdims=True)
        out = out + t * (projected * weight[k : k + 1])
    return out


LEFT = pl.ds(0, MESH_X, stride=MESH_X)
RIGHT = pl.ds(MESH_X - 1, MESH_X, stride=MESH_X)
TOP = pl.ds(0, MESH_X)
BOTTOM = pl.ds(NODES - MESH_X, MESH_X)


def apply_inside(v, out, stiffness, anchor_t):
    column = lax.broadcasted_iota(jnp.int32, (MESH_X, LANES), 0)
    inner = jnp.where((column == 0) | (column == MESH_X - 1), 1.0, 2.0)
    for i in range(MESH_Y):
        here = v[MESH_X * i : MESH_X * (i + 1), :]
        beside = along_row(here, column)
        degree = inner
        if i > 0:
            beside += v[MESH_X * (i - 1) : MESH_X * i, :]
            degree = degree + 1.0
        if i < MESH_Y - 1:
            beside += v[MESH_X * (i + 1) : MESH_X * (i + 2), :]
            degree = degree + 1.0
        out[MESH_X * i : MESH_X * (i + 1), :] = (
            stiffness * (degree * here - beside) + anchor_t[MESH_X * i : MESH_X * (i + 1), :] * here
        )
    out[NODES:, :] = jnp.zeros((TALL - NODES, LANES), F32)


def along_row(x, node):
    before = jnp.where(node == 0, 0.0, pltpu.roll(x, 1, axis=0))
    return before + jnp.where(node == MESH_X - 1, 0.0, pltpu.roll(x, MESH_X - 1, axis=0))


def along_column(x, node):
    after = jnp.where(node >= MESH_Y - 1, 0.0, pltpu.roll(x, MESH_X - 1, axis=0))
    return after + jnp.where(node >= MESH_Y, 0.0, pltpu.roll(x, 1, axis=0))


def add_forces(out, east, west, south, north):
    out[RIGHT, :] += east
    out[LEFT, :] -= west
    out[BOTTOM, :] += south
    out[TOP, :] -= north


def inner_product(a, b):
    return jnp.sum(a[0:NODES, :] * b[0:NODES, :], axis=0, keepdims=True)


def message_kernel(tiles, role, terms, terms_south, from_north, info, anchor_t, out):
    lane = lax.broadcasted_iota(jnp.int32, (1, LANES), 1)
    out[0:32, :] = terms[...]
    out[25:26, :] = info[4:5, :]
    north = roll_tiles(terms_south[0:32, :], 1, from_north[0:32, :], tiles)
    out[32:40, :] = jnp.zeros((8, LANES), F32)
    for k, row in enumerate((0, 8, 16, 24)):
        out[32 + k : 33 + k, :] = north[row : row + 1]
    first, second, last = [anchor_t[pl.ds(j, MESH_Y, stride=MESH_X), :] for j in (0, 1, MESH_X - 1)]
    to_west = jnp.where(lane < COMP, first, second)
    out[40 : 40 + MESH_Y, :] = jnp.where(role[0] == 1, to_west, last)
    out[40 + MESH_Y :, :] = jnp.zeros((MESH_X - MESH_Y, LANES), F32)


def roll_tiles(x, by, outside, tiles):
    lane = lax.broadcasted_iota(jnp.int32, (1, LANES), 1) % COMP
    if by == 1:
        edge, beyond = lane == 0, pltpu.roll(outside, LANES - (tiles - 1), axis=1)
    else:
        edge, beyond = lane == tiles - 1, pltpu.roll(outside, tiles - 1, axis=1)
    return jnp.where(edge, beyond, pltpu.roll(x, by % LANES, axis=1))


def pick_lane(x, source, target):
    lane = lax.broadcasted_iota(jnp.int32, (1, LANES), 1)
    return both(jnp.where(lane == target, pltpu.roll(x, (target - source) % LANES, axis=1), 0.0))


def near_tents(offset):
    return [
        jnp.maximum(0.0, 1.0 - jnp.abs(offset + (PATCH // 2 - GAP * n - GAP / 2)) / GAP) for n in (1, 2)
    ]


def near_pair(weight, x, y, offset):
    one, two = near_tents(offset)
    lane = lax.broadcasted_iota(jnp.int32, (1, LANES), 1)
    load = weight * jnp.where(lane < COMP, x, y)
    force = weight * one * (one * (2.0 * one * load) + two * (2.0 * two * load))
    return one * load, two * load, force


def mesh_kernel(tiles, *refs):
    role, terms_south, terms_within, terms_across, within, across, next_top, from_north, info, anchor_t = refs[:10]
    v0, v1, v2, v3, match, gram, flip = refs[10:]
    within_is_east = role[0] == 0
    from_east = jnp.where(within_is_east, within[...], across[...])
    from_west = jnp.where(within_is_east, across[...], within[...])
    lane = lax.broadcasted_iota(jnp.int32, (1, LANES), 1)
    node = lax.broadcasted_iota(jnp.int32, (MESH_X, LANES), 0)
    low, inside = lane < tiles // 2, lane < tiles
    side = terms_within[...] + terms_across[...]
    south_terms = terms_south[0:32, :]
    terms = [
        jnp.where(low, side, from_east[0:32, :]),
        jnp.where(low, from_west[0:32, :], side),
        south_terms,
        roll_tiles(south_terms, 1, from_north[0:32, :], tiles),
    ]
    tables_here = []
    for q, table in enumerate(terms):
        table = jnp.where(inside, table, 0.0)
        deep, along = table[8:16], table[16:24]
        x, y = (deep, along) if q < 2 else (along, deep)
        tables_here.append((both(table[0:8]), x, y, tents(table[24:25], MESH_X)))
    east, west, south, north = tables_here
    stiffness = both(info[4:5, :])

    flip[...] = jnp.zeros_like(flip)
    for q, (weight, x, y, _) in enumerate((east, south)):
        for s, rows in enumerate((jnp.where(lane < COMP, weight, 0.0), x, y)):
            flip[24 * q + 8 * s : 24 * q + 8 * s + 8, :] = rows
    match[...] = flip[...].T[0:tiles, 0:48]

    force_e, force_w, force_s, force_n = [load_force(t) for t in tables_here]
    v0[...] = jnp.zeros_like(v0)
    add_forces(v0, force_e, force_w, force_s, force_n)

    outside_east, outside_west = both(from_east[25:26, :]), both(from_west[25:26, :])
    packed = from_east[40:72, :]
    turned = pltpu.roll(packed, COMP, axis=1)
    anchor_e0 = jnp.where(lane < COMP, packed, turned)
    anchor_e1 = jnp.where(lane < COMP, turned, packed)
    anchor_w0 = from_west[40:72, :]
    last = tiles - 1
    statics = next_top[0, :, SIDE:].astype(F32)
    outside_south = sum(pick_lane(statics[0:1], STATICS + k, last) for k in (3, 4, 5))
    anchor_south = sum(pick_lane(statics, STATICS + k, last) for k in (0, 1, 2))
    anchor_s0, anchor_s1 = anchor_south[:MESH_X], anchor_south[MESH_X:]
    outside_north = pick_lane(from_north[25:26, :], last, 0)
    anchor_n0 = pick_lane(from_north[32:64, :], last, 0)

    degree_c = jnp.where((node == 0) | (node == MESH_Y - 1), 2.0, 3.0)
    degree_r = jnp.where((node == 0) | (node == MESH_X - 1), 2.0, 3.0)

    near_n = near_pair(*[both(from_east[32 + k : 33 + k, :]) for k in (0, 2, 1, 3)])
    e0 = -force_e
    e1, e2, e1_pairs = [-jnp.where(node == 0, x, 0.0) for x in near_n]
    w0 = force_w
    near_w = near_pair(*[pick_lane(side[k : k + 1, :], EXTRA, last) for k in (0, 8, 16, 24)])
    s0 = -force_s
    s1, s2, s1_pairs = [-jnp.where(node == 0, x, 0.0) for x in near_w]
    n0 = force_n

    apply_inside(v0, v1, stiffness, anchor_t)
    pull_e = edge_force(east, v0[RIGHT, :] - e0)
    pull_w = edge_force(west, w0 - v0[LEFT, :])
    pull_s = edge_force(south, v0[BOTTOM, :] - s0)
    pull_n = edge_force(north, n0 - v0[TOP, :])
    add_forces(v1, pull_e, pull_w, pull_s, pull_n)
    e0, e1 = (
        outside_east * (degree_c * e0 - along_column(e0, node) - e1) + anchor_e0 * e0 - pull_e,
        outside_east * ((degree_c + 1.0) * e1 - along_column(e1, node) - e0 - e2) + anchor_e1 * e1 + e1_pairs,
    )
    w0, w1 = (
        outside_west * (degree_c * w0 - along_column(w0, node)) + anchor_w0 * w0 + pull_w,
        -outside_west * w0,
    )
    s0, s1 = (
        outside_south * (degree_r * s0 - along_row(s0, node) - s1) + anchor_s0 * s0 - pull_s,
        outside_south * ((degree_r + 1.0) * s1 - along_row(s1, node) - s0 - s2) + anchor_s1 * s1 + s1_pairs,
    )
    n0, n1 = (
        outside_north * (degree_r * n0 - along_row(n0, node)) + anchor_n0 * n0 + pull_n,
        -outside_north * n0,
    )

    def pulls(v, e0, w0, s0, n0):
        top, bottom = v[TOP, :], v[BOTTOM, :]
        spot = lane % COMP
        below = jnp.where(spot == last, s0, pltpu.roll(top, LANES - 1, axis=1))
        above = jnp.where(spot == 0, n0, pltpu.roll(bottom, 1, axis=1))
        return (
            edge_force(east, v[RIGHT, :] - e0),
            edge_force(west, w0 - v[LEFT, :]),
            edge_force(south, bottom - below),
            edge_force(north, above - top),
        )

    apply_inside(v1, v2, stiffness, anchor_t)
    pull_e, pull_w, pull_s, pull_n = pulls(v1, e0, w0, s0, n0)
    add_forces(v2, pull_e, pull_w, pull_s, pull_n)
    e0 = outside_east * (degree_c * e0 - along_column(e0, node) - e1) + anchor_e0 * e0 - pull_e
    w0 = outside_west * (degree_c * w0 - along_column(w0, node) - w1) + anchor_w0 * w0 + pull_w
    s0 = outside_south * (degree_r * s0 - along_row(s0, node) - s1) + anchor_s0 * s0 - pull_s
    n0 = outside_north * (degree_r * n0 - along_row(n0, node) - n1) + anchor_n0 * n0 + pull_n

    apply_inside(v2, v3, stiffness, anchor_t)
    add_forces(v3, *pulls(v2, e0, w0, s0, n0))

    gram[...] = jnp.zeros_like(gram)
    for k, (a, b) in enumerate(((v0, v0), (v0, v1), (v1, v1), (v1, v2), (v2, v2), (v2, v3))):
        gram[k : k + 1, :] = inner_product(a, b)


def final_kernel(tiles, gram, v0, v1, v2, v3, positions, residual):
    moments = jnp.sum(gram[...], axis=1, keepdims=True)
    mu = [moments[k : k + 1, :] for k in range(6)]
    zero, one = jnp.zeros_like(mu[0]), jnp.ones_like(mu[0])

    def form(a, b, shift):
        out = zero
        for i, x in enumerate(a):
            for j, y in enumerate(b):
                out = out + x * y * mu[i + j + shift]
        return out

    res, direction, pos = [one], [one], []
    norm_now = mu[0]
    for iteration in range(3):
        step = norm_now / form(direction, direction, 1)
        pos = [p + step * d for p, d in zip(pos + [zero] * (len(direction) - len(pos)), direction)]
        res = [
            r - step * d for r, d in zip(res + [zero], [zero] + direction)
        ]
        if iteration == 2:
            break
        norm_next = form(res, res, 0)
        ratio = norm_next / norm_now
        direction = [r + ratio * d for r, d in zip(res, direction + [zero])]
        norm_now = norm_next
    for out, coefficients in ((positions, pos), (residual, res)):
        for i in range(NODES // LANES):
            rows = slice(LANES * i, LANES * (i + 1))
            part = sum(c * v[rows, :] for c, v in zip(coefficients, (v0, v1, v2, v3)))
            part = part.T
            for c in range(2):
                out[:, c, rows] = part[COMP * c : COMP * c + tiles, :]


def shifted(x, axis, by):
    peers = lax.axis_size(axis)
    return lax.ppermute(x, axis, [(i, i + by) for i in range(peers) if 0 <= i + by < peers])


def diagonal(x):
    rows, cols = lax.axis_size("row"), lax.axis_size("col")
    pairs = [
        ((r - 1) * cols + c + 1, r * cols + c) for r in range(1, rows) for c in range(cols - 1)
    ]
    return lax.ppermute(x, ("row", "col"), pairs)


def swapped(x, axis, first):
    peers = lax.axis_size(axis)
    pairs = [(i, i + 1) for i in range(first, peers - 1, 2)]
    return lax.ppermute(x, axis, pairs + [(b, a) for a, b in pairs])


def add_over(x, axis, stride, radix):
    peers = lax.axis_size(axis)
    got = [
        lax.ppermute(x, axis, [(i, i ^ (k * stride)) for i in range(peers)]) for k in range(1, radix)
    ]
    for other in got:
        x = x + other
    return x


def sum_everywhere(x):
    for axis, order in (("row", (2, 4, 4)), ("col", (4,))):
        left, stride = lax.axis_size(axis), 1
        for radix in order:
            radix = math.gcd(radix, left)
            if radix > 1:
                x = add_over(x, axis, stride, radix)
                stride, left = stride * radix, left // radix
        if left > 1:
            x = add_over(x, axis, stride, left)
    return x


def per_device(strips, pair_counts, pair_offsets, tile_stiffness, anchor):
    tiles = strips.shape[0]
    own = strips[:, 0]
    field = (TALL, LANES)
    within_role = (lax.axis_index("row") % 2).astype(jnp.int32).reshape(1)
    across_role = 1 - within_role
    to_north, to_corner, info = edge(
        own, pair_counts[:, 0].T, pair_offsets[:, 0].T, tile_stiffness.T, anchor
    )
    next_top = shifted(to_north, "col", -1)
    corner = diagonal(to_corner)
    packed_across, packed_within, anchor_t = pack(within_role, own, info, anchor)
    strips_across = swapped(packed_across, "row", 1)
    packed_within, next_top = lax.optimization_barrier((packed_within, next_top))
    strips_within = swapped(packed_within, "row", 0)
    tabs = tables()
    terms_south = south_terms(own, next_top, info, anchor_t, tabs)
    from_north = shifted(terms_south, "col", 1)
    message = whole(functools.partial(message_kernel, tiles), [(72, LANES)], "message")
    terms_within = side_terms("within_pairs", within_role, own, strips_within, next_top, corner, info, tabs)
    (to_within,) = message(within_role, terms_within, terms_south, from_north, info, anchor_t)
    to_within, strips_across = lax.optimization_barrier((to_within, strips_across))
    within = swapped(to_within, "row", 0)
    terms_across = side_terms("across_pairs", across_role, own, strips_across, next_top, corner, info, tabs)
    terms_across, within = lax.optimization_barrier((terms_across, within))
    (to_across,) = message(across_role, terms_across, terms_south, from_north, info, anchor_t)
    across = swapped(to_across, "row", 1)
    v0, v1, v2, v3, match, gram = whole(
        functools.partial(mesh_kernel, tiles),
        [field, field, field, field, (tiles, 48), (8, LANES)],
        "powers",
        [pltpu.VMEM((LANES, LANES), F32)],
    )(within_role, terms_south, terms_within, terms_across, within, across, next_top, from_north, info, anchor_t)
    gram = sum_everywhere(gram)
    positions, residual = whole(
        functools.partial(final_kernel, tiles),
        [(tiles, 2, NODES), (tiles, 2, NODES)],
        "combine",
        with_role=False,
    )(gram, v0, v1, v2, v3)
    return match.reshape(tiles, 1, 2, 3, 8), positions[:, None], residual[:, None]


def solution(mesh):
    return jax.shard_map(
        per_device,
        mesh=mesh,
        in_specs=(
            P("col", "row", None, None, None),
            P("col", "row", None),
            P("col", "row", None),
            P("col", "row"),
            P("col", "row", None),
        ),
        out_specs=(
            P("col", "row", None, None, None),
            P("col", "row", None, None),
            P("col", "row", None, None),
        ),
        check_vma=False,
    )
```

```python
import functools
import math

import jax
import jax.numpy as jnp
import numpy as np
from jax import lax
from jax.experimental import pallas as pl
from jax.experimental.pallas import tpu as pltpu
from jax.sharding import PartitionSpec as P

MESH_Y = 28
MESH_X = 32
NODES = MESH_Y * MESH_X
PATCH = 64
MOST = 5
WIDE = MOST * PATCH
SIDE = 384
ROWS = 32
EXTRA = 40
LANES = 128
COMP = 64
GROUP = 10
TALL = MESH_X * MESH_X
SMALL_WEIGHT = 1e-06
GAP = 16.0
F32 = jnp.float32
BF16 = jnp.bfloat16
HIGHEST = lax.Precision.HIGHEST


def tables():
    index = np.arange(PATCH)
    angle = (index[:, None] * index[None, :] % PATCH) * (2.0 * math.pi / PATCH)
    bf = jnp.bfloat16
    cos = np.cos(angle).astype(bf).astype(np.float32)
    sin = np.sin(angle).astype(bf).astype(np.float32)
    half = PATCH // 2
    depth = np.concatenate([cos[: half + 1], -sin[1:half]])
    pair = np.eye(2, dtype=np.float32)
    cos2, sin2 = np.kron(pair, cos), np.kron(pair, sin)
    forward = np.block([[cos2, -sin2], [sin2, cos2]])
    ends = np.kron(pair, np.concatenate([cos2, -sin2], axis=1))
    back = np.block([[cos2, sin2], [-sin2, cos2]])
    back_swapped = np.block([[cos2, sin2], [sin2, -cos2]])
    twice = np.full((PATCH,), 2.0, np.float32)
    twice[0] = twice[half] = 1.0
    final = np.concatenate([cos[:, : half + 1], -sin[:, 1:half]], axis=1) * twice
    offset = ((index + PATCH // 2) % PATCH - PATCH // 2).astype(np.float32)
    pick = np.zeros((8, LANES), np.float32)
    pick[0, :PATCH] = 1.0
    pick[1, PATCH:] = 1.0
    pick[2, :PATCH] = offset
    pick[3, PATCH:] = offset
    rows = np.repeat(offset[:, None], LANES, axis=1)
    as_bf = lambda a: jnp.asarray(a, BF16)
    backs = np.stack([back, back_swapped])
    return as_bf(depth), as_bf(forward), as_bf(ends), as_bf(backs), as_bf(final), jnp.asarray(pick), jnp.asarray(rows)


def block_pairs(strips):
    out = []
    for one, two in zip(strips[0::2], strips[1::2]):
        out += [
            one[:, 0:128],
            one[:, 128:256],
            two[:, 0:128],
            two[:, 128:256],
            jnp.concatenate([one[:, 256:320], two[:, 256:320]], axis=1),
        ]
    return out


def cross_power(first_real, first_imag, second_real, second_imag):
    denominator = (
        0.5
        * (
            first_real * first_real
            + first_imag * first_imag
            + second_real * second_real
            + second_imag * second_imag
        )
        + 1.0
    )
    inverse = 1.0 / denominator
    real = (first_real * second_real + first_imag * second_imag) * inverse
    imag = (first_imag * second_real - first_real * second_imag) * inverse
    return real, imag


def correlate_group(cols, depth, forward, ends, back, final, rows, r0, r1, at, extra=None):
    count = len(cols)
    half = count // 2
    lanes = [slice(LANES * i, LANES * (i + 1)) for i in range(count)]
    spec = jnp.dot(depth, jnp.concatenate(cols, axis=1), preferred_element_type=F32)
    stacked = jnp.concatenate(
        [jnp.concatenate([spec[:ROWS, s], spec[ROWS:, s]], axis=1) for s in lanes], axis=0
    ).astype(BF16)
    end_rows = jnp.concatenate(
        [
            jnp.concatenate([spec[0:1, s] for s in lanes], axis=0),
            jnp.concatenate([spec[ROWS : ROWS + 1, s] for s in lanes], axis=0),
        ],
        axis=1,
    ).astype(BF16)
    full = jnp.dot(stacked, forward, preferred_element_type=F32)
    end = jnp.dot(end_rows, ends, preferred_element_type=F32)
    split = half * ROWS
    cross_real, cross_imag = cross_power(
        full[:split, :LANES], full[:split, LANES:], full[split:, :LANES], full[split:, LANES:]
    )
    cross = jnp.concatenate([cross_real, cross_imag], axis=1).astype(BF16)
    end_cross = []
    for s in (0, 2 * LANES):
        end_cross.append(
            jnp.concatenate(
                cross_power(
                    end[:half, s : s + LANES],
                    end[:half, s + LANES : s + 2 * LANES],
                    end[half:, s : s + LANES],
                    end[half:, s + LANES : s + 2 * LANES],
                ),
                axis=1,
            )
        )
    end_back = [
        jnp.dot(c.astype(BF16), back[:, :LANES], preferred_element_type=F32) for c in end_cross
    ]
    back_half = jnp.dot(cross, back, preferred_element_type=F32)
    is_end = lax.broadcasted_iota(jnp.int32, (8, LANES), 0) == 0

    def side(i):
        parts = []
        for part in range(2):
            block = back_half[ROWS * i : ROWS * (i + 1), lanes[part]]
            parts.append(jnp.where(is_end, end_back[part][i : i + 1], block[:8]))
            parts.append(block[8:])
        return jnp.concatenate(parts, axis=0)

    sides = jnp.concatenate([side(i) for i in range(half)], axis=1).astype(BF16)
    surface = jnp.dot(final, sides, preferred_element_type=F32)
    for i in range(half):
        part = surface[:, lanes[i]]
        power = part * part
        total = jnp.sum(power, axis=0, keepdims=True)
        moment = jnp.sum(power * rows, axis=0, keepdims=True)
        place = i % 5
        if i == 5 * (half // 5):
            r0[0, pl.ds(extra, 1), :] = total
            r1[0, pl.ds(extra, 1), :] = moment
        elif place < 4:
            row = at + 2 * (i // 5) + place // 2
            r0[place % 2, pl.ds(row, 1), :] = total
            r1[place % 2, pl.ds(row, 1), :] = moment
        else:
            for row in (at + 2 * (i // 5), at + 2 * (i // 5) + 1):
                r0[2, pl.ds(row, 1), :] = total
                r1[2, pl.ds(row, 1), :] = moment


def lane_sums(pick, table):
    return lax.dot_general(
        pick, table, (((1,), (1,)), ((), ())), precision=HIGHEST, preferred_element_type=F32
    )


def finish_terms(pick, r0, r1, counts, offsets, out):
    scale = 1.0 / float(PATCH * PATCH) ** 2
    lane = lax.broadcasted_iota(jnp.int32, (1, LANES), 1)
    even = lane % 2 == 0
    plain = [lane_sums(pick, r0[s]) for s in range(3)]
    tilted = [lane_sums(pick, r1[s]) for s in range(3)]
    out[...] = jnp.zeros_like(out)
    for k in range(MOST):
        slot, side = k // 2, k % 2
        if k < 4:
            weight = plain[slot][side : side + 1]
            along = plain[slot][2 + side : 3 + side]
            deep = tilted[slot][side : side + 1]
        else:
            weight = jnp.where(even, plain[2][0:1], plain[2][1:2])
            along = jnp.where(even, plain[2][2:3], plain[2][3:4])
            deep = jnp.where(even, tilted[2][0:1], tilted[2][1:2])
        valid = counts > float(k) + 0.5
        if k < 2:
            valid = valid | (lane == EXTRA + 1)
        if k == 1:
            valid = valid | (lane == EXTRA)
        weight = weight * scale
        inverse = scale / (weight + SMALL_WEIGHT)
        out[k : k + 1, :] = jnp.where(valid, weight, 0.0)
        out[8 + k : 9 + k, :] = jnp.where(valid, deep * inverse, 0.0)
        out[16 + k : 17 + k, :] = jnp.where(valid, along * inverse, 0.0)
    out[24:25, :] = offsets


def south_kernel(strips, nxt, info, depth, forward, ends, backs, final, pick, rows, out, first, second, r0, r1, sems, last_sem):
    tiles = first.shape[0]
    steps = tiles // GROUP
    side = pl.ds(0, SIDE)

    def first_copy(c):
        at = pl.ds(GROUP * c, GROUP)
        return pltpu.make_async_copy(strips.at[at, 2, :, side], first.at[at], sems.at[0, c])

    def second_copy(c, count=GROUP):
        below = strips.at[pl.ds(GROUP * c + 1, count), 1, :, side]
        return pltpu.make_async_copy(below, second.at[pl.ds(GROUP * c, count)], sems.at[1, c])

    last_copies = (
        second_copy(steps - 1, GROUP - 1),
        pltpu.make_async_copy(nxt.at[0, :, side], second.at[tiles - 1], last_sem),
    )
    for c in range(steps):
        first_copy(c).start()
        if c < steps - 1:
            second_copy(c).start()
        else:
            for copy in last_copies:
                copy.start()
    r0[...] = jnp.zeros_like(r0)
    r1[...] = jnp.zeros_like(r1)

    def step(c, carry):
        first_copy(c).wait()

        @pl.when(c < steps - 1)
        def _():
            second_copy(c).wait()

        @pl.when(c == steps - 1)
        def _():
            for copy in last_copies:
                copy.wait()

        columns = [
            block_pairs([ref[GROUP * c + j, :, :WIDE] for j in range(GROUP)]) for ref in (first, second)
        ]
        correlate_group(
            columns[0] + columns[1],
            depth[...], forward[...], ends[...], backs[0], final[...], rows[...], r0, r1, GROUP * c,
        )
        return carry

    lax.fori_loop(0, steps, step, 0)
    finish_terms(pick[...], r0, r1, info[2:3, :], info[3:4, :], out)


def side_kernel(part, role, strips, received, next_top, last_bottom, info, depth, forward, ends, backs, final, pick, rows, out, own, other, top, columns, r0, r1, sems, extra_sems):
    half = own.shape[0]
    steps = half // GROUP
    slots = GROUP // 2
    spare = half // 2
    west = role[0]
    base = west * half

    def own_copy(c):
        source = strips.at[pl.ds(base + GROUP * c, GROUP), 3 - 3 * west, :, pl.ds(0, SIDE)]
        return pltpu.make_async_copy(source, own.at[pl.ds(GROUP * c, GROUP)], sems.at[0, c])

    def other_copy(c):
        at = pl.ds(slots * c, slots)
        return pltpu.make_async_copy(received.at[at], other.at[at], sems.at[1, c])

    extra_copies = (
        pltpu.make_async_copy(received.at[spare], other.at[spare], extra_sems.at[0]),
        pltpu.make_async_copy(strips.at[0, 1, :, pl.ds(0, SIDE)], top, extra_sems.at[1]),
    )
    for c in range(steps):
        own_copy(c).start()
        other_copy(c).start()
        if c == 0:
            for copy in extra_copies:
                copy.start()
    r0[...] = jnp.zeros_like(r0)
    r1[...] = jnp.zeros_like(r1)
    for copy in extra_copies:
        copy.wait()
    swapped_order = west == 1
    here, above = top[:, :WIDE], last_bottom[0, :, :WIDE]
    mine, theirs = jnp.where(swapped_order, here, above), jnp.where(swapped_order, above, here)
    two = slice(part * LANES, (part + 1) * LANES)
    columns[0, 0] = jnp.concatenate([next_top[0, :, SIDE : SIDE + COMP], mine[:, 4 * PATCH :]], axis=1)
    columns[0, 1] = jnp.concatenate([other[spare, :, :COMP], theirs[:, 4 * PATCH :]], axis=1)
    columns[1, 0] = mine[:, two]
    columns[1, 1] = theirs[:, two]

    def step(c, carry):
        own_copy(c).wait()
        other_copy(c).wait()
        owns = block_pairs([own[GROUP * c + j, :, :WIDE] for j in range(GROUP)])
        others = [
            other[slots * c + slot, :, LANES * i : LANES * (i + 1)] for slot in range(slots) for i in range(5)
        ]
        correlate_group(
            owns + [columns[c, 0]] + others + [columns[c, 1]],
            depth[...], forward[...], ends[...], backs[west], final[...], rows[...], r0, r1, base + GROUP * c, EXTRA + c,
        )
        return carry

    lax.fori_loop(0, steps, step, 0)
    lane = lax.broadcasted_iota(jnp.int32, (8, LANES), 1)
    info_west = other[spare, 0:16, 2 * LANES : 3 * LANES].astype(F32)[0:8]
    table = jnp.where(west == 1, info_west, info[0:8, :])
    mine = (lane >= base) & (lane < base + half) | (lane == EXTRA) & (west == 1)
    table = jnp.where(mine, table, 0.0)
    finish_terms(pick[...], r0, r1, table[0:1], table[1:2], out)


SUMS = [pltpu.VMEM((3, LANES, LANES), F32), pltpu.VMEM((3, LANES, LANES), F32)]
VMEM_BYTES = 48 * 1024 * 1024
ANY = pl.BlockSpec(memory_space=pl.ANY)
VMEM = pl.BlockSpec(memory_space=pltpu.VMEM)
SMEM = pl.BlockSpec(memory_space=pltpu.SMEM)


def pair_call(kernel, name, tiles, rows, specs, buffers, semaphores):
    steps = tiles // GROUP
    return pl.pallas_call(
        kernel,
        name=name,
        in_specs=specs + [VMEM] * 7,
        out_specs=VMEM,
        out_shape=jax.ShapeDtypeStruct((rows, LANES), F32),
        scratch_shapes=buffers + SUMS + [pltpu.SemaphoreType.DMA((2, steps))] + semaphores,
        compiler_params=pltpu.CompilerParams(vmem_limit_bytes=VMEM_BYTES),
        cost_estimate=pl.CostEstimate(
            flops=tiles * MOST * 12_000_000,
            bytes_accessed=tiles * 2 * PATCH * SIDE * 2,
            transcendentals=0,
        ),
    )


def south_terms(strips, nxt, info, tabs):
    tiles = strips.shape[0]
    buffers = [pltpu.VMEM((tiles, PATCH, SIDE), BF16)] * 2
    return pair_call(
        south_kernel, "south_pairs", tiles, 32, [ANY, VMEM, VMEM], buffers, [pltpu.SemaphoreType.DMA]
    )(strips, nxt, info, *tabs)


def side_terms(name, part, role, strips, received, next_top, last_bottom, info, tabs):
    half = strips.shape[0] // 2
    buffers = [
        pltpu.VMEM((half, PATCH, SIDE), BF16),
        pltpu.VMEM((half // 2 + 1, PATCH, 2 * WIDE), BF16),
        pltpu.VMEM((PATCH, SIDE), BF16),
        pltpu.VMEM((2, 2, PATCH, LANES), BF16),
    ]
    return pair_call(
        functools.partial(side_kernel, part),
        name,
        half,
        32,
        [SMEM, ANY, ANY, VMEM, VMEM, VMEM],
        buffers,
        [pltpu.SemaphoreType.DMA((2,))],
    )(role, strips, received, next_top, last_bottom, info, *tabs)


STATICS = COMP
MESSAGE = (1, PATCH, 2 * WIDE)


def pieces(x):
    high = x.astype(BF16).astype(F32)
    middle = (x - high).astype(BF16).astype(F32)
    return [high, middle, x - high - middle]


def edge_kernel(col_role, strips, counts, offsets, stiffness, anchor, one, two, info, left, count_s, offset_s, stiff_s, anchor_s, turn, sems):
    tiles = counts.shape[1]
    lanes = pl.ds(0, LANES)
    even = 1 - col_role[0]
    right = strips.at[0, 3, :, lanes]
    copies = [(right, out.at[0, :, pl.ds(4 * LANES, LANES)]) for out in (one, two)]
    for out, south in ((one, even), (two, 1 - even)):
        strip = strips.at[(tiles - 1) * south, 1 + south, :, pl.ds(0, SIDE)]
        copies.append((strip, out.at[0, :, pl.ds(0, SIDE)]))
    copies += [
        (strips.at[0, 0, :, lanes], left),
        (counts, count_s),
        (offsets, offset_s),
        (stiffness, stiff_s),
        (anchor.at[0], anchor_s.at[0]),
        (anchor.at[tiles - 1], anchor_s.at[1]),
    ]
    copies = [pltpu.make_async_copy(a, b, sems.at[k]) for k, (a, b) in enumerate(copies)]
    for copy in copies:
        copy.start()
    turn[...] = jnp.zeros_like(turn)
    info[...] = jnp.zeros_like(info)
    for copy in copies:
        copy.wait()
    here = pl.ds(0, tiles)
    info[0:1, here] = count_s[0:1, :].astype(F32)
    info[1:2, here] = offset_s[0:1, :].astype(F32)
    info[2:3, here] = count_s[1:2, :].astype(F32)
    info[3:4, here] = offset_s[1:2, :].astype(F32)
    info[4:5, here] = stiff_s[...]
    turn[0:1, :] = anchor_s[0, 0:1, lanes]
    turn[1:2, :] = anchor_s[1, 0:1, pl.ds(NODES - LANES, LANES)]
    turned = turn[...].T
    first, last = slice(0, 1), slice(tiles - 1, tiles)
    bottom_row = jnp.concatenate([turned[LANES - MESH_X :, 1:2], turned[: PATCH - MESH_X, 2:3]], axis=0)
    north = pieces(turned[:PATCH, 0:1]) + pieces(info[4:5, first]) + [info[0:1, first], info[1:2, first]]
    south = pieces(bottom_row) + pieces(info[4:5, last]) + [info[2:3, last], info[3:4, last]]
    lane = lax.broadcasted_iota(jnp.int32, (PATCH, LANES), 1)
    block = jnp.where(lane < COMP, left[...].astype(F32), 0.0)
    blocks = []
    for columns in (south, north):
        filled = block
        for k, x in enumerate(columns):
            filled = jnp.where(lane == STATICS + k, x, filled)
        blocks.append(filled)
    own = pl.ds(SIDE, LANES)
    one[0, :, own] = jnp.where(even == 1, blocks[0], blocks[1]).astype(BF16)
    two[0, :, own] = jnp.where(even == 1, blocks[1], blocks[0]).astype(BF16)


def pack_kernel(role, strips, anchor, across, within, anchor_t, buffers, wide, sems):
    tiles = anchor.shape[0]
    half = tiles // 2
    moves = []
    for k, east in enumerate((role[0], 1 - role[0])):
        source = strips.at[pl.ds(east * half, half), 3 * east, :, pl.ds(0, SIDE)]
        moves.append(pltpu.make_async_copy(source, buffers.at[k], sems.at[k]))
        moves[k].start()
    wide[...] = jnp.zeros_like(wide)
    for first in (0, COMP):
        wide[first : first + tiles, :] = anchor[:, 0, :]
    for i in range(NODES // LANES):
        anchor_t[LANES * i : LANES * (i + 1), :] = wide[:, LANES * i : LANES * (i + 1)].T
    for k, packed in enumerate((across, within)):
        moves[k].wait()
        for slot in range(half // 2):
            columns = block_pairs([buffers[k, 2 * slot + j, :, :WIDE] for j in range(2)])
            for i, x in enumerate(columns):
                packed[slot, :, LANES * i : LANES * (i + 1)] = x


def fill_kernel(col_role, one, two, info, across_in, within_in, next_top, last_bottom, across, within):
    even = col_role[0] == 0
    next_top[...] = jnp.where(even, one[...], two[...])
    last_bottom[...] = jnp.where(even, two[...], one[...])
    spare = across.shape[0] - 1
    lane = lax.broadcasted_iota(jnp.int32, (16, LANES), 1)
    row = lax.broadcasted_iota(jnp.int32, (16, LANES), 0)
    statics = next_top[0, 0:16, SIDE : SIDE + LANES].astype(F32)
    count = pltpu.roll(statics, (EXTRA - STATICS - 6) % LANES, axis=1)
    offset = pltpu.roll(statics, (EXTRA - STATICS - 7) % LANES, axis=1)
    facts = jnp.where(lane == EXTRA, jnp.where(row == 0, count, offset), info[...])
    for packed in (across, within):
        packed[spare] = jnp.zeros((PATCH, 2 * WIDE), BF16)
        packed[spare, :, 0:LANES] = next_top[0, :, 4 * LANES :]
        packed[spare, 0:16, 2 * LANES : 3 * LANES] = facts.astype(BF16)


def edge(col_role, strips, counts, offsets, stiffness, anchor):
    tiles = strips.shape[0]
    message = jax.ShapeDtypeStruct(MESSAGE, BF16)
    return pl.pallas_call(
        edge_kernel,
        name="edge",
        in_specs=[SMEM] + [ANY] * 5,
        out_specs=[VMEM] * 3,
        out_shape=[message, message, jax.ShapeDtypeStruct((16, LANES), F32)],
        scratch_shapes=[
            pltpu.VMEM((PATCH, LANES), BF16),
            pltpu.VMEM((2, tiles), jnp.int32),
            pltpu.VMEM((2, tiles), jnp.int32),
            pltpu.VMEM((1, tiles), F32),
            pltpu.VMEM((2, 1, NODES), F32),
            pltpu.VMEM((LANES, LANES), F32),
            pltpu.SemaphoreType.DMA((10,)),
        ],
    )(col_role, strips, counts, offsets, stiffness, anchor)


def pack(role, strips, anchor):
    tiles = strips.shape[0]
    packed = jax.ShapeDtypeStruct((tiles // 4 + 1, PATCH, 2 * WIDE), BF16)
    return pl.pallas_call(
        pack_kernel,
        name="pack",
        in_specs=[SMEM, ANY, VMEM],
        out_specs=[VMEM] * 3,
        out_shape=[packed, packed, jax.ShapeDtypeStruct((NODES, LANES), F32)],
        scratch_shapes=[
            pltpu.VMEM((2, tiles // 2, PATCH, SIDE), BF16),
            pltpu.VMEM((LANES, NODES), F32),
            pltpu.SemaphoreType.DMA((2,)),
        ],
        compiler_params=pltpu.CompilerParams(vmem_limit_bytes=VMEM_BYTES),
        cost_estimate=pl.CostEstimate(flops=0, bytes_accessed=6_000_000, transcendentals=0),
    )(role, strips, anchor)


def fill(col_role, one, two, info, across, within):
    packed = jax.ShapeDtypeStruct(across.shape, BF16)
    message = jax.ShapeDtypeStruct(MESSAGE, BF16)
    return pl.pallas_call(
        fill_kernel,
        name="fill",
        in_specs=[SMEM] + [VMEM] * 5,
        out_specs=[VMEM] * 4,
        out_shape=[message, message, packed, packed],
        input_output_aliases={4: 2, 5: 3},
        compiler_params=pltpu.CompilerParams(vmem_limit_bytes=VMEM_BYTES),
    )(col_role, one, two, info, across, within)


def whole(kernel, outs, name, scratch=(), with_role=True):
    shapes = [jax.ShapeDtypeStruct(s, F32) for s in outs]

    def call(*args):
        return pl.pallas_call(
            kernel,
            name=name,
            in_specs=[SMEM] + [VMEM] * (len(args) - 1) if with_role else [VMEM] * len(args),
            out_specs=[VMEM] * len(outs),
            out_shape=shapes,
            scratch_shapes=list(scratch),
            compiler_params=pltpu.CompilerParams(vmem_limit_bytes=VMEM_BYTES),
            cost_estimate=pl.CostEstimate(
                flops=4_000_000, bytes_accessed=2_000_000, transcendentals=0
            ),
        )(*args)

    return call


def both(x):
    return x + pltpu.roll(x, COMP, axis=1)


def tents(offset, count):
    offset = both(offset)
    node = lax.broadcasted_iota(jnp.int32, (count, LANES), 0).astype(F32) * GAP + GAP / 2
    out = []
    for k in range(MOST):
        centre = offset + float(PATCH * k + PATCH // 2)
        out.append(jnp.maximum(0.0, 1.0 - jnp.abs(centre - node) / GAP))
    return out


def load_force(table):
    weight, x, y, shapes = table
    lane = lax.broadcasted_iota(jnp.int32, (1, LANES), 1)
    loads = weight * jnp.where(lane < COMP, x, pltpu.roll(y, COMP, axis=1))
    return sum(t * loads[k : k + 1] for k, t in enumerate(shapes))


def edge_force(table, difference):
    weight, _, _, shapes = table
    out = 0.0
    for k, t in enumerate(shapes):
        projected = jnp.sum(t * difference, axis=0, keepdims=True)
        out = out + t * (projected * weight[k : k + 1])
    return out


LEFT = pl.ds(0, MESH_X, stride=MESH_X)
RIGHT = pl.ds(MESH_X - 1, MESH_X, stride=MESH_X)
TOP = pl.ds(0, MESH_X)
BOTTOM = pl.ds(NODES - MESH_X, MESH_X)


def apply_inside(v, out, stiffness, anchor_t):
    column = lax.broadcasted_iota(jnp.int32, (MESH_X, LANES), 0)
    inner = jnp.where((column == 0) | (column == MESH_X - 1), 1.0, 2.0)
    for i in range(MESH_Y):
        here = v[MESH_X * i : MESH_X * (i + 1), :]
        beside = along_row(here, column)
        degree = inner
        if i > 0:
            beside += v[MESH_X * (i - 1) : MESH_X * i, :]
            degree = degree + 1.0
        if i < MESH_Y - 1:
            beside += v[MESH_X * (i + 1) : MESH_X * (i + 2), :]
            degree = degree + 1.0
        out[MESH_X * i : MESH_X * (i + 1), :] = (
            stiffness * (degree * here - beside) + anchor_t[MESH_X * i : MESH_X * (i + 1), :] * here
        )
    out[NODES:, :] = jnp.zeros((TALL - NODES, LANES), F32)


def along_row(x, node):
    before = jnp.where(node == 0, 0.0, pltpu.roll(x, 1, axis=0))
    return before + jnp.where(node == MESH_X - 1, 0.0, pltpu.roll(x, MESH_X - 1, axis=0))


def along_column(x, node):
    after = jnp.where(node >= MESH_Y - 1, 0.0, pltpu.roll(x, MESH_X - 1, axis=0))
    return after + jnp.where(node >= MESH_Y, 0.0, pltpu.roll(x, 1, axis=0))


def add_forces(out, east, west, south, north):
    out[RIGHT, :] += east
    out[LEFT, :] -= west
    out[BOTTOM, :] += south
    out[TOP, :] -= north


def inner_product(a, b):
    return jnp.sum(a[0:NODES, :] * b[0:NODES, :], axis=0, keepdims=True)


def message_kernel(tiles, role, terms, terms_within, terms_south, last_bottom, info, anchor_t, out):
    lane = lax.broadcasted_iota(jnp.int32, (1, LANES), 1)
    out[0:32, :] = terms[...]
    out[25:26, :] = info[4:5, :]
    north = north_terms(terms_south[...], terms_within[...], terms_within[...], bottom_statics(last_bottom))
    out[32:40, :] = jnp.zeros((8, LANES), F32)
    for k, row in enumerate((0, 8, 16, 24)):
        out[32 + k : 33 + k, :] = north[row : row + 1]
    first, second, last = [anchor_t[pl.ds(j, MESH_Y, stride=MESH_X), :] for j in (0, 1, MESH_X - 1)]
    to_west = jnp.where(lane < COMP, first, second)
    out[40 : 40 + MESH_Y, :] = jnp.where(role[0] == 1, to_west, last)
    out[40 + MESH_Y :, :] = jnp.zeros((MESH_X - MESH_Y, LANES), F32)


def bottom_statics(last_bottom):
    return last_bottom[0, :, SIDE : SIDE + LANES].astype(F32)


def north_terms(south, within, across, statics):
    lane = lax.broadcasted_iota(jnp.int32, (32, LANES), 1)
    row = lax.broadcasted_iota(jnp.int32, (32, LANES), 0)
    block = row % 8
    to_front = lambda x, source: pltpu.roll(x, LANES - source, axis=1)
    first = jnp.where(
        block < 2,
        to_front(within, EXTRA + 1),
        jnp.where(
            block < 4,
            pltpu.roll(to_front(across, EXTRA + 1), 2, axis=0),
            pltpu.roll(to_front(within, EXTRA), 3, axis=0),
        ),
    )
    count = to_front(statics[0:1], STATICS + 6)
    offset = to_front(statics[0:1], STATICS + 7)
    first = jnp.where((row < 24) & (block < MOST) & (block.astype(F32) < count), first, 0.0)
    first = jnp.where(row == 24, offset, first)
    return jnp.where(lane == 0, first, pltpu.roll(south, 1, axis=1))


def pick_lane(x, source, target):
    lane = lax.broadcasted_iota(jnp.int32, (1, LANES), 1)
    return both(jnp.where(lane == target, pltpu.roll(x, (target - source) % LANES, axis=1), 0.0))


def near_tents(offset):
    return [
        jnp.maximum(0.0, 1.0 - jnp.abs(offset + (PATCH // 2 - GAP * n - GAP / 2)) / GAP) for n in (1, 2)
    ]


def near_pair(weight, x, y, offset):
    one, two = near_tents(offset)
    lane = lax.broadcasted_iota(jnp.int32, (1, LANES), 1)
    load = weight * jnp.where(lane < COMP, x, y)
    force = weight * one * (one * (2.0 * one * load) + two * (2.0 * two * load))
    return one * load, two * load, force


def mesh_kernel(tiles, *refs):
    role, terms_south, terms_within, terms_across, within, across, next_top, last_bottom, info, anchor_t = refs[:10]
    v0, v1, v2, v3, match, gram, flip = refs[10:]
    within_is_east = role[0] == 0
    from_east = jnp.where(within_is_east, within[...], across[...])
    from_west = jnp.where(within_is_east, across[...], within[...])
    lane = lax.broadcasted_iota(jnp.int32, (1, LANES), 1)
    node = lax.broadcasted_iota(jnp.int32, (MESH_X, LANES), 0)
    low, inside = lane < tiles // 2, lane < tiles
    side = terms_within[...] + terms_across[...]
    south_terms = terms_south[0:32, :]
    terms = [
        jnp.where(low, side, from_east[0:32, :]),
        jnp.where(low, from_west[0:32, :], side),
        south_terms,
        north_terms(south_terms, terms_within[...], terms_across[...], bottom_statics(last_bottom)),
    ]
    tables_here = []
    for q, table in enumerate(terms):
        table = jnp.where(inside, table, 0.0)
        deep, along = table[8:16], table[16:24]
        x, y = (deep, along) if q < 2 else (along, deep)
        tables_here.append((both(table[0:8]), x, y, tents(table[24:25], MESH_X)))
    east, west, south, north = tables_here
    stiffness = both(info[4:5, :])

    flip[...] = jnp.zeros_like(flip)
    for q, (weight, x, y, _) in enumerate((east, south)):
        for s, rows in enumerate((jnp.where(lane < COMP, weight, 0.0), x, y)):
            flip[24 * q + 8 * s : 24 * q + 8 * s + 8, :] = rows
    match[...] = flip[...].T[0:tiles, 0:48]

    force_e, force_w, force_s, force_n = [load_force(t) for t in tables_here]
    v0[...] = jnp.zeros_like(v0)
    add_forces(v0, force_e, force_w, force_s, force_n)

    outside_east, outside_west = both(from_east[25:26, :]), both(from_west[25:26, :])
    packed = from_east[40:72, :]
    turned = pltpu.roll(packed, COMP, axis=1)
    anchor_e0 = jnp.where(lane < COMP, packed, turned)
    anchor_e1 = jnp.where(lane < COMP, turned, packed)
    anchor_w0 = from_west[40:72, :]
    last = tiles - 1
    statics = next_top[0, :, SIDE : SIDE + LANES].astype(F32)
    outside_south = sum(pick_lane(statics[0:1], STATICS + k, last) for k in (3, 4, 5))
    anchor_south = sum(pick_lane(statics, STATICS + k, last) for k in (0, 1, 2))
    anchor_s0, anchor_s1 = anchor_south[:MESH_X], anchor_south[MESH_X:]
    statics = bottom_statics(last_bottom)
    outside_north = sum(pick_lane(statics[0:1], STATICS + k, 0) for k in (3, 4, 5))
    anchor_n0 = sum(pick_lane(statics[:MESH_X], STATICS + k, 0) for k in (0, 1, 2))

    degree_c = jnp.where((node == 0) | (node == MESH_Y - 1), 2.0, 3.0)
    degree_r = jnp.where((node == 0) | (node == MESH_X - 1), 2.0, 3.0)

    near_n = near_pair(*[both(from_east[32 + k : 33 + k, :]) for k in (0, 2, 1, 3)])
    e0 = -force_e
    e1, e2, e1_pairs = [-jnp.where(node == 0, x, 0.0) for x in near_n]
    w0 = force_w
    near_w = near_pair(*[pick_lane(side[k : k + 1, :], EXTRA, last) for k in (0, 8, 16, 24)])
    s0 = -force_s
    s1, s2, s1_pairs = [-jnp.where(node == 0, x, 0.0) for x in near_w]
    n0 = force_n

    apply_inside(v0, v1, stiffness, anchor_t)
    pull_e = edge_force(east, v0[RIGHT, :] - e0)
    pull_w = edge_force(west, w0 - v0[LEFT, :])
    pull_s = edge_force(south, v0[BOTTOM, :] - s0)
    pull_n = edge_force(north, n0 - v0[TOP, :])
    add_forces(v1, pull_e, pull_w, pull_s, pull_n)
    e0, e1 = (
        outside_east * (degree_c * e0 - along_column(e0, node) - e1) + anchor_e0 * e0 - pull_e,
        outside_east * ((degree_c + 1.0) * e1 - along_column(e1, node) - e0 - e2) + anchor_e1 * e1 + e1_pairs,
    )
    w0, w1 = (
        outside_west * (degree_c * w0 - along_column(w0, node)) + anchor_w0 * w0 + pull_w,
        -outside_west * w0,
    )
    s0, s1 = (
        outside_south * (degree_r * s0 - along_row(s0, node) - s1) + anchor_s0 * s0 - pull_s,
        outside_south * ((degree_r + 1.0) * s1 - along_row(s1, node) - s0 - s2) + anchor_s1 * s1 + s1_pairs,
    )
    n0, n1 = (
        outside_north * (degree_r * n0 - along_row(n0, node)) + anchor_n0 * n0 + pull_n,
        -outside_north * n0,
    )

    def pulls(v, e0, w0, s0, n0):
        top, bottom = v[TOP, :], v[BOTTOM, :]
        spot = lane % COMP
        below = jnp.where(spot == last, s0, pltpu.roll(top, LANES - 1, axis=1))
        above = jnp.where(spot == 0, n0, pltpu.roll(bottom, 1, axis=1))
        return (
            edge_force(east, v[RIGHT, :] - e0),
            edge_force(west, w0 - v[LEFT, :]),
            edge_force(south, bottom - below),
            edge_force(north, above - top),
        )

    apply_inside(v1, v2, stiffness, anchor_t)
    pull_e, pull_w, pull_s, pull_n = pulls(v1, e0, w0, s0, n0)
    add_forces(v2, pull_e, pull_w, pull_s, pull_n)
    e0 = outside_east * (degree_c * e0 - along_column(e0, node) - e1) + anchor_e0 * e0 - pull_e
    w0 = outside_west * (degree_c * w0 - along_column(w0, node) - w1) + anchor_w0 * w0 + pull_w
    s0 = outside_south * (degree_r * s0 - along_row(s0, node) - s1) + anchor_s0 * s0 - pull_s
    n0 = outside_north * (degree_r * n0 - along_row(n0, node) - n1) + anchor_n0 * n0 + pull_n

    apply_inside(v2, v3, stiffness, anchor_t)
    add_forces(v3, *pulls(v2, e0, w0, s0, n0))

    gram[...] = jnp.zeros_like(gram)
    for k, (a, b) in enumerate(((v0, v0), (v0, v1), (v1, v1), (v1, v2), (v2, v2), (v2, v3))):
        gram[k : k + 1, :] = inner_product(a, b)


def final_kernel(tiles, gram, v0, v1, v2, v3, positions, residual):
    moments = jnp.sum(gram[...], axis=1, keepdims=True)
    mu = [moments[k : k + 1, :] for k in range(6)]
    zero, one = jnp.zeros_like(mu[0]), jnp.ones_like(mu[0])

    def form(a, b, shift):
        out = zero
        for i, x in enumerate(a):
            for j, y in enumerate(b):
                out = out + x * y * mu[i + j + shift]
        return out

    res, direction, pos = [one], [one], []
    norm_now = mu[0]
    for iteration in range(3):
        step = norm_now / form(direction, direction, 1)
        pos = [p + step * d for p, d in zip(pos + [zero] * (len(direction) - len(pos)), direction)]
        res = [
            r - step * d for r, d in zip(res + [zero], [zero] + direction)
        ]
        if iteration == 2:
            break
        norm_next = form(res, res, 0)
        ratio = norm_next / norm_now
        direction = [r + ratio * d for r, d in zip(res, direction + [zero])]
        norm_now = norm_next
    for out, coefficients in ((positions, pos), (residual, res)):
        for i in range(NODES // LANES):
            rows = slice(LANES * i, LANES * (i + 1))
            part = sum(c * v[rows, :] for c, v in zip(coefficients, (v0, v1, v2, v3)))
            part = part.T
            for c in range(2):
                out[:, c, rows] = part[COMP * c : COMP * c + tiles, :]


def shifted(x, axis, by):
    peers = lax.axis_size(axis)
    return lax.ppermute(x, axis, [(i, i + by) for i in range(peers) if 0 <= i + by < peers])


def swapped(x, axis, first):
    peers = lax.axis_size(axis)
    pairs = [(i, i + 1) for i in range(first, peers - 1, 2)]
    return lax.ppermute(x, axis, pairs + [(b, a) for a, b in pairs])


def add_over(x, axis, stride, radix):
    peers = lax.axis_size(axis)
    got = [
        lax.ppermute(x, axis, [(i, i ^ (k * stride)) for i in range(peers)]) for k in range(1, radix)
    ]
    for other in got:
        x = x + other
    return x


def sum_everywhere(x):
    for axis, order in (("row", (2, 4, 4)), ("col", (4,))):
        left, stride = lax.axis_size(axis), 1
        for radix in order:
            radix = math.gcd(radix, left)
            if radix > 1:
                x = add_over(x, axis, stride, radix)
                stride, left = stride * radix, left // radix
        if left > 1:
            x = add_over(x, axis, stride, left)
    return x


def per_device(strips, pair_counts, pair_offsets, tile_stiffness, anchor):
    tiles = strips.shape[0]
    own = strips[:, 0]
    field = (TALL, LANES)
    within_role = (lax.axis_index("row") % 2).astype(jnp.int32).reshape(1)
    across_role = 1 - within_role
    col_role = (lax.axis_index("col") % 2).astype(jnp.int32).reshape(1)
    one, two, info = edge(
        col_role, own, pair_counts[:, 0].T, pair_offsets[:, 0].T, tile_stiffness.T, anchor
    )
    one, two = swapped(one, "col", 0), swapped(two, "col", 1)
    packed_across, packed_within, anchor_t = pack(within_role, own, anchor)
    next_top, last_bottom, packed_across, packed_within = fill(
        col_role, one, two, info, packed_across, packed_within
    )
    strips_across = swapped(packed_across, "row", 1)
    strips_within = swapped(packed_within, "row", 0)
    tabs = tables()
    terms_south = south_terms(own, next_top, info, tabs)
    message = whole(functools.partial(message_kernel, tiles), [(72, LANES)], "message")
    terms_within = side_terms(
        "within_pairs", 0, within_role, own, strips_within, next_top, last_bottom, info, tabs
    )
    (to_within,) = message(
        within_role, terms_within, terms_within, terms_south, last_bottom, info, anchor_t
    )
    to_within, strips_across = lax.optimization_barrier((to_within, strips_across))
    within = swapped(to_within, "row", 0)
    terms_across = side_terms(
        "across_pairs", 1, across_role, own, strips_across, next_top, last_bottom, info, tabs
    )
    terms_across, within = lax.optimization_barrier((terms_across, within))
    (to_across,) = message(
        across_role, terms_across, terms_within, terms_south, last_bottom, info, anchor_t
    )
    across = swapped(to_across, "row", 1)
    v0, v1, v2, v3, match, gram = whole(
        functools.partial(mesh_kernel, tiles),
        [field, field, field, field, (tiles, 48), (8, LANES)],
        "powers",
        [pltpu.VMEM((LANES, LANES), F32)],
    )(within_role, terms_south, terms_within, terms_across, within, across, next_top, last_bottom, info, anchor_t)
    gram = sum_everywhere(gram)
    positions, residual = whole(
        functools.partial(final_kernel, tiles),
        [(tiles, 2, NODES), (tiles, 2, NODES)],
        "combine",
        with_role=False,
    )(gram, v0, v1, v2, v3)
    return match.reshape(tiles, 1, 2, 3, 8), positions[:, None], residual[:, None]


def solution(mesh):
    return jax.shard_map(
        per_device,
        mesh=mesh,
        in_specs=(
            P("col", "row", None, None, None),
            P("col", "row", None),
            P("col", "row", None),
            P("col", "row"),
            P("col", "row", None),
        ),
        out_specs=(
            P("col", "row", None, None, None),
            P("col", "row", None, None),
            P("col", "row", None, None),
        ),
        check_vma=False,
    )
```
